32 devices in a mesh: dp: 4 (over y, x), ctx: 8 (over z, core).
Axes of the slice: x: 2, y: 2, z: 4, core: 2. Of those that a mesh axis runs over, the one named last changes fastest.
Arguments:
- block_input: float32 [4, 1024, 768], P('dp', 'ctx'), may hold values from -6 to 6
- out_cotangent: float32 [4, 1024, 768], P('dp', 'ctx'), may hold values from -6 to 6
- first_gain: float32 [768], replicated, may hold values from 0.25 to 1.75
- first_shift: float32 [768], replicated, may hold values from -3 to 3
- mix_weight: bfloat16 [768, 2304], P('dp'), may hold values from -0.21875 to 0.21875
- query_bias: float32 [768], replicated, may hold values from -3 to 3
- value_bias: float32 [768], replicated, may hold values from -3 to 3
- attn_weight: bfloat16 [768, 768], P('dp'), may hold values from -0.75 to 0.75
- attn_bias: float32 [768], replicated, may hold values from -3 to 3
- second_gain: float32 [768], replicated, may hold values from 0.25 to 1.75
- second_shift: float32 [768], replicated, may hold values from -3 to 3
- up_weight: bfloat16 [768, 3072], P('dp'), may hold values from -0.21875 to 0.21875
- up_bias: float32 [3072], replicated, may hold values from -3 to 3
- down_weight: bfloat16 [3072, 768], P('dp'), may hold values from -0.109375 to 0.109375
- down_bias: float32 [768], replicated, may hold values from -3 to 3
Outputs:
- block_output: float32 [4, 1024, 768], P('dp', 'ctx')
- input_grad: float32 [4, 1024, 768], P('dp', 'ctx')
- first_gain_grad: float32 [768], replicated
- first_shift_grad: float32 [768], replicated
- mix_weight_grad: float32 [768, 2304], P('dp')
- query_bias_grad: float32 [768], replicated
- value_bias_grad: float32 [768], replicated
- attn_weight_grad: float32 [768, 768], P('dp')
- attn_bias_grad: float32 [768], replicated
- second_gain_grad: float32 [768], replicated
- second_shift_grad: float32 [768], replicated
- up_weight_grad: float32 [768, 3072], P('dp')
- up_bias_grad: float32 [3072], replicated
- down_weight_grad: float32 [3072, 768], P('dp')
- down_bias_grad: float32 [768], replicated
The draws below stay inside these ranges and needn't reach their ends.
All inputs are finite; a program needn't handle non-finite values.
Results may differ from the reference program's by a relative error of at most 0.023.
Values may be sent and summed in bfloat16 or wider, within the bound.
A program may use at most 128 MiB of HBM per device.

```python
import math
import jax
import jax.numpy as jnp
from jax import lax

D = 768
H = 12
HD = 64
FF = 3072
LEN = 1024
SEQS = 4


def block_levels(rng, shape, cuts, low, largest):
    def one(axis_at, shards_of):
        draws = jax.random.uniform(jax.random.fold_in(jax.random.fold_in(rng, 6), axis_at), (shards_of,), jnp.float32, low / len(cuts), largest / len(cuts))
        return jnp.repeat(jnp.exp(draws), shape[axis_at] // shards_of).reshape((-1,) + (1,) * (len(shape) - axis_at - 1))

    level = one(*cuts[0])
    for cut in cuts[1:]:
        level = level * one(*cut)
    return level


def centred(rng, dims, scale, limit, split=(), held_as=jnp.bfloat16):
    level = block_levels(rng, dims, split, -0.22, 0.18) if split else 1.0
    entries = jax.random.normal(rng, dims, jnp.float32) * scale * level
    return jnp.minimum(jnp.maximum(entries, -limit), limit).astype(held_as)


def setup_inputs(seed: int = 0) -> dict:
    streams_of = jax.random.split(jax.random.key(seed), 16)
    block_input = centred(streams_of[0], (SEQS, LEN, D), 1.0, 6.0, ((0, 4), (1, 8)), jnp.float32)
    out_cotangent = centred(streams_of[1], (SEQS, LEN, D), 1.0, 6.0, ((0, 4), (1, 8)), jnp.float32)
    first_gain = jnp.clip(1.0 + 0.15 * jax.random.normal(streams_of[2], (D,), jnp.float32), 0.25, 1.75)
    first_shift = centred(streams_of[3], (D,), 0.5, 3.0, (), jnp.float32)
    mix_weight = centred(streams_of[4], (D, 3 * D), D ** -0.5, 0.21875, ((0, 4),))
    query_bias = centred(streams_of[5], (D,), 0.5, 3.0, (), jnp.float32)
    value_bias = centred(streams_of[6], (D,), 0.5, 3.0, (), jnp.float32)
    attn_weight = centred(streams_of[7], (D, D), HD ** -0.5, 0.75, ((0, 4),))
    attn_bias = centred(streams_of[8], (D,), 0.5, 3.0, (), jnp.float32)
    second_gain = jnp.clip(1.0 + 0.15 * jax.random.normal(streams_of[9], (D,), jnp.float32), 0.25, 1.75)
    second_shift = centred(streams_of[10], (D,), 0.5, 3.0, (), jnp.float32)
    up_weight = centred(streams_of[11], (D, FF), D ** -0.5, 0.21875, ((0, 4),))
    up_bias = centred(streams_of[12], (FF,), 0.5, 3.0, (), jnp.float32)
    down_weight = centred(streams_of[13], (FF, D), FF ** -0.5, 0.109375, ((0, 4),))
    down_bias = centred(streams_of[14], (D,), 0.5, 3.0, (), jnp.float32)
    return dict(block_input=block_input, out_cotangent=out_cotangent, first_gain=first_gain, first_shift=first_shift, mix_weight=mix_weight, query_bias=query_bias, value_bias=value_bias, attn_weight=attn_weight, attn_bias=attn_bias, second_gain=second_gain, second_shift=second_shift, up_weight=up_weight, up_bias=up_bias, down_weight=down_weight, down_bias=down_bias)


EPS = 1e-05
GELU_C = math.sqrt(2.0 / math.pi)

def layer_norm(x, gain, shift):
    centered = x - lax.optimization_barrier(jnp.mean(x, axis=-1, keepdims=True))
    rstd = lax.rsqrt(lax.optimization_barrier(jnp.mean(centered * centered, axis=-1, keepdims=True)) + EPS)
    x_hat = centered * rstd
    return (x_hat, rstd, x_hat * gain + shift)

def norm_back(grad, x_hat, rstd, gain):
    g = grad * gain
    return rstd * (g - lax.optimization_barrier(jnp.mean(g, axis=-1, keepdims=True)) - x_hat * lax.optimization_barrier(jnp.mean(g * x_hat, axis=-1, keepdims=True)))

def gelu_pair(u):
    inner = GELU_C * (u + 0.044715 * u * u * u)
    t = jnp.tanh(inner)
    value = 0.5 * u * (1.0 + t)
    slope = 0.5 * (1.0 + t) + 0.5 * u * (1.0 - t * t) * GELU_C * (1.0 + 3.0 * 0.044715 * u * u)
    return (value, slope)

def matmul(a, b):
    return jnp.dot(a, b, preferred_element_type=jnp.float32)

def matmul_tn(a, b):
    return jnp.dot(a.T, b, preferred_element_type=jnp.float32)

def matmul_nt(a, b):
    return jnp.dot(a, b.T, preferred_element_type=jnp.float32)

def attention_forward(queries, keys, values):
    length = queries.shape[0]
    qblock = math.gcd(length, 512)
    nblocks = length // qblock
    scale = HD ** (-0.5)
    keys_f = keys.astype(jnp.float32)
    values_f = values.astype(jnp.float32)
    key_pos = jnp.arange(length).astype(jnp.int32)

    def one_block(index):
        start = (index * qblock).astype(jnp.int32)
        q_blk = lax.dynamic_slice_in_dim(queries, start, qblock, 0).astype(jnp.float32)
        scores = jnp.einsum('qhd,khd->hqk', q_blk, keys_f) * scale
        q_pos = start + jnp.arange(qblock).astype(jnp.int32)
        allowed = (key_pos[None, :] <= q_pos[:, None])[None]
        scores = jnp.where(allowed, scores, -1e+30)
        row_max = lax.optimization_barrier(jnp.max(scores, axis=-1))
        expo = jnp.where(allowed, jnp.exp(scores - row_max[..., None]), 0.0)
        total = lax.optimization_barrier(jnp.sum(expo, axis=-1))
        out = jnp.einsum('hqk,khd->qhd', expo, values_f, precision=lax.Precision.HIGHEST) / total.T[..., None]
        return (out, row_max + jnp.log(total))
    outs, lses = lax.map(one_block, jnp.arange(nblocks).astype(jnp.int32))
    attended = outs.reshape(length, H * HD).astype(jnp.bfloat16)
    lse = jnp.transpose(lses, (1, 0, 2)).reshape(H, length)
    return (attended, lse)

def attention_backward(queries, keys, values, attended, lse, attended_grad):
    length = queries.shape[0]
    qblock = math.gcd(length, 512)
    nblocks = length // qblock
    scale = HD ** (-0.5)
    keys_f = keys.astype(jnp.float32)
    values_f = values.astype(jnp.float32)
    grad_f = attended_grad.astype(jnp.float32).reshape(length, H, HD)
    delta = lax.optimization_barrier(jnp.sum(grad_f * attended.astype(jnp.float32).reshape(length, H, HD), axis=-1))
    key_pos = jnp.arange(length).astype(jnp.int32)

    def one_block(carry, index):
        key_acc, value_acc = carry
        start = (index * qblock).astype(jnp.int32)
        q_blk = lax.dynamic_slice_in_dim(queries, start, qblock, 0).astype(jnp.float32)
        g_blk = lax.dynamic_slice_in_dim(grad_f, start, qblock, 0)
        d_blk = lax.dynamic_slice_in_dim(delta, start, qblock, 0)
        l_blk = lax.dynamic_slice_in_dim(lse, start, qblock, 1)
        scores = jnp.einsum('qhd,khd->hqk', q_blk, keys_f) * scale
        q_pos = start + jnp.arange(qblock).astype(jnp.int32)
        allowed = (key_pos[None, :] <= q_pos[:, None])[None]
        probs = jnp.where(allowed, jnp.exp(scores - l_blk[..., None]), 0.0)
        dprob = jnp.einsum('qhd,khd->hqk', g_blk, values_f)
        dscore = probs * (dprob - d_blk.T[..., None])
        probs_b = probs.astype(jnp.bfloat16).astype(jnp.float32)
        dscore_b = dscore.astype(jnp.bfloat16).astype(jnp.float32)
        value_acc = value_acc + jnp.einsum('hqk,qhd->khd', probs_b, g_blk)
        key_acc = key_acc + jnp.einsum('hqk,qhd->khd', dscore_b, q_blk) * scale
        q_grad = jnp.einsum('hqk,khd->qhd', dscore_b, keys_f) * scale
        return ((key_acc, value_acc), q_grad)
    zeros = jnp.zeros((length, H, HD), jnp.float32)
    (key_grad, value_grad), q_grads = lax.scan(one_block, (zeros, zeros), jnp.arange(nblocks).astype(jnp.int32))
    query_grad = q_grads.reshape(length, H * HD)
    return (query_grad, key_grad.reshape(length, H * HD), value_grad.reshape(length, H * HD))

def one_sequence(x, cot, params):
    first_gain, first_shift, mix_weight, query_bias, value_bias, attn_weight, attn_bias, second_gain, second_shift, up_weight, up_bias, down_weight, down_bias = params
    width = x.shape[1]
    length = x.shape[0]
    first_hat, first_rstd, first_out = layer_norm(x, first_gain, first_shift)
    first_in = first_out.astype(jnp.bfloat16)
    mixed = matmul(first_in, mix_weight)
    queries = (mixed[:, :width] + query_bias).astype(jnp.bfloat16)
    keys = mixed[:, width:2 * width].astype(jnp.bfloat16)
    values = (mixed[:, 2 * width:] + value_bias).astype(jnp.bfloat16)
    q3 = queries.reshape(length, H, HD)
    k3 = keys.reshape(length, H, HD)
    v3 = values.reshape(length, H, HD)
    attended, lse = attention_forward(q3, k3, v3)
    after_attn = x + matmul(attended, attn_weight) + attn_bias
    second_hat, second_rstd, second_out = layer_norm(after_attn, second_gain, second_shift)
    second_in = second_out.astype(jnp.bfloat16)
    pre_act = matmul(second_in, up_weight) + up_bias
    act_value, act_slope = gelu_pair(pre_act)
    activ = act_value.astype(jnp.bfloat16)
    block_output = after_attn + matmul(activ, down_weight) + down_bias
    cot_b = cot.astype(jnp.bfloat16)
    down_weight_grad = matmul_tn(activ, cot_b)
    down_bias_grad = lax.optimization_barrier(jnp.sum(cot, axis=0))
    pre_grad = matmul_nt(cot_b, down_weight) * act_slope
    pre_grad_b = pre_grad.astype(jnp.bfloat16)
    up_weight_grad = matmul_tn(second_in, pre_grad_b)
    up_bias_grad = lax.optimization_barrier(jnp.sum(pre_grad, axis=0))
    second_grad = matmul_nt(pre_grad_b, up_weight)
    second_gain_grad = lax.optimization_barrier(jnp.sum(second_grad * second_hat, axis=0))
    second_shift_grad = lax.optimization_barrier(jnp.sum(second_grad, axis=0))
    resid_grad = cot + norm_back(second_grad, second_hat, second_rstd, second_gain)
    resid_b = resid_grad.astype(jnp.bfloat16)
    attn_weight_grad = matmul_tn(attended, resid_b)
    attn_bias_grad = lax.optimization_barrier(jnp.sum(resid_grad, axis=0))
    attended_grad = matmul_nt(resid_b, attn_weight).astype(jnp.bfloat16)
    query_grad, key_grad, value_grad = attention_backward(q3, k3, v3, attended, lse, attended_grad)
    query_bias_grad = lax.optimization_barrier(jnp.sum(query_grad, axis=0))
    value_bias_grad = lax.optimization_barrier(jnp.sum(value_grad, axis=0))
    mixed_grad = jnp.concatenate([query_grad, key_grad, value_grad], axis=1).astype(jnp.bfloat16)
    mix_weight_grad = matmul_tn(first_in, mixed_grad)
    first_grad = matmul_nt(mixed_grad, mix_weight)
    first_gain_grad = lax.optimization_barrier(jnp.sum(first_grad * first_hat, axis=0))
    first_shift_grad = lax.optimization_barrier(jnp.sum(first_grad, axis=0))
    input_grad = resid_grad + norm_back(first_grad, first_hat, first_rstd, first_gain)
    grads = (first_gain_grad, first_shift_grad, mix_weight_grad, query_bias_grad, value_bias_grad, attn_weight_grad, attn_bias_grad, second_gain_grad, second_shift_grad, up_weight_grad, up_bias_grad, down_weight_grad, down_bias_grad)
    return (block_output, input_grad, grads)

def reference(block_input, out_cotangent, first_gain, first_shift, mix_weight, query_bias, value_bias, attn_weight, attn_bias, second_gain, second_shift, up_weight, up_bias, down_weight, down_bias):
    params = (first_gain, first_shift, mix_weight, query_bias, value_bias, attn_weight, attn_bias, second_gain, second_shift, up_weight, up_bias, down_weight, down_bias)
    zero_grads = tuple((jnp.zeros(p.shape, jnp.float32) for p in params))

    def step(carry, item):
        x, cot = item
        out, in_grad, grads = one_sequence(x, cot, params)
        carry = tuple((c + g for c, g in zip(carry, grads)))
        return (carry, (out, in_grad))
    totals, (outputs, input_grads) = lax.scan(step, zero_grads, (block_input, out_cotangent))
    return (outputs, input_grads, totals[0], totals[1], totals[2], totals[3], totals[4], totals[5], totals[6], totals[7], totals[8], totals[9], totals[10], totals[11], totals[12])
```

```python
import functools
import math

import jax
import jax.numpy as jnp
from jax import lax
from jax.experimental import pallas as pl
from jax.experimental.pallas import tpu as pltpu
from jax.sharding import PartitionSpec as P

H = 12
HD = 64


EPS = 1e-05
GELU_C = math.sqrt(2.0 / math.pi)


def from_behind(value, axis, steps):
    count = lax.axis_size(axis)
    pairs = [(source, (source + steps) % count) for source in range(count)]
    return lax.ppermute(value, axis, pairs)


def layer_norm(x, gain, shift):
    centered = x - jnp.mean(x, axis=-1, keepdims=True)
    rstd = lax.rsqrt(jnp.mean(centered * centered, axis=-1, keepdims=True) + EPS)
    x_hat = centered * rstd
    return (x_hat, rstd, x_hat * gain + shift)


def norm_back(grad, x_hat, rstd, gain):
    g = grad * gain
    return rstd * (
        g
        - jnp.mean(g, axis=-1, keepdims=True)
        - x_hat * jnp.mean(g * x_hat, axis=-1, keepdims=True)
    )


def gelu_pair(u):
    inner = GELU_C * (u + 0.044715 * u * u * u)
    t = jnp.tanh(inner)
    value = 0.5 * u * (1.0 + t)
    slope = 0.5 * (1.0 + t) + 0.5 * u * (1.0 - t * t) * GELU_C * (1.0 + 3.0 * 0.044715 * u * u)
    return (value, slope)


def matmul(a, b):
    return jnp.dot(a, b, preferred_element_type=jnp.float32)


def matmul_tn(a, b):
    return lax.dot_general(a, b, (((0,), (0,)), ((), ())), preferred_element_type=jnp.float32)


def matmul_nt(a, b):
    return lax.dot_general(a, b, (((1,), (1,)), ((), ())), preferred_element_type=jnp.float32)


def body(
    block_input,
    out_cotangent,
    first_gain,
    first_shift,
    mix_weight,
    query_bias,
    value_bias,
    attn_weight,
    attn_bias,
    second_gain,
    second_shift,
    up_weight,
    up_bias,
    down_weight,
    down_bias,
):
    rows = block_input.shape[1]
    width = block_input.shape[2]
    scale = HD ** (-0.5)
    x_rows = block_input.reshape(rows, width)
    cot = out_cotangent.reshape(rows, width)
    mix_full, attn_full, up_full, down_full = (
        lax.all_gather(mix_weight, "dp", axis=0, tiled=True),
        lax.all_gather(attn_weight, "dp", axis=0, tiled=True),
        lax.all_gather(up_weight, "dp", axis=0, tiled=True),
        lax.all_gather(down_weight, "dp", axis=0, tiled=True),
    )
    first_hat, first_rstd, first_out = layer_norm(x_rows, first_gain, first_shift)
    first_in = first_out.astype(jnp.bfloat16)
    mixed = matmul(first_in, mix_full)
    queries = (mixed[:, :width] + query_bias).astype(jnp.bfloat16)
    keys = mixed[:, width : 2 * width].astype(jnp.bfloat16)
    values = (mixed[:, 2 * width :] + value_bias).astype(jnp.bfloat16)
    q3 = queries.reshape(rows, H, HD)
    me = lax.axis_index("ctx")
    cycle_size = lax.axis_size("ctx")
    q_pos = me * rows + jnp.arange(rows)
    q_last = me * rows + rows - 1
    start_state = (
        jnp.full((H, rows), -1e30, jnp.float32),
        jnp.zeros((H, rows), jnp.float32),
        jnp.zeros((H, rows, HD), jnp.float32),
    )
    carry = start_state
    key_piece = lax.all_gather(keys, "ctx", axis=0, tiled=True)
    value_piece = lax.all_gather(values, "ctx", axis=0, tiled=True)
    count = key_piece.shape[0]
    kblock = math.gcd(count, 512)
    nblocks = count // kblock
    key_blocks = key_piece.reshape(nblocks, kblock, H, HD)
    value_blocks = value_piece.reshape(nblocks, kblock, H, HD)
    offsets = jnp.arange(nblocks) * kblock

    def one_block(state, item):
        key_blk, value_blk, offset = item

        def compute(state_in):
            run_max, run_total, run_acc = state_in
            key_pos = offset + jnp.arange(kblock)
            allowed = (key_pos[None, :] <= q_pos[:, None])[None]
            scores = (
                jnp.einsum("qhd,khd->hqk", q3, key_blk, preferred_element_type=jnp.float32) * scale
            )
            scores = jnp.where(allowed, scores, -1e30)
            new_max = jnp.maximum(run_max, jnp.max(scores, axis=-1))
            expo = jnp.where(allowed, jnp.exp(scores - new_max[..., None]), 0.0)
            factor = jnp.exp(run_max - new_max)
            new_total = run_total * factor + jnp.sum(expo, axis=-1)
            new_acc = run_acc * factor[..., None] + jnp.einsum(
                "hqk,khd->hqd", expo, value_blk.astype(jnp.float32), precision=lax.Precision.HIGHEST
            )
            return (new_max, new_total, new_acc)

        def keep_state(state_in):
            return state_in

        return (lax.cond(offset <= q_last, compute, keep_state, state), None)

    carry, unused = lax.scan(one_block, carry, (key_blocks, value_blocks, offsets))
    run_max, run_total, run_acc = carry
    attended = (
        (run_acc / run_total[..., None])
        .transpose(1, 0, 2)
        .reshape(rows, width)
        .astype(jnp.bfloat16)
    )
    lse = run_max + jnp.log(run_total)
    after_attn = x_rows + matmul(attended, attn_full) + attn_bias
    second_hat, second_rstd, second_out = layer_norm(after_attn, second_gain, second_shift)
    second_in = second_out.astype(jnp.bfloat16)
    pre_act = matmul(second_in, up_full) + up_bias
    act_value, act_slope = gelu_pair(pre_act)
    activ = act_value.astype(jnp.bfloat16)
    block_output = after_attn + matmul(activ, down_full) + down_bias
    mix_back, attn_back, up_back, down_back = (
        lax.all_gather(mix_weight, "dp", axis=0, tiled=True),
        lax.all_gather(attn_weight, "dp", axis=0, tiled=True),
        lax.all_gather(up_weight, "dp", axis=0, tiled=True),
        lax.all_gather(down_weight, "dp", axis=0, tiled=True),
    )
    cot_b = cot.astype(jnp.bfloat16)
    down_weight_grad = matmul_tn(activ, cot_b)
    down_bias_grad = jnp.sum(cot, axis=0)
    pre_grad = matmul_nt(cot_b, down_back) * act_slope
    pre_grad_b = pre_grad.astype(jnp.bfloat16)
    up_weight_grad = matmul_tn(second_in, pre_grad_b)
    up_bias_grad = jnp.sum(pre_grad, axis=0)
    second_grad = matmul_nt(pre_grad_b, up_back)
    second_gain_grad = jnp.sum(second_grad * second_hat, axis=0)
    second_shift_grad = jnp.sum(second_grad, axis=0)
    resid_grad = cot + norm_back(second_grad, second_hat, second_rstd, second_gain)
    resid_b = resid_grad.astype(jnp.bfloat16)
    attn_weight_grad = matmul_tn(attended, resid_b)
    attn_bias_grad = jnp.sum(resid_grad, axis=0)
    attended_grad = matmul_nt(resid_b, attn_back).astype(jnp.bfloat16)
    grad3 = attended_grad.reshape(rows, H, HD)
    delta = jnp.sum(
        grad3.astype(jnp.float32) * attended.astype(jnp.float32).reshape(rows, H, HD), axis=-1
    ).T

    def block_grads(key_blk, value_blk, key_start):
        count = key_blk.shape[0]
        key3 = key_blk.reshape(count, H, HD)
        value3 = value_blk.reshape(count, H, HD)
        key_pos = key_start + jnp.arange(count)
        allowed = (key_pos[None, :] <= q_pos[:, None])[None]
        scores = jnp.einsum("qhd,khd->hqk", q3, key3, preferred_element_type=jnp.float32) * scale
        probs = jnp.where(allowed, jnp.exp(scores - lse[..., None]), 0.0)
        dprob = jnp.einsum("qhd,khd->hqk", grad3, value3, preferred_element_type=jnp.float32)
        dscore = probs * (dprob - delta[..., None])
        probs_b = probs.astype(jnp.bfloat16)
        dscore_b = dscore.astype(jnp.bfloat16)
        value_add = jnp.einsum("hqk,qhd->khd", probs_b, grad3, preferred_element_type=jnp.float32)
        key_add = (
            jnp.einsum("hqk,qhd->khd", dscore_b, q3, preferred_element_type=jnp.float32) * scale
        )
        query_add = (
            jnp.einsum("hqk,khd->qhd", dscore_b, key3, preferred_element_type=jnp.float32) * scale
        )
        return (
            query_add.reshape(rows, width),
            key_add.reshape(count, width),
            value_add.reshape(count, width),
        )

    def skip_grads(key_blk, value_blk, key_start):
        count = key_blk.shape[0]
        empty = jnp.zeros((count, width), jnp.float32)
        return (jnp.zeros((rows, width), jnp.float32), empty, empty)

    zeros = jnp.zeros((rows, width), jnp.float32)

    def pass_grads(key_acc, value_acc):
        return (
            from_behind(key_acc.astype(jnp.bfloat16), "ctx", -1).astype(key_acc.dtype),
            from_behind(value_acc.astype(jnp.bfloat16), "ctx", -1).astype(value_acc.dtype),
        )

    def cycle_turn(step, state):
        key_blk, value_blk, key_acc, value_acc, query_acc = state
        owner = (me + step) % cycle_size
        query_add, key_add, value_add = lax.cond(
            owner <= me, block_grads, skip_grads, key_blk, value_blk, owner * rows
        )
        key_blk, value_blk = from_behind((key_blk, value_blk), "ctx", -1)
        key_acc, value_acc = pass_grads(key_acc + key_add, value_acc + value_add)
        return (key_blk, value_blk, key_acc, value_acc, query_acc + query_add)

    key_blk, value_blk, key_acc, value_acc, query_acc = lax.fori_loop(
        0, cycle_size - 1, cycle_turn, (keys, values, zeros, zeros, zeros)
    )
    last_owner = (me + cycle_size - 1) % cycle_size
    query_add, key_add, value_add = lax.cond(
        last_owner <= me, block_grads, skip_grads, key_blk, value_blk, last_owner * rows
    )
    key_grad, value_grad = pass_grads(key_acc + key_add, value_acc + value_add)
    query_grad = query_acc + query_add
    query_bias_grad = jnp.sum(query_grad, axis=0)
    value_bias_grad = jnp.sum(value_grad, axis=0)
    mixed_grad = jnp.concatenate([query_grad, key_grad, value_grad], axis=1).astype(jnp.bfloat16)
    mix_weight_grad = matmul_tn(first_in, mixed_grad)
    first_grad = matmul_nt(mixed_grad, mix_back)
    first_gain_grad = jnp.sum(first_grad * first_hat, axis=0)
    first_shift_grad = jnp.sum(first_grad, axis=0)
    input_grad = resid_grad + norm_back(first_grad, first_hat, first_rstd, first_gain)
    local_mats = (mix_weight_grad, attn_weight_grad, up_weight_grad, down_weight_grad)
    shard_sums = (
        lax.psum_scatter(
            local_mats[0].astype(jnp.bfloat16), "dp", scatter_dimension=0, tiled=True
        ).astype(jnp.float32),
        lax.psum_scatter(
            local_mats[1].astype(jnp.bfloat16), "dp", scatter_dimension=0, tiled=True
        ).astype(jnp.float32),
        lax.psum_scatter(
            local_mats[2].astype(jnp.bfloat16), "dp", scatter_dimension=0, tiled=True
        ).astype(jnp.float32),
        lax.psum_scatter(
            local_mats[3].astype(jnp.bfloat16), "dp", scatter_dimension=0, tiled=True
        ).astype(jnp.float32),
    )
    mats = (
        lax.psum(shard_sums[0].astype(jnp.bfloat16), "ctx").astype(jnp.float32),
        lax.psum(shard_sums[1].astype(jnp.bfloat16), "ctx").astype(jnp.float32),
        lax.psum(shard_sums[2].astype(jnp.bfloat16), "ctx").astype(jnp.float32),
        lax.psum(shard_sums[3].astype(jnp.bfloat16), "ctx").astype(jnp.float32),
    )
    smalls = lax.psum(
        (
            first_gain_grad,
            first_shift_grad,
            query_bias_grad,
            value_bias_grad,
            attn_bias_grad,
            second_gain_grad,
            second_shift_grad,
            up_bias_grad,
            down_bias_grad,
        ),
        ("dp", "ctx"),
    )
    return (
        block_output.reshape(1, rows, width),
        input_grad.reshape(1, rows, width),
        smalls[0],
        smalls[1],
        mats[0],
        smalls[2],
        smalls[3],
        mats[1],
        smalls[4],
        smalls[5],
        smalls[6],
        mats[2],
        smalls[7],
        mats[3],
        smalls[8],
    )


def flip(index, mask):
    bit = 1
    while bit <= mask:
        if mask & bit:
            index = index + bit - 2 * bit * ((index // bit) % 2)
        bit *= 2
    return index


MESH = pl.DeviceIdType.MESH
GROUPS = ((2, 2), (0, 2))
SEMS = 160


class Links:
    def __init__(self, send, recv):
        self.send, self.recv, self.count, self.open = send, recv, 0, []

    def make(self, source, target, device):
        number = self.count
        self.count += 1
        return pltpu.make_async_remote_copy(
            src_ref=source,
            dst_ref=target,
            send_sem=self.send.at[number],
            recv_sem=self.recv.at[number],
            device_id=device,
            device_id_type=MESH,
        )

    def start(self, source, target, device):
        copy = self.make(source, target, device)
        copy.start()
        self.open.append(copy)
        return copy

    def finish(self):
        for copy in self.open:
            copy.wait_send()


def arrived(copies):
    for copy in copies:
        copy.wait_recv()


def flat(value):
    return value.reshape(-1, value.shape[-1])


def plane_kernel(
    x_in, cot_in, gain1, shift1, mix_w, q_bias, v_bias, attn_w, attn_bias, gain2, shift2,
    up_w, up_bias, down_w, down_bias,
    out_o, in_o, mix_o, attn_o, up_o, down_o, small_o,
    send_sem, recv_sem, local_sem,
    xv, cv, mw, aw, dw,
    xs, xh1, xh2, cs, ch1, ch2,
    mst, mixc, upc, fa, ca, sa, ra,
    qs, kv, kh, vh, att, lse, agr,
    hat1, aft, hat2, res,
    p1, p2, p3, p4, r1, r2, r3, r4,
    dact, act, pg,
    dg, dgr, dz, dz1, dz2,
    ug, ugr, us, ud, uz1, uz2,
    tg, tgr, tz, tz1, tz2,
    dka, dva, dkvs, dkvr, mg,
    mgr, mgx, ms, md, mz1, mz2, mf,
    od, oh1, idl, ih1,
    sm, sm1, sm2, sm3,
):
    b16, f32 = jnp.bfloat16, jnp.float32
    n, quarter, width = xs.shape
    nz = xh2.shape[0]
    rows = n * quarter
    half, _, hidden = upc.shape[2], 0, upc.shape[3]
    shard = 2 * half
    heads = kh.shape[0]
    dp, ctx = lax.axis_index("dp"), lax.axis_index("ctx")
    z, c = ctx // 2, ctx % 2
    oc = 1 - c
    dps = [flip(dp, k) for k in range(n)]
    zs = [flip(z, k) for k in range(nz)]
    to_dp = [(dps[k], ctx) for k in range(n)]
    to_z = [(dp, 2 * zs[k] + c) for k in range(nz)]
    to_core = (dp, 2 * z + oc)
    inner = (z + 1) // 2 % 2 == 1
    outer = (z + 1) // 2 % 2 == 0
    peers = (3, 1, 2)
    links = Links(send_sem, recv_sem)
    one = lambda index: pl.ds(index, 1)

    locals_ = []

    def fetch(source, target):
        copy = pltpu.make_async_copy(source, target, local_sem.at[len(locals_)])
        copy.start()
        locals_.append(copy)
        return copy

    my_half = pl.ds(pl.multiple_of(c * half, 16), half)
    get_x = fetch(x_in, xv)
    get_mix = fetch(mix_w.at[my_half], mw)
    get_cot = fetch(cot_in, cv)
    get_attn = fetch(attn_w, aw)
    get_down = fetch(down_w, dw)
    columns = lambda index: pl.ds(pl.multiple_of(index * hidden, 128), hidden)
    get_up = fetch(up_w.at[my_half, columns(dp)], upc.at[dp, c])

    barrier = pltpu.get_barrier_semaphore()
    everyone = to_dp[1:] + to_z[1:] + [to_core]
    for device in everyone:
        pl.semaphore_signal(barrier, inc=1, device_id=device, device_id_type=MESH)

    get_x.wait()
    xs[...] = xv[...].astype(b16).reshape(n, quarter, width)
    pl.semaphore_wait(barrier, len(everyone))

    def scatter_dp(source, target):
        return [links.start(source.at[dps[k]], target.at[dp], to_dp[k]) for k in peers]

    def scatter_z(source, target):
        return [links.start(source.at[zs[k]], target.at[z], to_z[k]) for k in peers]

    def gather(ref, first, count):
        part = lambda: ref.at[pl.ds(first, count), dp]
        return [links.start(part(), part(), to_dp[k]) for k in peers]

    def reduce_out(ref, recv, first, count):
        return [
            links.start(
                ref.at[pl.ds(first, count), dps[k]],
                recv.at[k - 1, pl.ds(first, count)],
                to_dp[k],
            )
            for k in peers
        ]

    def reduced(ref, recv, first, count):
        total = ref[first : first + count, one(dp)].astype(f32).reshape(count * quarter, width)
        for k in range(1, n):
            total += flat(recv[k - 1, first : first + count].astype(f32))
        return total

    hop_x = scatter_dp(xs, xh1)
    xh1[one(dp)] = xs[one(dp)]
    get_mix.wait()
    mv = mw[...]
    for d in range(n):
        mst[d] = jnp.concatenate(
            [mv[:, part * width + d * shard : part * width + (d + 1) * shard] for part in (1, 2, 0)],
            axis=1,
        )
    hop_mix = [links.start(mst.at[dps[k]], mixc.at[dp, c], to_dp[k]) for k in peers]
    mixc[one(dp), one(c)] = mst[one(dp)].reshape(1, 1, half, 3 * shard)
    get_cot.wait()
    cot = cv[...]
    cs[...] = cot.astype(b16).reshape(n, quarter, width)
    hop_c = scatter_dp(cs, ch1)
    ch1[one(dp)] = cs[one(dp)]
    sm[...] = jnp.zeros(sm.shape, f32)
    sm[7:8] = jnp.sum(cot, axis=0, keepdims=True)

    arrived(hop_x)
    hop_x = scatter_z(xh1, xh2)
    xh2[one(z)] = xh1[one(z)]
    arrived(hop_mix)
    mix_pair = links.start(mixc.at[:, c], mixc.at[:, c], to_core)
    arrived(hop_c)
    hop_c = scatter_z(ch1, ch2)
    ch2[one(z)] = ch1[one(z)]

    vec = lambda ref: ref[...].reshape(1, -1)

    def pick(ref, size):
        value = vec(ref)
        total = jnp.zeros((1, size), f32)
        for k in range(n):
            total = jnp.where(dp == k, value[:, k * size : (k + 1) * size], total)
        return total

    arrived(hop_x)
    x_hat, rstd1, first = layer_norm(flat(xh2[...]).astype(f32), vec(gain1), vec(shift1))
    hat1[...] = x_hat
    fa[:, one(dp)] = first.astype(b16).reshape(nz, 1, quarter, width)
    ag_first = gather(fa, 0, nz)
    kv_bias = jnp.concatenate([jnp.zeros((1, shard), f32), pick(v_bias, shard)], axis=1)
    own_q_bias = pick(q_bias, shard)
    arrived(hop_c)
    ca[:, one(dp)] = ch2[...].reshape(nz, 1, quarter, width)

    arrived(ag_first)
    hop_up = [
        links.start(up_w.at[my_half, columns(dps[k])], upc.at[dp, c], to_dp[k]) for k in peers
    ]
    ag_cot = gather(ca, 0, nz)
    mix_pair.wait_recv()
    first_all = flat(fa[...])
    mixed = matmul(first_all, flat(mixc[:, :, :, : 2 * shard])) + kv_bias
    kv[:, one(c)] = mixed.astype(b16).reshape(nz, 1, rows, 2 * shard)
    kv_pair = links.start(kv.at[:, c], kv.at[:, c], to_core)
    scale = HD ** (-0.5)
    queries = matmul(first_all, flat(mixc[:, :, :, 2 * shard :])) + own_q_bias
    qs[...] = (queries * scale).astype(b16)
    kv_pair.wait_recv()
    for h in range(heads):
        kh[h] = flat(kv[:, :, :, h * HD : (h + 1) * HD])
        vh[h] = flat(kv[:, :, :, shard + h * HD : shard + (h + 1) * HD])

    last = 2 * rows
    allowed = (
        lax.broadcasted_iota(jnp.int32, (rows, last), 1)
        <= lax.broadcasted_iota(jnp.int32, (rows, last), 0) + c * rows
    )

    def spans(j):
        return ([(0, j * last)] if j else []) + [(j * last, (j + 1) * last)]

    def attend(j):
        at = slice(j * rows, (j + 1) * rows)
        for h in range(heads):
            q = qs[at, h * HD : (h + 1) * HD]
            scores = []
            for a, b in spans(j):
                s = matmul_nt(q, kh[h, a:b])
                scores.append(jnp.where(allowed, s, -1e30) if b == (j + 1) * last else s)
            top = functools.reduce(
                jnp.maximum, [jnp.max(s, axis=-1, keepdims=True) for s in scores]
            )
            total, result = 0.0, 0.0
            for s, (a, b) in zip(scores, spans(j)):
                w = jnp.exp(s - top)
                total = total + jnp.sum(w, axis=-1, keepdims=True)
                result = result + matmul(w.astype(b16), vh[h, a:b])
            att[at, h * HD : (h + 1) * HD] = (result / total).astype(b16)
            lse[h, at] = top + jnp.log(total)

    get_attn.wait()
    rs_attn = []
    for first, count in GROUPS:
        for j in range(first + count - 1, first - 1, -1):
            attend(j)
        part = matmul(att[first * rows : (first + count) * rows], aw[...])
        p1[first : first + count] = part.astype(b16).reshape(count, n, quarter, width)
        rs_attn.append(reduce_out(p1, r1, first, count))

    arrived(hop_up)
    get_up.wait()
    up_pair = links.start(upc.at[:, c], upc.at[:, c], to_core)
    get_down.wait()
    arrived(ag_cot)
    for first, count in GROUPS:
        dact[first * rows : (first + count) * rows] = matmul_nt(
            flat(ca[first : first + count]), dw[...]
        )

    ag_second, rstd2 = [], []
    for (first, count), copies in zip(GROUPS, rs_attn):
        arrived(copies)
        at = slice(first * quarter, (first + count) * quarter)
        after = reduced(p1, r1, first, count) + vec(attn_bias)
        aft[at] = after
        after = after + flat(xh2[first : first + count]).astype(f32)
        hat, rstd, second = layer_norm(after, vec(gain2), vec(shift2))
        hat2[at] = hat
        rstd2.append(rstd)
        sa[first : first + count, one(dp)] = second.astype(b16).reshape(count, 1, quarter, width)
        ag_second.append(gather(sa, first, count))

    up_pair.wait_recv()
    own_up_bias = up_bias[columns(dp)].reshape(1, hidden)
    up_sum = jnp.zeros((1, hidden), f32)
    rs_second = []
    for (first, count), copies in zip(GROUPS, ag_second):
        arrived(copies)
        at = slice(first * rows, (first + count) * rows)
        pre_act = matmul(flat(sa[first : first + count]), flat(upc[...])) + own_up_bias
        value, slope = gelu_pair(pre_act)
        act[at] = value.astype(b16)
        pre_grad = dact[at] * slope
        up_sum += jnp.sum(pre_grad, axis=0, keepdims=True)
        pg[at] = pre_grad.astype(b16)
        part = matmul_nt(pg[at], flat(upc[...]))
        p2[first : first + count] = part.astype(b16).reshape(count, n, quarter, width)
        rs_second.append(reduce_out(p2, r2, first, count))
    for k in range(n):
        sm[8 + k : 9 + k] = jnp.where(dp == k, up_sum, 0.0)

    dg[...] = matmul_tn(act[...], flat(ca[...])).astype(b16).reshape(dg.shape)
    down_pair = links.start(dg.at[oc], dgr, to_core)
    ug[...] = matmul_tn(flat(sa[...]), pg[...]).astype(b16).reshape(ug.shape)
    up_grad_pair = links.start(ug.at[:, oc], ugr, to_core)

    ag_resid = []
    gain_sum, shift_sum, bias_sum = 0.0, 0.0, 0.0
    for (first, count), copies, rstd in zip(GROUPS, rs_second, rstd2):
        arrived(copies)
        at = slice(first * quarter, (first + count) * quarter)
        second_grad = reduced(p2, r2, first, count)
        hat = hat2[at]
        back = norm_back(second_grad, hat, rstd, vec(gain2))
        res[at] = back
        resid = flat(ch2[first : first + count]).astype(f32) + back
        ra[first : first + count, one(dp)] = resid.astype(b16).reshape(count, 1, quarter, width)
        ag_resid.append(gather(ra, first, count))
        gain_sum += jnp.sum(second_grad * hat, axis=0, keepdims=True)
        shift_sum += jnp.sum(second_grad, axis=0, keepdims=True)
        bias_sum += jnp.sum(resid, axis=0, keepdims=True)
    sm[4:5] = bias_sum
    sm[5:6] = gain_sum
    sm[6:7] = shift_sum

    class Reduce:
        def __init__(self, mine, sum1, sum2, total, other_total):
            self.mine, self.sum1, self.sum2, self.total = mine, sum1, sum2, total
            self.one = links.make(mine, sum1, to_z[1])
            self.two = links.make(mine, sum2, to_z[3])
            self.three = links.make(total, total, to_z[1])
            self.pair = links.make(total, total, to_core)

        def first(self):
            pl.when(outer)(lambda: self.one.start())

        def second(self):
            @pl.when(inner)
            def _():
                self.one.wait_recv()
                value = self.mine[...].astype(f32) + self.sum1[...].astype(f32)
                self.mine[...] = value.astype(b16)
                self.two.start()

        def third(self):
            @pl.when(inner)
            def _():
                self.two.wait_recv()
                value = self.mine[...].astype(f32) + self.sum2[...].astype(f32)
                self.total[...] = value.astype(b16).reshape(self.total.shape)
                self.three.start()
                self.pair.start()

        def fourth(self):
            @pl.when(outer)
            def _():
                self.three.wait_recv()
                self.pair.start()

        def done(self):
            self.pair.wait()

            @pl.when(outer)
            def _():
                self.one.wait_send()

            @pl.when(inner)
            def _():
                self.two.wait_send()
                self.three.wait_send()

    down_pair.wait_recv()
    dz[...] = (dg[one(c)].reshape(dz.shape).astype(f32) + dgr[...].astype(f32)).astype(b16)
    red_down = Reduce(dz, dz1, dz2, down_o.at[c], None)
    red_down.first()
    up_grad_pair.wait_recv()
    us[...] = (ug[:, one(c)].reshape(us.shape).astype(f32) + ugr[...].astype(f32)).astype(b16)
    hop_ud = [links.start(us.at[dps[k]], ud.at[:, columns(dp)], to_dp[k]) for k in peers]
    ud[:, columns(dp)] = us[one(dp)].reshape(half, hidden)
    part = matmul(act[...], dw[...])
    p3[...] = part.astype(b16).reshape(p3.shape)

    dq = {}

    def attend_back(j, fresh):
        at = slice(j * rows, (j + 1) * rows)
        for h in range(heads):
            cols = slice(h * HD, (h + 1) * HD)
            q, grad = qs[at, cols], agr[at, cols]
            delta = jnp.sum(grad.astype(f32) * att[at, cols].astype(f32), axis=-1, keepdims=True)
            base, total = lse[h, at], 0.0
            for a, b in spans(j):
                keys = kh[h, a:b]
                p = jnp.exp(matmul_nt(q, keys) - base)
                if b == (j + 1) * last:
                    p = jnp.where(allowed, p, 0.0)
                ds = (p * (matmul_nt(grad, vh[h, a:b]) - delta)).astype(b16)
                total = total + matmul(ds, keys)
                shape = ((b - a) // last, 2, rows, HD)
                dk = matmul_tn(ds, q).reshape(shape)
                dv = matmul_tn(p.astype(b16), grad).reshape(shape)
                blocks = slice(a // last, b // last)
                if fresh:
                    dka[h, blocks], dva[h, blocks] = dk, dv
                else:
                    dka[h, blocks] += dk
                    dva[h, blocks] += dv
            total = total * scale
            q_sum[h] = q_sum.get(h, 0.0) + jnp.sum(total, axis=0, keepdims=True)
            mg[at, 2 * shard + h * HD : 2 * shard + (h + 1) * HD] = total.astype(b16)

    q_sum = {}
    red_up = Reduce(ud, uz1, uz2, up_o.at[c], None)
    rs_out = None
    for number, ((first, count), copies) in enumerate(zip(GROUPS, ag_resid)):
        arrived(copies)
        at = slice(first * rows, (first + count) * rows)
        agr[at] = matmul_nt(flat(ra[first : first + count]), aw[...]).astype(b16)
        if number == len(GROUPS) - 1:
            rs_out = reduce_out(p3, r3, 0, nz)
        for j in range(first + count - 1, first - 1, -1):
            attend_back(j, j == nz - 1)
        if number == 0:
            red_down.second()
            arrived(hop_ud)
            red_up.first()

    for h in range(heads):
        dkvs[:, :, h * HD : (h + 1) * HD] = (
            dka[h, :, one(oc)].reshape(nz, rows, HD).astype(b16)
        )
        dkvs[:, :, shard + h * HD : shard + (h + 1) * HD] = (
            dva[h, :, one(oc)].reshape(nz, rows, HD).astype(b16)
        )
    dkv_pair = links.start(dkvs, dkvr, to_core)
    tg[...] = matmul_tn(att[...], flat(ra[...])).astype(b16).reshape(tg.shape)
    attn_pair = links.start(tg.at[oc], tgr, to_core)
    red_up.second()
    red_down.third()

    def place(value):
        return jnp.concatenate([jnp.where(dp == k, value, 0.0) for k in range(n)], axis=1)

    sm[2:3] = place(jnp.concatenate([q_sum[h] for h in range(heads)], axis=1))
    v_sum = [
        jnp.sum(dva[h].reshape(2 * nz * rows, HD), axis=0, keepdims=True) for h in range(heads)
    ]
    sm[3:4] = place(jnp.concatenate(v_sum, axis=1))
    dkv_pair.wait_recv()
    for h in range(heads):
        for ref, offset in ((dka, 0), (dva, shard)):
            cols = slice(offset + h * HD, offset + (h + 1) * HD)
            mg[:, cols] = (
                ref[h, :, one(c)].reshape(nz * rows, HD) + flat(dkvr[:, :, cols]).astype(f32)
            ).astype(b16)
    rs_first = []
    for first, count in GROUPS:
        part = matmul_nt(mg[first * rows : (first + count) * rows], flat(mixc[...]))
        p4[first : first + count] = part.astype(b16).reshape(count, n, quarter, width)
        rs_first.append(reduce_out(p4, r4, first, count))
    mgr[...] = matmul_tn(flat(fa[...]), mg[...]).astype(b16).reshape(mgr.shape)
    mix_grad_pair = links.start(mgr.at[:, oc], mgx, to_core)

    attn_pair.wait_recv()
    tz[...] = (tg[one(c)].reshape(tz.shape).astype(f32) + tgr[...].astype(f32)).astype(b16)
    red_attn = Reduce(tz, tz1, tz2, attn_o.at[c], None)
    red_attn.first()
    mix_grad_pair.wait_recv()
    ms[...] = (mgr[:, one(c)].reshape(ms.shape).astype(f32) + mgx[...].astype(f32)).astype(b16)
    hop_md = scatter_dp(ms, md)
    md[one(dp)] = ms[one(dp)]
    red_mix = Reduce(md, mz1, mz2, mf.at[:, c], None)

    arrived(rs_out)
    out_delta = aft[...] + reduced(p3, r3, 0, nz) + vec(down_bias)
    od[...] = out_delta.astype(b16).reshape(od.shape)
    hop_o = scatter_z(od, oh1)
    oh1[one(z)] = od[one(z)]
    red_up.third()
    red_down.fourth()
    red_attn.second()

    gain_sum, shift_sum = 0.0, 0.0
    for (first, count), copies in zip(GROUPS, rs_first):
        arrived(copies)
        at = slice(first * quarter, (first + count) * quarter)
        first_grad = reduced(p4, r4, first, count)
        hat = hat1[at]
        back = res[at] + norm_back(first_grad, hat, rstd1[at], vec(gain1))
        idl[first : first + count] = back.astype(b16).reshape(count, quarter, width)
        gain_sum += jnp.sum(first_grad * hat, axis=0, keepdims=True)
        shift_sum += jnp.sum(first_grad, axis=0, keepdims=True)
    hop_i = scatter_z(idl, ih1)
    ih1[one(z)] = idl[one(z)]
    sm[0:1] = gain_sum
    sm[1:2] = shift_sum

    arrived(hop_md)
    red_mix.first()
    sm1[one(dp)] = sm[...].reshape(1, *sm.shape)
    small_dp = [links.start(sm, sm1.at[dp], to_dp[k]) for k in peers]
    arrived(hop_o)
    hop_o = scatter_dp(oh1, out_o)
    out_o[one(dp)] = oh1[one(dp)]
    red_up.fourth()
    red_attn.third()
    arrived(small_dp)
    sm2[one(z)] = jnp.sum(sm1[...], axis=0, keepdims=True)
    small_z = [links.start(sm2.at[z], sm2.at[z], to_z[k]) for k in peers]
    red_mix.second()
    arrived(hop_i)
    hop_i = scatter_dp(ih1, in_o)
    in_o[one(dp)] = ih1[one(dp)]
    arrived(small_z)
    sm3[one(c)] = jnp.sum(sm2[...], axis=0, keepdims=True)
    small_core = links.start(sm3.at[c], sm3.at[c], to_core)
    red_attn.fourth()
    red_mix.third()
    small_core.wait_recv()
    small_o[...] = sm3[0] + sm3[1]
    red_mix.fourth()
    red_down.done()
    red_up.done()
    red_attn.done()
    red_mix.done()
    for d in range(n):
        value = mf[d].reshape(shard, 3 * shard)
        for part, place_at in ((0, 1), (1, 2), (2, 0)):
            start = place_at * width + d * shard
            mix_o[:, start : start + shard] = value[:, part * shard : (part + 1) * shard]
    arrived(hop_o)
    arrived(hop_i)
    links.finish()


def plane_body(
    block_input,
    out_cotangent,
    first_gain,
    first_shift,
    mix_weight,
    query_bias,
    value_bias,
    attn_weight,
    attn_bias,
    second_gain,
    second_shift,
    up_weight,
    up_bias,
    down_weight,
    down_bias,
):
    b16, f32 = jnp.bfloat16, jnp.float32
    n, nz = lax.axis_size("dp"), lax.axis_size("ctx") // 2
    rows, width = block_input.shape[1:]
    quarter = rows // n
    shard = width // n
    half = shard // 2
    hidden = up_weight.shape[1] // n
    heads = H // n
    tokens = nz * rows
    keys = 2 * tokens
    x_rows = block_input.reshape(rows, width)
    cot = out_cotangent.reshape(rows, width)
    vm = pltpu.VMEM
    stack = vm((n, quarter, width), b16)
    part = vm((nz, n, quarter, width), b16)
    part_recv = vm((n - 1, nz, quarter, width), b16)
    own = vm((nz * quarter, width), f32)
    scratch = [
        pltpu.SemaphoreType.DMA((SEMS,)),
        pltpu.SemaphoreType.DMA((SEMS,)),
        pltpu.SemaphoreType.DMA((8,)),
        vm((rows, width), f32), vm((rows, width), f32),
        vm((half, 3 * width), b16), vm((shard, width), b16), vm((hidden, width), b16),
        stack, stack, stack, stack, stack, stack,
        vm((n, half, 3 * shard), b16), vm((n, 2, half, 3 * shard), b16),
        vm((n, 2, half, hidden), b16), part, part, part, part,
        vm((tokens, shard), b16), vm((nz, 2, rows, 2 * shard), b16),
        vm((heads, keys, HD), b16), vm((heads, keys, HD), b16),
        vm((tokens, shard), b16), vm((heads, tokens, 1), f32), vm((tokens, shard), b16),
        own, own, own, own,
        part, part, part, part, part_recv, part_recv, part_recv, part_recv,
        vm((tokens, hidden), f32), vm((tokens, hidden), b16), vm((tokens, hidden), b16),
        vm((2, hidden // 2, width), b16),
    ] + [vm((hidden // 2, width), b16)] * 4 + [
        vm((n, 2, half, hidden), b16), vm((n, half, hidden), b16), vm((n, half, hidden), b16),
    ] + [vm((half, n * hidden), b16)] * 3 + [
        vm((2, half, width), b16),
    ] + [vm((half, width), b16)] * 4 + [
        vm((heads, nz, 2, rows, HD), f32), vm((heads, nz, 2, rows, HD), f32),
        vm((nz, rows, 2 * shard), b16), vm((nz, rows, 2 * shard), b16),
        vm((tokens, 3 * shard), b16),
        vm((n, 2, half, 3 * shard), b16),
    ] + [vm((n, half, 3 * shard), b16)] * 5 + [
        vm((n, 2, half, 3 * shard), b16),
        stack, stack, stack, stack,
        vm((16, width), f32), vm((n, 16, width), f32), vm((nz, 16, width), f32),
        vm((2, 16, width), f32),
    ]
    hbm = pl.BlockSpec(memory_space=pl.ANY)
    near = pl.BlockSpec(memory_space=pltpu.VMEM)
    shapes = [
        ((n, quarter, width), b16),
        ((n, quarter, width), b16),
        ((shard, 3 * width), b16),
        ((2, half, width), b16),
        ((2, half, n * hidden), b16),
        ((2, hidden // 2, width), b16),
        ((16, width), f32),
    ]
    out, grad, mix_g, attn_g, up_g, down_g, small = pl.pallas_call(
        plane_kernel,
        out_shape=[jax.ShapeDtypeStruct(shape, dtype) for shape, dtype in shapes],
        in_specs=[hbm, hbm, near, near, hbm, near, near, hbm, near, near, near, hbm, near, hbm, near],
        out_specs=[near] * len(shapes),
        scratch_shapes=scratch,
        compiler_params=pltpu.CompilerParams(
            collective_id=0, has_side_effects=True, vmem_limit_bytes=60 * 1024 * 1024
        ),
        name="plane",
    )(
        x_rows, cot, first_gain, first_shift, mix_weight, query_bias, value_bias, attn_weight,
        attn_bias, second_gain, second_shift, up_weight, up_bias, down_weight, down_bias,
    )
    block_output = x_rows + out.reshape(rows, width).astype(f32)
    input_grad = cot + grad.reshape(rows, width).astype(f32)
    return (
        block_output.reshape(1, rows, width),
        input_grad.reshape(1, rows, width),
        small[0],
        small[1],
        mix_g.astype(f32),
        small[2],
        small[3],
        attn_g.reshape(shard, width).astype(f32),
        small[4],
        small[5],
        small[6],
        up_g.reshape(shard, n * hidden).astype(f32),
        small[8:12].reshape(n * hidden),
        down_g.reshape(hidden, width).astype(f32),
        small[7],
    )


def fits(mesh):
    n, ctx = mesh.shape["dp"], mesh.shape["ctx"]
    return n == 4 and ctx == 8 and H % n == 0


def solution(mesh):
    placed = (
        P("dp", "ctx", None),
        P("dp", "ctx", None),
        P(),
        P(),
        P("dp", None),
        P(),
        P(),
        P("dp", None),
        P(),
        P(),
        P(),
        P("dp", None),
        P(),
        P("dp", None),
        P(),
    )
    return jax.shard_map(
        plane_body if fits(mesh) else body,
        mesh=mesh,
        in_specs=placed,
        out_specs=(
            P("dp", "ctx", None),
            P("dp", "ctx", None),
            P(),
            P(),
            P("dp", None),
            P(),
            P(),
            P("dp", None),
            P(),
            P(),
            P(),
            P("dp", None),
            P(),
            P("dp", None),
            P(),
        ),
        check_vma=False,
    )
```

```python
import functools
import math

import jax
import jax.numpy as jnp
from jax import lax
from jax.experimental import pallas as pl
from jax.experimental.pallas import tpu as pltpu
from jax.sharding import PartitionSpec as P

H = 12
HD = 64


EPS = 1e-05
GELU_C = math.sqrt(2.0 / math.pi)


def from_behind(value, axis, steps):
    count = lax.axis_size(axis)
    pairs = [(source, (source + steps) % count) for source in range(count)]
    return lax.ppermute(value, axis, pairs)


def layer_norm(x, gain, shift):
    centered = x - jnp.mean(x, axis=-1, keepdims=True)
    rstd = lax.rsqrt(jnp.mean(centered * centered, axis=-1, keepdims=True) + EPS)
    x_hat = centered * rstd
    return (x_hat, rstd, x_hat * gain + shift)


def norm_back(grad, x_hat, rstd, gain):
    g = grad * gain
    return rstd * (
        g
        - jnp.mean(g, axis=-1, keepdims=True)
        - x_hat * jnp.mean(g * x_hat, axis=-1, keepdims=True)
    )


def gelu_pair(u):
    inner = GELU_C * (u + 0.044715 * u * u * u)
    t = jnp.tanh(inner)
    value = 0.5 * u * (1.0 + t)
    slope = 0.5 * (1.0 + t) + 0.5 * u * (1.0 - t * t) * GELU_C * (1.0 + 3.0 * 0.044715 * u * u)
    return (value, slope)


def matmul(a, b):
    return jnp.dot(a, b, preferred_element_type=jnp.float32)


def matmul_tn(a, b):
    return lax.dot_general(a, b, (((0,), (0,)), ((), ())), preferred_element_type=jnp.float32)


def matmul_nt(a, b):
    return lax.dot_general(a, b, (((1,), (1,)), ((), ())), preferred_element_type=jnp.float32)


def body(
    block_input,
    out_cotangent,
    first_gain,
    first_shift,
    mix_weight,
    query_bias,
    value_bias,
    attn_weight,
    attn_bias,
    second_gain,
    second_shift,
    up_weight,
    up_bias,
    down_weight,
    down_bias,
):
    rows = block_input.shape[1]
    width = block_input.shape[2]
    scale = HD ** (-0.5)
    x_rows = block_input.reshape(rows, width)
    cot = out_cotangent.reshape(rows, width)
    mix_full, attn_full, up_full, down_full = (
        lax.all_gather(mix_weight, "dp", axis=0, tiled=True),
        lax.all_gather(attn_weight, "dp", axis=0, tiled=True),
        lax.all_gather(up_weight, "dp", axis=0, tiled=True),
        lax.all_gather(down_weight, "dp", axis=0, tiled=True),
    )
    first_hat, first_rstd, first_out = layer_norm(x_rows, first_gain, first_shift)
    first_in = first_out.astype(jnp.bfloat16)
    mixed = matmul(first_in, mix_full)
    queries = (mixed[:, :width] + query_bias).astype(jnp.bfloat16)
    keys = mixed[:, width : 2 * width].astype(jnp.bfloat16)
    values = (mixed[:, 2 * width :] + value_bias).astype(jnp.bfloat16)
    q3 = queries.reshape(rows, H, HD)
    me = lax.axis_index("ctx")
    cycle_size = lax.axis_size("ctx")
    q_pos = me * rows + jnp.arange(rows)
    q_last = me * rows + rows - 1
    start_state = (
        jnp.full((H, rows), -1e30, jnp.float32),
        jnp.zeros((H, rows), jnp.float32),
        jnp.zeros((H, rows, HD), jnp.float32),
    )
    carry = start_state
    key_piece = lax.all_gather(keys, "ctx", axis=0, tiled=True)
    value_piece = lax.all_gather(values, "ctx", axis=0, tiled=True)
    count = key_piece.shape[0]
    kblock = math.gcd(count, 512)
    nblocks = count // kblock
    key_blocks = key_piece.reshape(nblocks, kblock, H, HD)
    value_blocks = value_piece.reshape(nblocks, kblock, H, HD)
    offsets = jnp.arange(nblocks) * kblock

    def one_block(state, item):
        key_blk, value_blk, offset = item

        def compute(state_in):
            run_max, run_total, run_acc = state_in
            key_pos = offset + jnp.arange(kblock)
            allowed = (key_pos[None, :] <= q_pos[:, None])[None]
            scores = (
                jnp.einsum("qhd,khd->hqk", q3, key_blk, preferred_element_type=jnp.float32) * scale
            )
            scores = jnp.where(allowed, scores, -1e30)
            new_max = jnp.maximum(run_max, jnp.max(scores, axis=-1))
            expo = jnp.where(allowed, jnp.exp(scores - new_max[..., None]), 0.0)
            factor = jnp.exp(run_max - new_max)
            new_total = run_total * factor + jnp.sum(expo, axis=-1)
            new_acc = run_acc * factor[..., None] + jnp.einsum(
                "hqk,khd->hqd", expo, value_blk.astype(jnp.float32), precision=lax.Precision.HIGHEST
            )
            return (new_max, new_total, new_acc)

        def keep_state(state_in):
            return state_in

        return (lax.cond(offset <= q_last, compute, keep_state, state), None)

    carry, unused = lax.scan(one_block, carry, (key_blocks, value_blocks, offsets))
    run_max, run_total, run_acc = carry
    attended = (
        (run_acc / run_total[..., None])
        .transpose(1, 0, 2)
        .reshape(rows, width)
        .astype(jnp.bfloat16)
    )
    lse = run_max + jnp.log(run_total)
    after_attn = x_rows + matmul(attended, attn_full) + attn_bias
    second_hat, second_rstd, second_out = layer_norm(after_attn, second_gain, second_shift)
    second_in = second_out.astype(jnp.bfloat16)
    pre_act = matmul(second_in, up_full) + up_bias
    act_value, act_slope = gelu_pair(pre_act)
    activ = act_value.astype(jnp.bfloat16)
    block_output = after_attn + matmul(activ, down_full) + down_bias
    mix_back, attn_back, up_back, down_back = (
        lax.all_gather(mix_weight, "dp", axis=0, tiled=True),
        lax.all_gather(attn_weight, "dp", axis=0, tiled=True),
        lax.all_gather(up_weight, "dp", axis=0, tiled=True),
        lax.all_gather(down_weight, "dp", axis=0, tiled=True),
    )
    cot_b = cot.astype(jnp.bfloat16)
    down_weight_grad = matmul_tn(activ, cot_b)
    down_bias_grad = jnp.sum(cot, axis=0)
    pre_grad = matmul_nt(cot_b, down_back) * act_slope
    pre_grad_b = pre_grad.astype(jnp.bfloat16)
    up_weight_grad = matmul_tn(second_in, pre_grad_b)
    up_bias_grad = jnp.sum(pre_grad, axis=0)
    second_grad = matmul_nt(pre_grad_b, up_back)
    second_gain_grad = jnp.sum(second_grad * second_hat, axis=0)
    second_shift_grad = jnp.sum(second_grad, axis=0)
    resid_grad = cot + norm_back(second_grad, second_hat, second_rstd, second_gain)
    resid_b = resid_grad.astype(jnp.bfloat16)
    attn_weight_grad = matmul_tn(attended, resid_b)
    attn_bias_grad = jnp.sum(resid_grad, axis=0)
    attended_grad = matmul_nt(resid_b, attn_back).astype(jnp.bfloat16)
    grad3 = attended_grad.reshape(rows, H, HD)
    delta = jnp.sum(
        grad3.astype(jnp.float32) * attended.astype(jnp.float32).reshape(rows, H, HD), axis=-1
    ).T

    def block_grads(key_blk, value_blk, key_start):
        count = key_blk.shape[0]
        key3 = key_blk.reshape(count, H, HD)
        value3 = value_blk.reshape(count, H, HD)
        key_pos = key_start + jnp.arange(count)
        allowed = (key_pos[None, :] <= q_pos[:, None])[None]
        scores = jnp.einsum("qhd,khd->hqk", q3, key3, preferred_element_type=jnp.float32) * scale
        probs = jnp.where(allowed, jnp.exp(scores - lse[..., None]), 0.0)
        dprob = jnp.einsum("qhd,khd->hqk", grad3, value3, preferred_element_type=jnp.float32)
        dscore = probs * (dprob - delta[..., None])
        probs_b = probs.astype(jnp.bfloat16)
        dscore_b = dscore.astype(jnp.bfloat16)
        value_add = jnp.einsum("hqk,qhd->khd", probs_b, grad3, preferred_element_type=jnp.float32)
        key_add = (
            jnp.einsum("hqk,qhd->khd", dscore_b, q3, preferred_element_type=jnp.float32) * scale
        )
        query_add = (
            jnp.einsum("hqk,khd->qhd", dscore_b, key3, preferred_element_type=jnp.float32) * scale
        )
        return (
            query_add.reshape(rows, width),
            key_add.reshape(count, width),
            value_add.reshape(count, width),
        )

    def skip_grads(key_blk, value_blk, key_start):
        count = key_blk.shape[0]
        empty = jnp.zeros((count, width), jnp.float32)
        return (jnp.zeros((rows, width), jnp.float32), empty, empty)

    zeros = jnp.zeros((rows, width), jnp.float32)

    def pass_grads(key_acc, value_acc):
        return (
            from_behind(key_acc.astype(jnp.bfloat16), "ctx", -1).astype(key_acc.dtype),
            from_behind(value_acc.astype(jnp.bfloat16), "ctx", -1).astype(value_acc.dtype),
        )

    def cycle_turn(step, state):
        key_blk, value_blk, key_acc, value_acc, query_acc = state
        owner = (me + step) % cycle_size
        query_add, key_add, value_add = lax.cond(
            owner <= me, block_grads, skip_grads, key_blk, value_blk, owner * rows
        )
        key_blk, value_blk = from_behind((key_blk, value_blk), "ctx", -1)
        key_acc, value_acc = pass_grads(key_acc + key_add, value_acc + value_add)
        return (key_blk, value_blk, key_acc, value_acc, query_acc + query_add)

    key_blk, value_blk, key_acc, value_acc, query_acc = lax.fori_loop(
        0, cycle_size - 1, cycle_turn, (keys, values, zeros, zeros, zeros)
    )
    last_owner = (me + cycle_size - 1) % cycle_size
    query_add, key_add, value_add = lax.cond(
        last_owner <= me, block_grads, skip_grads, key_blk, value_blk, last_owner * rows
    )
    key_grad, value_grad = pass_grads(key_acc + key_add, value_acc + value_add)
    query_grad = query_acc + query_add
    query_bias_grad = jnp.sum(query_grad, axis=0)
    value_bias_grad = jnp.sum(value_grad, axis=0)
    mixed_grad = jnp.concatenate([query_grad, key_grad, value_grad], axis=1).astype(jnp.bfloat16)
    mix_weight_grad = matmul_tn(first_in, mixed_grad)
    first_grad = matmul_nt(mixed_grad, mix_back)
    first_gain_grad = jnp.sum(first_grad * first_hat, axis=0)
    first_shift_grad = jnp.sum(first_grad, axis=0)
    input_grad = resid_grad + norm_back(first_grad, first_hat, first_rstd, first_gain)
    local_mats = (mix_weight_grad, attn_weight_grad, up_weight_grad, down_weight_grad)
    shard_sums = (
        lax.psum_scatter(
            local_mats[0].astype(jnp.bfloat16), "dp", scatter_dimension=0, tiled=True
        ).astype(jnp.float32),
        lax.psum_scatter(
            local_mats[1].astype(jnp.bfloat16), "dp", scatter_dimension=0, tiled=True
        ).astype(jnp.float32),
        lax.psum_scatter(
            local_mats[2].astype(jnp.bfloat16), "dp", scatter_dimension=0, tiled=True
        ).astype(jnp.float32),
        lax.psum_scatter(
            local_mats[3].astype(jnp.bfloat16), "dp", scatter_dimension=0, tiled=True
        ).astype(jnp.float32),
    )
    mats = (
        lax.psum(shard_sums[0].astype(jnp.bfloat16), "ctx").astype(jnp.float32),
        lax.psum(shard_sums[1].astype(jnp.bfloat16), "ctx").astype(jnp.float32),
        lax.psum(shard_sums[2].astype(jnp.bfloat16), "ctx").astype(jnp.float32),
        lax.psum(shard_sums[3].astype(jnp.bfloat16), "ctx").astype(jnp.float32),
    )
    smalls = lax.psum(
        (
            first_gain_grad,
            first_shift_grad,
            query_bias_grad,
            value_bias_grad,
            attn_bias_grad,
            second_gain_grad,
            second_shift_grad,
            up_bias_grad,
            down_bias_grad,
        ),
        ("dp", "ctx"),
    )
    return (
        block_output.reshape(1, rows, width),
        input_grad.reshape(1, rows, width),
        smalls[0],
        smalls[1],
        mats[0],
        smalls[2],
        smalls[3],
        mats[1],
        smalls[4],
        smalls[5],
        smalls[6],
        mats[2],
        smalls[7],
        mats[3],
        smalls[8],
    )


def flip(index, mask):
    bit = 1
    while bit <= mask:
        if mask & bit:
            index = index + bit - 2 * bit * ((index // bit) % 2)
        bit *= 2
    return index


MESH = pl.DeviceIdType.MESH
GROUPS = ((2, 2), (0, 2))
SEMS = 160


class Links:
    def __init__(self, send, recv):
        self.send, self.recv, self.count, self.open = send, recv, 0, []

    def make(self, source, target, device):
        number = self.count
        self.count += 1
        return pltpu.make_async_remote_copy(
            src_ref=source,
            dst_ref=target,
            send_sem=self.send.at[number],
            recv_sem=self.recv.at[number],
            device_id=device,
            device_id_type=MESH,
        )

    def start(self, source, target, device):
        copy = self.make(source, target, device)
        copy.start()
        self.open.append(copy)
        return copy

    def finish(self):
        for copy in self.open:
            copy.wait_send()


def arrived(copies):
    for copy in copies:
        copy.wait_recv()


def flat(value):
    return value.reshape(-1, value.shape[-1])


def plane_kernel(
    x_in, cot_in, gain1_in, shift1_in, mix_w, q_bias_in, v_bias_in, attn_w, attn_bias_in, gain2_in,
    shift2_in, up_w, up_bias_in, down_w, down_bias_in,
    out_o, in_o, mix_o, attn_o, up_o, down_o, small_o,
    send_sem, recv_sem, local_sem,
    gain1, shift1, q_bias, v_bias, attn_bias, gain2, shift2, up_bias, down_bias,
    xv, cv, mw, aw, dw,
    xs, xh1, xh2, cs, ch1, ch2,
    mst, mixc, upc, fa, ca, sa, ra,
    qs, kv, kh, vh, att, lse, agr,
    hat1, aft, hat2, res,
    p1, p2, p3, p4, r1, r2, r3, r4,
    dact, act, pg,
    dg, dgr, dz, dz1, dz2,
    ug, ugr, us, ud, uz1, uz2,
    tg, tgr, tz, tz1, tz2,
    dka, dva, dkvs, dkvr, mg,
    mgr, mgx, ms, md, mz1, mz2,
    od, oh1, idl, ih1,
    sm, sm1, sm2, sm3,
):
    b16, f32 = jnp.bfloat16, jnp.float32
    n, quarter, width = xs.shape
    nz = xh2.shape[0]
    rows = n * quarter
    half, _, hidden = upc.shape[2], 0, upc.shape[3]
    shard = 2 * half
    heads = kh.shape[0]
    dp, ctx = lax.axis_index("dp"), lax.axis_index("ctx")
    z, c = ctx // 2, ctx % 2
    oc = 1 - c
    dps = [flip(dp, k) for k in range(n)]
    zs = [flip(z, k) for k in range(nz)]
    to_dp = [(dps[k], ctx) for k in range(n)]
    to_z = [(dp, 2 * zs[k] + c) for k in range(nz)]
    to_core = (dp, 2 * z + oc)
    inner = (z + 1) // 2 % 2 == 1
    outer = (z + 1) // 2 % 2 == 0
    peers = (3, 1, 2)
    links = Links(send_sem, recv_sem)
    one = lambda index: pl.ds(index, 1)

    locals_ = []

    def fetch(source, target):
        copy = pltpu.make_async_copy(source, target, local_sem.at[len(locals_)])
        copy.start()
        locals_.append(copy)
        return copy

    my_half = pl.ds(pl.multiple_of(c * half, 16), half)
    get_x = fetch(x_in, xv)
    get_mix = fetch(mix_w.at[my_half], mw)
    get_cot = fetch(cot_in, cv)
    get_vectors = [
        fetch(source, target)
        for source, target in (
            (gain1_in, gain1), (shift1_in, shift1), (q_bias_in, q_bias), (v_bias_in, v_bias),
            (attn_bias_in, attn_bias), (gain2_in, gain2), (shift2_in, shift2),
            (up_bias_in, up_bias), (down_bias_in, down_bias),
        )
    ]
    get_attn = fetch(attn_w, aw)
    get_down = fetch(down_w, dw)
    columns = lambda index: pl.ds(pl.multiple_of(index * hidden, 128), hidden)
    get_up = fetch(up_w.at[my_half, columns(dp)], upc.at[dp, c])

    barrier = pltpu.get_barrier_semaphore()
    everyone = to_dp[1:] + to_z[1:] + [to_core]
    for device in everyone:
        pl.semaphore_signal(barrier, inc=1, device_id=device, device_id_type=MESH)

    get_x.wait()
    xs[...] = xv[...].astype(b16).reshape(n, quarter, width)
    get_mix.wait()
    mv = mw[...]
    for d in range(n):
        mst[d] = jnp.concatenate(
            [mv[:, part * width + d * shard : part * width + (d + 1) * shard] for part in (1, 2, 0)],
            axis=1,
        )
    mixc[one(dp), one(c)] = mst[one(dp)].reshape(1, 1, half, 3 * shard)
    pl.semaphore_wait(barrier, len(everyone))

    def scatter_dp(source, target):
        return [links.start(source.at[dps[k]], target.at[dp], to_dp[k]) for k in peers]

    def scatter_z(source, target):
        return [links.start(source.at[zs[k]], target.at[z], to_z[k]) for k in peers]

    def gather(ref, first, count):
        part = lambda: ref.at[pl.ds(first, count), dp]
        return [links.start(part(), part(), to_dp[k]) for k in peers]

    def reduce_out(ref, recv, first, count):
        return [
            links.start(
                ref.at[pl.ds(first, count), dps[k]],
                recv.at[k - 1, pl.ds(first, count)],
                to_dp[k],
            )
            for k in peers
        ]

    def reduced(ref, recv, first, count):
        total = ref[first : first + count, one(dp)].astype(f32).reshape(count * quarter, width)
        for k in range(1, n):
            total += flat(recv[k - 1, first : first + count].astype(f32))
        return total

    hop_x = scatter_dp(xs, xh1)
    xh1[one(dp)] = xs[one(dp)]
    for copy in [get_cot] + get_vectors:
        copy.wait()
    cot = cv[...]
    cs[...] = cot.astype(b16).reshape(n, quarter, width)
    ch1[one(dp)] = cs[one(dp)]
    arrived(hop_x)
    hop_x = scatter_z(xh1, xh2)
    hop_mix = [links.start(mst.at[dps[k]], mixc.at[dp, c], to_dp[k]) for k in peers]
    hop_c = scatter_dp(cs, ch1)
    xh2[one(z)] = xh1[one(z)]
    sm[...] = jnp.zeros(sm.shape, f32)
    sm[7:8] = jnp.sum(cot, axis=0, keepdims=True)

    vec = lambda ref: ref[...].reshape(1, -1)

    def pick(ref, size):
        value = vec(ref)
        total = jnp.zeros((1, size), f32)
        for k in range(n):
            total = jnp.where(dp == k, value[:, k * size : (k + 1) * size], total)
        return total

    arrived(hop_x)
    x_hat, rstd1, first = layer_norm(flat(xh2[...]).astype(f32), vec(gain1), vec(shift1))
    hat1[...] = x_hat
    fa[:, one(dp)] = first.astype(b16).reshape(nz, 1, quarter, width)
    ag_first = gather(fa, 0, nz)
    kv_bias = jnp.concatenate([jnp.zeros((1, shard), f32), pick(v_bias, shard)], axis=1)
    own_q_bias = pick(q_bias, shard)
    arrived(hop_mix)
    mix_pair = links.start(mixc.at[:, c], mixc.at[:, c], to_core)
    arrived(hop_c)
    hop_c = scatter_z(ch1, ch2)
    ch2[one(z)] = ch1[one(z)]

    arrived(ag_first)
    hop_up = [
        links.start(up_w.at[my_half, columns(dps[k])], upc.at[dp, c], to_dp[k]) for k in peers
    ]
    arrived(hop_c)
    ca[:, one(dp)] = ch2[...].reshape(nz, 1, quarter, width)
    ag_cot = gather(ca, 0, nz)
    mix_pair.wait_recv()
    first_all = flat(fa[...])
    mixed = matmul(first_all, flat(mixc[:, :, :, : 2 * shard])) + kv_bias
    kv[:, one(c)] = mixed.astype(b16).reshape(nz, 1, rows, 2 * shard)
    kv_pair = links.start(kv.at[:, c], kv.at[:, c], to_core)
    scale = HD ** (-0.5)
    queries = matmul(first_all, flat(mixc[:, :, :, 2 * shard :])) + own_q_bias
    qs[...] = (queries * scale).astype(b16)
    kv_pair.wait_recv()
    for h in range(heads):
        kh[h] = flat(kv[:, :, :, h * HD : (h + 1) * HD])
        vh[h] = flat(kv[:, :, :, shard + h * HD : shard + (h + 1) * HD])

    last = 2 * rows
    allowed = (
        lax.broadcasted_iota(jnp.int32, (rows, last), 1)
        <= lax.broadcasted_iota(jnp.int32, (rows, last), 0) + c * rows
    )

    def spans(j):
        return ([(0, j * last)] if j else []) + [(j * last, (j + 1) * last)]

    def attend(j):
        at = slice(j * rows, (j + 1) * rows)
        for h in range(heads):
            q = qs[at, h * HD : (h + 1) * HD]
            scores = []
            for a, b in spans(j):
                s = matmul_nt(q, kh[h, a:b])
                scores.append(jnp.where(allowed, s, -1e30) if b == (j + 1) * last else s)
            top = functools.reduce(
                jnp.maximum, [jnp.max(s, axis=-1, keepdims=True) for s in scores]
            )
            total, result = 0.0, 0.0
            for s, (a, b) in zip(scores, spans(j)):
                w = jnp.exp(s - top)
                total = total + jnp.sum(w, axis=-1, keepdims=True)
                result = result + matmul(w.astype(b16), vh[h, a:b])
            att[at, h * HD : (h + 1) * HD] = (result / total).astype(b16)
            lse[h, at] = top + jnp.log(total)

    get_attn.wait()
    rs_attn = []
    for first, count in GROUPS:
        for j in range(first + count - 1, first - 1, -1):
            attend(j)
        part = matmul(att[first * rows : (first + count) * rows], aw[...])
        p1[first : first + count] = part.astype(b16).reshape(count, n, quarter, width)
        rs_attn.append(reduce_out(p1, r1, first, count))

    arrived(hop_up)
    get_up.wait()
    up_pair = links.start(upc.at[:, c], upc.at[:, c], to_core)
    get_down.wait()
    arrived(ag_cot)
    for first, count in GROUPS:
        dact[first * rows : (first + count) * rows] = matmul_nt(
            flat(ca[first : first + count]), dw[...]
        )

    ag_second, rstd2 = [], []
    for (first, count), copies in zip(GROUPS, rs_attn):
        arrived(copies)
        at = slice(first * quarter, (first + count) * quarter)
        after = reduced(p1, r1, first, count) + vec(attn_bias)
        aft[at] = after
        after = after + flat(xh2[first : first + count]).astype(f32)
        hat, rstd, second = layer_norm(after, vec(gain2), vec(shift2))
        hat2[at] = hat
        rstd2.append(rstd)
        sa[first : first + count, one(dp)] = second.astype(b16).reshape(count, 1, quarter, width)
        ag_second.append(gather(sa, first, count))

    up_pair.wait_recv()
    own_up_bias = up_bias[columns(dp)].reshape(1, hidden)
    up_sum = jnp.zeros((1, hidden), f32)
    rs_second = []
    for (first, count), copies in zip(GROUPS, ag_second):
        arrived(copies)
        at = slice(first * rows, (first + count) * rows)
        pre_act = matmul(flat(sa[first : first + count]), flat(upc[...])) + own_up_bias
        value, slope = gelu_pair(pre_act)
        act[at] = value.astype(b16)
        pre_grad = dact[at] * slope
        up_sum += jnp.sum(pre_grad, axis=0, keepdims=True)
        pg[at] = pre_grad.astype(b16)
        part = matmul_nt(pg[at], flat(upc[...]))
        p2[first : first + count] = part.astype(b16).reshape(count, n, quarter, width)
        rs_second.append(reduce_out(p2, r2, first, count))
    for k in range(n):
        sm[8 + k : 9 + k] = jnp.where(dp == k, up_sum, 0.0)

    dg[...] = matmul_tn(act[...], flat(ca[...])).astype(b16).reshape(dg.shape)
    down_pair = links.start(dg.at[oc], dgr, to_core)
    ug[...] = matmul_tn(flat(sa[...]), pg[...]).astype(b16).reshape(ug.shape)
    up_grad_pair = links.start(ug.at[:, oc], ugr, to_core)

    def each(chunks, step):
        for chunk in chunks:
            getattr(chunk, step)()

    class Reduce:
        def __init__(self, mine, sum1, sum2, total):
            self.mine, self.sum1, self.sum2, self.total = mine, sum1, sum2, total
            self.one = links.make(mine, sum1, to_z[1])
            self.two = links.make(mine, sum2, to_z[3])
            self.three = links.make(total, total, to_z[1])
            self.pair = links.make(total, total, to_core)

        def first(self):
            pl.when(outer)(lambda: self.one.start())

        def second(self):
            @pl.when(inner)
            def _():
                self.one.wait_recv()
                value = self.mine[...].astype(f32) + self.sum1[...].astype(f32)
                self.mine[...] = value.astype(b16)
                self.two.start()

        def third(self):
            @pl.when(inner)
            def _():
                self.two.wait_recv()
                value = self.mine[...].astype(f32) + self.sum2[...].astype(f32)
                self.total[...] = value.astype(b16).reshape(self.total.shape)
                self.three.start()
                self.pair.start()

        def fourth(self):
            @pl.when(outer)
            def _():
                self.three.wait_recv()
                self.pair.start()

        def done(self):
            self.pair.wait()

            @pl.when(outer)
            def _():
                self.one.wait_send()

            @pl.when(inner)
            def _():
                self.two.wait_send()
                self.three.wait_send()

    down_pair.wait_recv()
    dz[...] = (dg[one(c)].reshape(dz.shape).astype(f32) + dgr[...].astype(f32)).astype(b16)
    size = dz.shape[0] // n
    red_down = [
        Reduce(dz.at[part], dz1.at[part], dz2.at[part], down_o.at[c, part])
        for part in [pl.ds(k * size, size) for k in range(n)]
    ]
    each(red_down, "first")
    up_grad_pair.wait_recv()
    us[...] = (ug[:, one(c)].reshape(us.shape).astype(f32) + ugr[...].astype(f32)).astype(b16)
    ud[:, columns(dp)] = us[one(dp)].reshape(half, hidden)

    ag_resid = []
    gain_sum, shift_sum, bias_sum = 0.0, 0.0, 0.0
    for (first, count), copies, rstd in zip(GROUPS, rs_second, rstd2):
        arrived(copies)
        at = slice(first * quarter, (first + count) * quarter)
        second_grad = reduced(p2, r2, first, count)
        hat = hat2[at]
        back = norm_back(second_grad, hat, rstd, vec(gain2))
        res[at] = back
        resid = flat(ch2[first : first + count]).astype(f32) + back
        ra[first : first + count, one(dp)] = resid.astype(b16).reshape(count, 1, quarter, width)
        ag_resid.append(gather(ra, first, count))
        gain_sum += jnp.sum(second_grad * hat, axis=0, keepdims=True)
        shift_sum += jnp.sum(second_grad, axis=0, keepdims=True)
        bias_sum += jnp.sum(resid, axis=0, keepdims=True)
    sm[4:5] = bias_sum
    sm[5:6] = gain_sum
    sm[6:7] = shift_sum

    hop_ud = [links.start(us.at[dps[k]], ud.at[:, columns(dp)], to_dp[k]) for k in peers]
    part = matmul(act[...], dw[...])
    p3[...] = part.astype(b16).reshape(p3.shape)

    dq = {}

    def attend_back(j, fresh):
        at = slice(j * rows, (j + 1) * rows)
        for h in range(heads):
            cols = slice(h * HD, (h + 1) * HD)
            q, grad = qs[at, cols], agr[at, cols]
            delta = jnp.sum(grad.astype(f32) * att[at, cols].astype(f32), axis=-1, keepdims=True)
            base, total = lse[h, at], 0.0
            for a, b in spans(j):
                keys = kh[h, a:b]
                p = jnp.exp(matmul_nt(q, keys) - base)
                if b == (j + 1) * last:
                    p = jnp.where(allowed, p, 0.0)
                ds = (p * (matmul_nt(grad, vh[h, a:b]) - delta)).astype(b16)
                total = total + matmul(ds, keys)
                shape = ((b - a) // last, 2, rows, HD)
                dk = matmul_tn(ds, q).reshape(shape)
                dv = matmul_tn(p.astype(b16), grad).reshape(shape)
                blocks = slice(a // last, b // last)
                if fresh:
                    dka[h, blocks], dva[h, blocks] = dk, dv
                else:
                    dka[h, blocks] += dk
                    dva[h, blocks] += dv
            total = total * scale
            q_sum[h] = q_sum.get(h, 0.0) + jnp.sum(total, axis=0, keepdims=True)
            mg[at, 2 * shard + h * HD : 2 * shard + (h + 1) * HD] = total.astype(b16)

    q_sum = {}
    red_up = [
        Reduce(ud.at[:, part], uz1.at[:, part], uz2.at[:, part], up_o.at[c, :, part])
        for part in [pl.ds(k * hidden, hidden) for k in range(n)]
    ]
    red_attn = Reduce(tz, tz1, tz2, attn_o.at[c])
    red_mix = [Reduce(md.at[k], mz1.at[k], mz2.at[k], mix_o.at[k, c]) for k in range(n)]

    def weights_of(first, count):
        return matmul_nt(flat(ra[first : first + count]), aw[...]).astype(b16)

    (first, count), (first2, count2) = GROUPS
    arrived(ag_resid[0])
    agr[first * rows : (first + count) * rows] = weights_of(first, count)
    red_down[0].second()
    attend_back(3, True)
    red_down[1].second()
    attend_back(2, False)
    red_down[2].second()
    red_down[0].third()
    arrived(ag_resid[1])
    agr[first2 * rows : (first2 + count2) * rows] = weights_of(first2, count2)
    rs_out = reduce_out(p3, r3, 0, nz)
    attend_back(1, False)
    red_down[3].second()
    red_down[1].third()
    arrived(hop_ud)
    each(red_up, "first")
    attend_back(0, False)

    for h in range(heads):
        dkvs[:, :, h * HD : (h + 1) * HD] = (
            dka[h, :, one(oc)].reshape(nz, rows, HD).astype(b16)
        )
        dkvs[:, :, shard + h * HD : shard + (h + 1) * HD] = (
            dva[h, :, one(oc)].reshape(nz, rows, HD).astype(b16)
        )
    dkv_pair = links.start(dkvs, dkvr, to_core)
    tg[...] = matmul_tn(att[...], flat(ra[...])).astype(b16).reshape(tg.shape)
    attn_pair = links.start(tg.at[oc], tgr, to_core)
    red_down[2].third()

    def place(value):
        return jnp.concatenate([jnp.where(dp == k, value, 0.0) for k in range(n)], axis=1)

    sm[2:3] = place(jnp.concatenate([q_sum[h] for h in range(heads)], axis=1))
    v_sum = [
        jnp.sum(dva[h].reshape(2 * nz * rows, HD), axis=0, keepdims=True) for h in range(heads)
    ]
    sm[3:4] = place(jnp.concatenate(v_sum, axis=1))
    dkv_pair.wait_recv()
    for h in range(heads):
        for ref, offset in ((dka, 0), (dva, shard)):
            cols = slice(offset + h * HD, offset + (h + 1) * HD)
            mg[:, cols] = (
                ref[h, :, one(c)].reshape(nz * rows, HD) + flat(dkvr[:, :, cols]).astype(f32)
            ).astype(b16)
    rs_first = []
    for first, count in GROUPS:
        part = matmul_nt(mg[first * rows : (first + count) * rows], flat(mixc[...]))
        p4[first : first + count] = part.astype(b16).reshape(count, n, quarter, width)
        rs_first.append(reduce_out(p4, r4, first, count))
    mgr[...] = matmul_tn(flat(fa[...]), mg[...]).astype(b16).reshape(mgr.shape)
    mix_grad_pair = links.start(mgr.at[:, oc], mgx, to_core)
    red_down[3].third()
    red_up[0].second()

    attn_pair.wait_recv()
    tz[...] = (tg[one(c)].reshape(tz.shape).astype(f32) + tgr[...].astype(f32)).astype(b16)
    red_attn.first()
    mix_grad_pair.wait_recv()
    ms[...] = (mgr[:, one(c)].reshape(ms.shape).astype(f32) + mgx[...].astype(f32)).astype(b16)
    hop_md = scatter_dp(ms, md)
    md[one(dp)] = ms[one(dp)]

    arrived(rs_out)
    out_delta = aft[...] + reduced(p3, r3, 0, nz) + vec(down_bias)
    od[...] = out_delta.astype(b16).reshape(od.shape)
    hop_o = scatter_z(od, oh1)
    oh1[one(z)] = od[one(z)]
    red_up[1].second()
    red_up[0].third()
    each(red_down, "fourth")
    red_up[2].second()
    red_up[1].third()

    gain_sum, shift_sum = 0.0, 0.0
    for (first, count), copies in zip(GROUPS, rs_first):
        arrived(copies)
        at = slice(first * quarter, (first + count) * quarter)
        first_grad = reduced(p4, r4, first, count)
        hat = hat1[at]
        back = res[at] + norm_back(first_grad, hat, rstd1[at], vec(gain1))
        idl[first : first + count] = back.astype(b16).reshape(count, quarter, width)
        gain_sum += jnp.sum(first_grad * hat, axis=0, keepdims=True)
        shift_sum += jnp.sum(first_grad, axis=0, keepdims=True)
    arrived(hop_md)
    each(red_mix, "first")
    hop_i = scatter_z(idl, ih1)
    ih1[one(z)] = idl[one(z)]
    sm[0:1] = gain_sum
    sm[1:2] = shift_sum
    sm1[one(dp)] = sm[...].reshape(1, *sm.shape)
    small_dp = [links.start(sm, sm1.at[dp], to_dp[k]) for k in peers]

    red_up[3].second()
    red_up[2].third()
    red_attn.second()
    red_up[3].third()
    arrived(hop_o)
    hop_o = scatter_dp(oh1, out_o)
    out_o[one(dp)] = oh1[one(dp)]
    red_mix[0].second()
    red_attn.third()
    arrived(small_dp)
    sm2[one(z)] = jnp.sum(sm1[...], axis=0, keepdims=True)
    small_z = [links.start(sm2.at[z], sm2.at[z], to_z[k]) for k in peers]
    red_mix[1].second()
    red_mix[0].third()
    red_mix[2].second()
    red_mix[1].third()
    each(red_up, "fourth")
    red_attn.fourth()
    arrived(hop_i)
    hop_i = scatter_dp(ih1, in_o)
    in_o[one(dp)] = ih1[one(dp)]
    arrived(small_z)
    sm3[one(c)] = jnp.sum(sm2[...], axis=0, keepdims=True)
    small_core = links.start(sm3.at[c], sm3.at[c], to_core)
    red_mix[3].second()
    red_mix[2].third()
    red_mix[3].third()
    each(red_mix, "fourth")
    small_core.wait_recv()
    small_o[...] = sm3[0] + sm3[1]
    each(red_down + red_up + [red_attn] + red_mix, "done")
    arrived(hop_o)
    arrived(hop_i)
    links.finish()


def finish_kernel(
    out_ref, in_ref, mix_ref, attn_ref, up_ref, down_ref, small_ref, x_ref, cot_ref,
    *refs,
):
    f32 = jnp.float32
    outs, mats, sems, xv, cv = refs[:15], refs[15:21], *refs[21:]
    get_x = pltpu.make_async_copy(x_ref, xv, sems.at[6])
    get_x.start()
    get_cot = pltpu.make_async_copy(cot_ref, cv, sems.at[7])
    get_cot.start()
    shard, width = mats[3].shape
    n = mix_ref.shape[0]
    copies = []

    def store(number, target):
        copy = pltpu.make_async_copy(mats[number], target, sems.at[number])
        copy.start()
        copies.append(copy)

    mats[5][...] = flat(down_ref[...]).astype(f32)
    store(5, outs[13])
    mats[4][...] = flat(up_ref[...]).astype(f32)
    store(4, outs[11])
    for d in range(n):
        value = mix_ref[d].reshape(shard, 3 * shard).astype(f32)
        for part, place_at in ((0, 1), (1, 2), (2, 0)):
            start = place_at * width + d * shard
            mats[2][:, start : start + shard] = value[:, part * shard : (part + 1) * shard]
    store(2, outs[4])
    mats[3][...] = flat(attn_ref[...]).astype(f32)
    store(3, outs[7])
    get_x.wait()
    mats[0][...] = xv[...] + flat(out_ref[...]).astype(f32)
    store(0, outs[0])
    get_cot.wait()
    mats[1][...] = cv[...] + flat(in_ref[...]).astype(f32)
    store(1, outs[1])
    for number, row in ((2, 0), (3, 1), (5, 2), (6, 3), (8, 4), (9, 5), (10, 6), (14, 7)):
        outs[number][...] = small_ref[row : row + 1].reshape(width)
    for k in range(n):
        outs[12][k * width : (k + 1) * width] = small_ref[8 + k : 9 + k].reshape(width)
    for copy in copies:
        copy.wait()


def plane_body(
    block_input,
    out_cotangent,
    first_gain,
    first_shift,
    mix_weight,
    query_bias,
    value_bias,
    attn_weight,
    attn_bias,
    second_gain,
    second_shift,
    up_weight,
    up_bias,
    down_weight,
    down_bias,
):
    b16, f32 = jnp.bfloat16, jnp.float32
    n, nz = lax.axis_size("dp"), lax.axis_size("ctx") // 2
    rows, width = block_input.shape[1:]
    quarter = rows // n
    shard = width // n
    half = shard // 2
    hidden = up_weight.shape[1] // n
    heads = H // n
    tokens = nz * rows
    keys = 2 * tokens
    x_rows = block_input.reshape(rows, width)
    cot = out_cotangent.reshape(rows, width)
    vm = pltpu.VMEM
    stack = vm((n, quarter, width), b16)
    part = vm((nz, n, quarter, width), b16)
    part_recv = vm((n - 1, nz, quarter, width), b16)
    own = vm((nz * quarter, width), f32)
    scratch = [
        pltpu.SemaphoreType.DMA((SEMS,)),
        pltpu.SemaphoreType.DMA((SEMS,)),
        pltpu.SemaphoreType.DMA((16,)),
    ] + [vm((width,), f32)] * 7 + [
        vm((n * hidden,), f32), vm((width,), f32),
        vm((rows, width), f32), vm((rows, width), f32),
        vm((half, 3 * width), b16), vm((shard, width), b16), vm((hidden, width), b16),
        stack, stack, stack, stack, stack, stack,
        vm((n, half, 3 * shard), b16), vm((n, 2, half, 3 * shard), b16),
        vm((n, 2, half, hidden), b16), part, part, part, part,
        vm((tokens, shard), b16), vm((nz, 2, rows, 2 * shard), b16),
        vm((heads, keys, HD), b16), vm((heads, keys, HD), b16),
        vm((tokens, shard), b16), vm((heads, tokens, 1), f32), vm((tokens, shard), b16),
        own, own, own, own,
        part, part, part, part, part_recv, part_recv, part_recv, part_recv,
        vm((tokens, hidden), f32), vm((tokens, hidden), b16), vm((tokens, hidden), b16),
        vm((2, hidden // 2, width), b16),
    ] + [vm((hidden // 2, width), b16)] * 4 + [
        vm((n, 2, half, hidden), b16), vm((n, half, hidden), b16), vm((n, half, hidden), b16),
    ] + [vm((half, n * hidden), b16)] * 3 + [
        vm((2, half, width), b16),
    ] + [vm((half, width), b16)] * 4 + [
        vm((heads, nz, 2, rows, HD), f32), vm((heads, nz, 2, rows, HD), f32),
        vm((nz, rows, 2 * shard), b16), vm((nz, rows, 2 * shard), b16),
        vm((tokens, 3 * shard), b16),
        vm((n, 2, half, 3 * shard), b16),
    ] + [vm((n, half, 3 * shard), b16)] * 5 + [
        stack, stack, stack, stack,
        vm((16, width), f32), vm((n, 16, width), f32), vm((nz, 16, width), f32),
        vm((2, 16, width), f32),
    ]
    hbm = pl.BlockSpec(memory_space=pl.ANY)
    near = pl.BlockSpec(memory_space=pltpu.VMEM)
    far = pl.BlockSpec(memory_space=pltpu.HBM)
    shapes = [
        ((n, quarter, width), b16),
        ((n, quarter, width), b16),
        ((n, 2, half, 3 * shard), b16),
        ((2, half, width), b16),
        ((2, half, n * hidden), b16),
        ((2, hidden // 2, width), b16),
        ((16, width), f32),
    ]
    pieces = pl.pallas_call(
        plane_kernel,
        out_shape=[jax.ShapeDtypeStruct(shape, dtype) for shape, dtype in shapes],
        in_specs=[far] * 15,
        out_specs=[near] * len(shapes),
        scratch_shapes=scratch,
        compiler_params=pltpu.CompilerParams(
            collective_id=0, has_side_effects=True, vmem_limit_bytes=60 * 1024 * 1024
        ),
        name="plane",
    )(
        x_rows, cot, first_gain, first_shift, mix_weight, query_bias, value_bias, attn_weight,
        attn_bias, second_gain, second_shift, up_weight, up_bias, down_weight, down_bias,
    )
    final = [
        (rows, width), (rows, width), (width,), (width,), (shard, 3 * width), (width,), (width,),
        (shard, width), (width,), (width,), (width,), (shard, n * hidden), (n * hidden,),
        (hidden, width), (width,),
    ]
    large = (0, 1, 4, 7, 11, 13)
    outs = pl.pallas_call(
        finish_kernel,
        out_shape=[jax.ShapeDtypeStruct(shape, f32) for shape in final],
        in_specs=[near] * 7 + [far] * 2,
        out_specs=[hbm if k in large else near for k in range(len(final))],
        scratch_shapes=[vm(final[k], f32) for k in large] + [
            pltpu.SemaphoreType.DMA((8,)), vm((rows, width), f32), vm((rows, width), f32)
        ],
        compiler_params=pltpu.CompilerParams(vmem_limit_bytes=60 * 1024 * 1024),
        name="finish",
    )(*pieces, x_rows, cot)
    return (
        outs[0].reshape(1, rows, width),
        outs[1].reshape(1, rows, width),
        *outs[2:],
    )


def fits(mesh):
    n, ctx = mesh.shape["dp"], mesh.shape["ctx"]
    return n == 4 and ctx == 8 and H % n == 0


def solution(mesh):
    placed = (
        P("dp", "ctx", None),
        P("dp", "ctx", None),
        P(),
        P(),
        P("dp", None),
        P(),
        P(),
        P("dp", None),
        P(),
        P(),
        P(),
        P("dp", None),
        P(),
        P("dp", None),
        P(),
    )
    return jax.shard_map(
        plane_body if fits(mesh) else body,
        mesh=mesh,
        in_specs=placed,
        out_specs=(
            P("dp", "ctx", None),
            P("dp", "ctx", None),
            P(),
            P(),
            P("dp", None),
            P(),
            P(),
            P("dp", None),
            P(),
            P(),
            P(),
            P("dp", None),
            P(),
            P("dp", None),
            P(),
        ),
        check_vma=False,
    )
```

```python
import functools
import math

import jax
import jax.numpy as jnp
from jax import lax
from jax.experimental import pallas as pl
from jax.experimental.pallas import tpu as pltpu
from jax.sharding import PartitionSpec as P

H = 12
HD = 64


EPS = 1e-05
GELU_C = math.sqrt(2.0 / math.pi)


def from_behind(value, axis, steps):
    count = lax.axis_size(axis)
    pairs = [(source, (source + steps) % count) for source in range(count)]
    return lax.ppermute(value, axis, pairs)


def layer_norm(x, gain, shift):
    centered = x - jnp.mean(x, axis=-1, keepdims=True)
    rstd = lax.rsqrt(jnp.mean(centered * centered, axis=-1, keepdims=True) + EPS)
    x_hat = centered * rstd
    return (x_hat, rstd, x_hat * gain + shift)


def norm_back(grad, x_hat, rstd, gain):
    g = grad * gain
    return rstd * (
        g
        - jnp.mean(g, axis=-1, keepdims=True)
        - x_hat * jnp.mean(g * x_hat, axis=-1, keepdims=True)
    )


def gelu_pair(u):
    inner = GELU_C * (u + 0.044715 * u * u * u)
    t = jnp.tanh(inner)
    value = 0.5 * u * (1.0 + t)
    slope = 0.5 * (1.0 + t) + 0.5 * u * (1.0 - t * t) * GELU_C * (1.0 + 3.0 * 0.044715 * u * u)
    return (value, slope)


def matmul(a, b):
    return jnp.dot(a, b, preferred_element_type=jnp.float32)


def matmul_tn(a, b):
    return lax.dot_general(a, b, (((0,), (0,)), ((), ())), preferred_element_type=jnp.float32)


def matmul_nt(a, b):
    return lax.dot_general(a, b, (((1,), (1,)), ((), ())), preferred_element_type=jnp.float32)


def body(
    block_input,
    out_cotangent,
    first_gain,
    first_shift,
    mix_weight,
    query_bias,
    value_bias,
    attn_weight,
    attn_bias,
    second_gain,
    second_shift,
    up_weight,
    up_bias,
    down_weight,
    down_bias,
):
    rows = block_input.shape[1]
    width = block_input.shape[2]
    scale = HD ** (-0.5)
    x_rows = block_input.reshape(rows, width)
    cot = out_cotangent.reshape(rows, width)
    mix_full, attn_full, up_full, down_full = (
        lax.all_gather(mix_weight, "dp", axis=0, tiled=True),
        lax.all_gather(attn_weight, "dp", axis=0, tiled=True),
        lax.all_gather(up_weight, "dp", axis=0, tiled=True),
        lax.all_gather(down_weight, "dp", axis=0, tiled=True),
    )
    first_hat, first_rstd, first_out = layer_norm(x_rows, first_gain, first_shift)
    first_in = first_out.astype(jnp.bfloat16)
    mixed = matmul(first_in, mix_full)
    queries = (mixed[:, :width] + query_bias).astype(jnp.bfloat16)
    keys = mixed[:, width : 2 * width].astype(jnp.bfloat16)
    values = (mixed[:, 2 * width :] + value_bias).astype(jnp.bfloat16)
    q3 = queries.reshape(rows, H, HD)
    me = lax.axis_index("ctx")
    cycle_size = lax.axis_size("ctx")
    q_pos = me * rows + jnp.arange(rows)
    q_last = me * rows + rows - 1
    start_state = (
        jnp.full((H, rows), -1e30, jnp.float32),
        jnp.zeros((H, rows), jnp.float32),
        jnp.zeros((H, rows, HD), jnp.float32),
    )
    carry = start_state
    key_piece = lax.all_gather(keys, "ctx", axis=0, tiled=True)
    value_piece = lax.all_gather(values, "ctx", axis=0, tiled=True)
    count = key_piece.shape[0]
    kblock = math.gcd(count, 512)
    nblocks = count // kblock
    key_blocks = key_piece.reshape(nblocks, kblock, H, HD)
    value_blocks = value_piece.reshape(nblocks, kblock, H, HD)
    offsets = jnp.arange(nblocks) * kblock

    def one_block(state, item):
        key_blk, value_blk, offset = item

        def compute(state_in):
            run_max, run_total, run_acc = state_in
            key_pos = offset + jnp.arange(kblock)
            allowed = (key_pos[None, :] <= q_pos[:, None])[None]
            scores = (
                jnp.einsum("qhd,khd->hqk", q3, key_blk, preferred_element_type=jnp.float32) * scale
            )
            scores = jnp.where(allowed, scores, -1e30)
            new_max = jnp.maximum(run_max, jnp.max(scores, axis=-1))
            expo = jnp.where(allowed, jnp.exp(scores - new_max[..., None]), 0.0)
            factor = jnp.exp(run_max - new_max)
            new_total = run_total * factor + jnp.sum(expo, axis=-1)
            new_acc = run_acc * factor[..., None] + jnp.einsum(
                "hqk,khd->hqd", expo, value_blk.astype(jnp.float32), precision=lax.Precision.HIGHEST
            )
            return (new_max, new_total, new_acc)

        def keep_state(state_in):
            return state_in

        return (lax.cond(offset <= q_last, compute, keep_state, state), None)

    carry, unused = lax.scan(one_block, carry, (key_blocks, value_blocks, offsets))
    run_max, run_total, run_acc = carry
    attended = (
        (run_acc / run_total[..., None])
        .transpose(1, 0, 2)
        .reshape(rows, width)
        .astype(jnp.bfloat16)
    )
    lse = run_max + jnp.log(run_total)
    after_attn = x_rows + matmul(attended, attn_full) + attn_bias
    second_hat, second_rstd, second_out = layer_norm(after_attn, second_gain, second_shift)
    second_in = second_out.astype(jnp.bfloat16)
    pre_act = matmul(second_in, up_full) + up_bias
    act_value, act_slope = gelu_pair(pre_act)
    activ = act_value.astype(jnp.bfloat16)
    block_output = after_attn + matmul(activ, down_full) + down_bias
    mix_back, attn_back, up_back, down_back = (
        lax.all_gather(mix_weight, "dp", axis=0, tiled=True),
        lax.all_gather(attn_weight, "dp", axis=0, tiled=True),
        lax.all_gather(up_weight, "dp", axis=0, tiled=True),
        lax.all_gather(down_weight, "dp", axis=0, tiled=True),
    )
    cot_b = cot.astype(jnp.bfloat16)
    down_weight_grad = matmul_tn(activ, cot_b)
    down_bias_grad = jnp.sum(cot, axis=0)
    pre_grad = matmul_nt(cot_b, down_back) * act_slope
    pre_grad_b = pre_grad.astype(jnp.bfloat16)
    up_weight_grad = matmul_tn(second_in, pre_grad_b)
    up_bias_grad = jnp.sum(pre_grad, axis=0)
    second_grad = matmul_nt(pre_grad_b, up_back)
    second_gain_grad = jnp.sum(second_grad * second_hat, axis=0)
    second_shift_grad = jnp.sum(second_grad, axis=0)
    resid_grad = cot + norm_back(second_grad, second_hat, second_rstd, second_gain)
    resid_b = resid_grad.astype(jnp.bfloat16)
    attn_weight_grad = matmul_tn(attended, resid_b)
    attn_bias_grad = jnp.sum(resid_grad, axis=0)
    attended_grad = matmul_nt(resid_b, attn_back).astype(jnp.bfloat16)
    grad3 = attended_grad.reshape(rows, H, HD)
    delta = jnp.sum(
        grad3.astype(jnp.float32) * attended.astype(jnp.float32).reshape(rows, H, HD), axis=-1
    ).T

    def block_grads(key_blk, value_blk, key_start):
        count = key_blk.shape[0]
        key3 = key_blk.reshape(count, H, HD)
        value3 = value_blk.reshape(count, H, HD)
        key_pos = key_start + jnp.arange(count)
        allowed = (key_pos[None, :] <= q_pos[:, None])[None]
        scores = jnp.einsum("qhd,khd->hqk", q3, key3, preferred_element_type=jnp.float32) * scale
        probs = jnp.where(allowed, jnp.exp(scores - lse[..., None]), 0.0)
        dprob = jnp.einsum("qhd,khd->hqk", grad3, value3, preferred_element_type=jnp.float32)
        dscore = probs * (dprob - delta[..., None])
        probs_b = probs.astype(jnp.bfloat16)
        dscore_b = dscore.astype(jnp.bfloat16)
        value_add = jnp.einsum("hqk,qhd->khd", probs_b, grad3, preferred_element_type=jnp.float32)
        key_add = (
            jnp.einsum("hqk,qhd->khd", dscore_b, q3, preferred_element_type=jnp.float32) * scale
        )
        query_add = (
            jnp.einsum("hqk,khd->qhd", dscore_b, key3, preferred_element_type=jnp.float32) * scale
        )
        return (
            query_add.reshape(rows, width),
            key_add.reshape(count, width),
            value_add.reshape(count, width),
        )

    def skip_grads(key_blk, value_blk, key_start):
        count = key_blk.shape[0]
        empty = jnp.zeros((count, width), jnp.float32)
        return (jnp.zeros((rows, width), jnp.float32), empty, empty)

    zeros = jnp.zeros((rows, width), jnp.float32)

    def pass_grads(key_acc, value_acc):
        return (
            from_behind(key_acc.astype(jnp.bfloat16), "ctx", -1).astype(key_acc.dtype),
            from_behind(value_acc.astype(jnp.bfloat16), "ctx", -1).astype(value_acc.dtype),
        )

    def cycle_turn(step, state):
        key_blk, value_blk, key_acc, value_acc, query_acc = state
        owner = (me + step) % cycle_size
        query_add, key_add, value_add = lax.cond(
            owner <= me, block_grads, skip_grads, key_blk, value_blk, owner * rows
        )
        key_blk, value_blk = from_behind((key_blk, value_blk), "ctx", -1)
        key_acc, value_acc = pass_grads(key_acc + key_add, value_acc + value_add)
        return (key_blk, value_blk, key_acc, value_acc, query_acc + query_add)

    key_blk, value_blk, key_acc, value_acc, query_acc = lax.fori_loop(
        0, cycle_size - 1, cycle_turn, (keys, values, zeros, zeros, zeros)
    )
    last_owner = (me + cycle_size - 1) % cycle_size
    query_add, key_add, value_add = lax.cond(
        last_owner <= me, block_grads, skip_grads, key_blk, value_blk, last_owner * rows
    )
    key_grad, value_grad = pass_grads(key_acc + key_add, value_acc + value_add)
    query_grad = query_acc + query_add
    query_bias_grad = jnp.sum(query_grad, axis=0)
    value_bias_grad = jnp.sum(value_grad, axis=0)
    mixed_grad = jnp.concatenate([query_grad, key_grad, value_grad], axis=1).astype(jnp.bfloat16)
    mix_weight_grad = matmul_tn(first_in, mixed_grad)
    first_grad = matmul_nt(mixed_grad, mix_back)
    first_gain_grad = jnp.sum(first_grad * first_hat, axis=0)
    first_shift_grad = jnp.sum(first_grad, axis=0)
    input_grad = resid_grad + norm_back(first_grad, first_hat, first_rstd, first_gain)
    local_mats = (mix_weight_grad, attn_weight_grad, up_weight_grad, down_weight_grad)
    shard_sums = (
        lax.psum_scatter(
            local_mats[0].astype(jnp.bfloat16), "dp", scatter_dimension=0, tiled=True
        ).astype(jnp.float32),
        lax.psum_scatter(
            local_mats[1].astype(jnp.bfloat16), "dp", scatter_dimension=0, tiled=True
        ).astype(jnp.float32),
        lax.psum_scatter(
            local_mats[2].astype(jnp.bfloat16), "dp", scatter_dimension=0, tiled=True
        ).astype(jnp.float32),
        lax.psum_scatter(
            local_mats[3].astype(jnp.bfloat16), "dp", scatter_dimension=0, tiled=True
        ).astype(jnp.float32),
    )
    mats = (
        lax.psum(shard_sums[0].astype(jnp.bfloat16), "ctx").astype(jnp.float32),
        lax.psum(shard_sums[1].astype(jnp.bfloat16), "ctx").astype(jnp.float32),
        lax.psum(shard_sums[2].astype(jnp.bfloat16), "ctx").astype(jnp.float32),
        lax.psum(shard_sums[3].astype(jnp.bfloat16), "ctx").astype(jnp.float32),
    )
    smalls = lax.psum(
        (
            first_gain_grad,
            first_shift_grad,
            query_bias_grad,
            value_bias_grad,
            attn_bias_grad,
            second_gain_grad,
            second_shift_grad,
            up_bias_grad,
            down_bias_grad,
        ),
        ("dp", "ctx"),
    )
    return (
        block_output.reshape(1, rows, width),
        input_grad.reshape(1, rows, width),
        smalls[0],
        smalls[1],
        mats[0],
        smalls[2],
        smalls[3],
        mats[1],
        smalls[4],
        smalls[5],
        smalls[6],
        mats[2],
        smalls[7],
        mats[3],
        smalls[8],
    )


def flip(index, mask):
    bit = 1
    while bit <= mask:
        if mask & bit:
            index = index + bit - 2 * bit * ((index // bit) % 2)
        bit *= 2
    return index


MESH = pl.DeviceIdType.MESH
GROUPS = ((2, 2), (0, 2))
SEMS = 224


class Links:
    def __init__(self, send, recv):
        self.send, self.recv, self.count, self.open = send, recv, 0, []

    def make(self, source, target, device):
        number = self.count
        self.count += 1
        return pltpu.make_async_remote_copy(
            src_ref=source,
            dst_ref=target,
            send_sem=self.send.at[number],
            recv_sem=self.recv.at[number],
            device_id=device,
            device_id_type=MESH,
        )

    def start(self, source, target, device):
        copy = self.make(source, target, device)
        copy.start()
        self.open.append(copy)
        return copy

    def finish(self):
        for copy in self.open:
            copy.wait_send()


def arrived(copies):
    for copy in copies:
        copy.wait_recv()


def flat(value):
    return value.reshape(-1, value.shape[-1])


def plane_kernel(
    x_in, cot_in, gain1_in, shift1_in, mix_w, q_bias_in, v_bias_in, attn_w, attn_bias_in, gain2_in,
    shift2_in, up_w, up_bias_in, down_w, down_bias_in,
    out_o, in_o, mix_o, attn_o, up_o, down_o, small_o,
    send_sem, recv_sem, local_sem,
    gain1, shift1, q_bias, v_bias, attn_bias, gain2, shift2, up_bias, down_bias,
    xv, cv, mw, aw, dw,
    xs, xh1, xh2, cs, ch1, ch2,
    mst, mixc, upc, fa, ca, sa, ra,
    qs, kv, kh, vh, att, lse, agr,
    hat1, aft, hat2, res,
    p1, p2, p3, p4, r1, r2, r3, r4, t1, t2, t3, t4,
    dact, act, pg,
    dg, dgr, dz, dz1, dz2,
    ug, ugr, us, ud, uz1, uz2,
    tg, tgr, tz, tz1, tz2,
    dka, dva, dkvs, dkvr, mg,
    mgr, mgx, ms, md, mz1, mz2,
    od, oh1, idl, ih1,
    sm, sm1, sm2, sm3,
):
    b16, f32 = jnp.bfloat16, jnp.float32
    n, quarter, width = xs.shape
    nz = xh2.shape[0]
    rows = n * quarter
    half, hidden = mixc.shape[2], upc.shape[3]
    shard = 2 * half
    heads = kh.shape[0]
    dp, ctx = lax.axis_index("dp"), lax.axis_index("ctx")
    z, c = ctx // 2, ctx % 2
    oc = 1 - c
    dps = [flip(dp, k) for k in range(n)]
    zs = [flip(z, k) for k in range(nz)]
    to_dp = [(dps[k], ctx) for k in range(n)]
    to_z = [(dp, 2 * zs[k] + c) for k in range(nz)]
    to_core = (dp, 2 * z + oc)
    inner = (z + 1) // 2 % 2 == 1
    outer = (z + 1) // 2 % 2 == 0
    peers = (3, 1, 2)
    links = Links(send_sem, recv_sem)
    one = lambda index: pl.ds(index, 1)

    locals_ = []

    def fetch(source, target):
        copy = pltpu.make_async_copy(source, target, local_sem.at[len(locals_)])
        copy.start()
        locals_.append(copy)
        return copy

    my_half = pl.ds(pl.multiple_of(c * half, 16), half)
    get_x = fetch(x_in, xv)
    get_mix = fetch(mix_w.at[my_half], mw)
    get_cot = fetch(cot_in, cv)
    get_vectors = [
        fetch(source, target)
        for source, target in (
            (gain1_in, gain1), (shift1_in, shift1), (q_bias_in, q_bias), (v_bias_in, v_bias),
            (attn_bias_in, attn_bias), (gain2_in, gain2), (shift2_in, shift2),
            (up_bias_in, up_bias), (down_bias_in, down_bias),
        )
    ]
    get_attn = fetch(attn_w, aw)
    get_down = fetch(down_w, dw)
    columns = lambda index: pl.ds(pl.multiple_of(index * hidden, 128), hidden)
    strip = shard // nz
    up_rows = pl.ds(pl.multiple_of(z * strip, 16), strip)
    up_half = lambda index: pl.ds(pl.multiple_of(index * (hidden // 2), 128), hidden // 2)
    up_piece = lambda index: up_w.at[
        up_rows, pl.ds(pl.multiple_of(index * hidden + c * (hidden // 2), 128), hidden // 2)
    ]
    get_up = fetch(up_piece(dp), upc.at[dp, z, :, up_half(c)])

    barrier = pltpu.get_barrier_semaphore()
    everyone = to_dp[1:] + to_z[1:] + [to_core]
    for device in everyone:
        pl.semaphore_signal(barrier, inc=1, device_id=device, device_id_type=MESH)

    get_x.wait()
    xs[...] = xv[...].astype(b16).reshape(n, quarter, width)
    get_mix.wait()
    mv = mw[...]
    for d in range(n):
        mst[d] = jnp.concatenate(
            [mv[:, part * width + d * shard : part * width + (d + 1) * shard] for part in (1, 2, 0)],
            axis=1,
        )
    mixc[one(dp), one(c)] = mst[one(dp)].reshape(1, 1, half, 3 * shard)
    pl.semaphore_wait(barrier, len(everyone))

    def scatter_dp(source, target):
        return [links.start(source.at[dps[k]], target.at[dp], to_dp[k]) for k in peers]

    def scatter_z(source, target):
        return [links.start(source.at[zs[k]], target.at[z], to_z[k]) for k in peers]

    class Gather:
        def __init__(self, ref, first, count):
            self.ref, self.first, self.mid = ref, first, first + count // 2
            part = ref.at[pl.ds(first, count), dp]
            self.near = [links.start(part, part, to_dp[k]) for k in (1, 2)]

        def forward(self):
            arrived(self.near)
            self.far = []
            for begin, origin, target in ((self.first, 1, 2), (self.mid, 2, 1)):
                part = self.ref.at[pl.ds(begin, self.mid - self.first), dps[origin]]
                self.far.append(links.start(part, part, to_dp[target]))

        def wait(self):
            arrived(self.far)

    class Scatter:
        def __init__(self, ref, recv, stage, first, count):
            self.ref, self.recv, self.stage = ref, recv, stage
            self.first, self.count, step = first, count, count // 2
            self.ways = ((first, step, 1, 2), (first + step, step, 2, 1))
            self.pass_on, self.mine = [], []
            for begin, size, near, _ in self.ways:
                for role, slot, copies in ((1, 3, self.pass_on), (0, near, self.mine)):
                    source = ref.at[pl.ds(begin, size), dps[slot]]
                    target = recv.at[role, pl.ds(begin, size)]
                    copies.append(links.start(source, target, to_dp[near]))

        def forward(self):
            self.last = []
            for (begin, size, _, beyond), copy in zip(self.ways, self.pass_on):
                copy.wait_recv()
                at = pl.ds(begin, size)
                value = self.ref[at, one(dps[beyond])].astype(f32).reshape(size, quarter, width)
                value = value + self.recv[1, at].astype(f32)
                self.stage[at] = value.astype(b16)
                self.last.append(
                    links.start(self.stage.at[at], self.recv.at[2, at], to_dp[beyond])
                )

        def result(self):
            arrived(self.mine)
            arrived(self.last)
            at = slice(self.first, self.first + self.count)
            total = self.ref[at, one(dp)].astype(f32).reshape(self.count * quarter, width)
            return total + flat(self.recv[0, at].astype(f32)) + flat(self.recv[2, at].astype(f32))

    def run(items, step):
        for item in items:
            getattr(item, step)()

    hop_x = scatter_dp(xs, xh1)
    xh1[one(dp)] = xs[one(dp)]
    for copy in [get_cot] + get_vectors:
        copy.wait()
    cot = cv[...]
    cs[...] = cot.astype(b16).reshape(n, quarter, width)
    ch1[one(dp)] = cs[one(dp)]
    arrived(hop_x)
    hop_x = scatter_z(xh1, xh2)
    hop_mix = [links.start(mst.at[dps[k]], mixc.at[dp, c], to_dp[k]) for k in peers]
    hop_c = scatter_dp(cs, ch1)
    xh2[one(z)] = xh1[one(z)]
    sm[...] = jnp.zeros(sm.shape, f32)
    sm[7:8] = jnp.sum(cot, axis=0, keepdims=True)

    vec = lambda ref: ref[...].reshape(1, -1)

    def pick(ref, size):
        value = vec(ref)
        total = jnp.zeros((1, size), f32)
        for k in range(n):
            total = jnp.where(dp == k, value[:, k * size : (k + 1) * size], total)
        return total

    arrived(hop_x)
    x_hat, rstd1, first = layer_norm(flat(xh2[...]).astype(f32), vec(gain1), vec(shift1))
    hat1[...] = x_hat
    fa[:, one(dp)] = first.astype(b16).reshape(nz, 1, quarter, width)
    ag_first = [Gather(fa, first, count) for first, count in GROUPS]
    kv_bias = jnp.concatenate([jnp.zeros((1, shard), f32), pick(v_bias, shard)], axis=1)
    own_q_bias = pick(q_bias, shard)
    arrived(hop_mix)
    mix_pair = links.start(mixc.at[:, c], mixc.at[:, c], to_core)
    arrived(hop_c)
    hop_c = scatter_z(ch1, ch2)
    ch2[one(z)] = ch1[one(z)]

    run(ag_first, "forward")
    run(ag_first, "wait")
    hop_up = [
        links.start(up_piece(dps[k]), upc.at[dp, z, :, up_half(c)], to_dp[k]) for k in peers
    ]
    arrived(hop_c)
    ca[:, one(dp)] = ch2[...].reshape(nz, 1, quarter, width)
    ag_cot = Gather(ca, 0, nz)
    mix_pair.wait_recv()
    first_all = flat(fa[...])
    mixed = matmul(first_all, flat(mixc[:, :, :, : 2 * shard])) + kv_bias
    kv[:, one(c)] = mixed.astype(b16).reshape(nz, 1, rows, 2 * shard)
    kv_pair = links.start(kv.at[:, c], kv.at[:, c], to_core)
    scale = HD ** (-0.5)
    queries = matmul(first_all, flat(mixc[:, :, :, 2 * shard :])) + own_q_bias
    qs[...] = (queries * scale).astype(b16)
    arrived(hop_up)
    get_up.wait()
    up_strip = upc.at[:, z, :, up_half(c)]
    hop_up = [links.start(up_strip, up_strip, to_z[k]) for k in peers]
    kv_pair.wait_recv()
    for h in range(heads):
        kh[h] = flat(kv[:, :, :, h * HD : (h + 1) * HD])
        vh[h] = flat(kv[:, :, :, shard + h * HD : shard + (h + 1) * HD])

    last = 2 * rows
    allowed = (
        lax.broadcasted_iota(jnp.int32, (rows, last), 1)
        <= lax.broadcasted_iota(jnp.int32, (rows, last), 0) + c * rows
    )

    def spans(j):
        return ([(0, j * last)] if j else []) + [(j * last, (j + 1) * last)]

    def attend(j):
        at = slice(j * rows, (j + 1) * rows)
        for h in range(heads):
            q = qs[at, h * HD : (h + 1) * HD]
            scores = []
            for a, b in spans(j):
                s = matmul_nt(q, kh[h, a:b])
                scores.append(jnp.where(allowed, s, -1e30) if b == (j + 1) * last else s)
            top = functools.reduce(
                jnp.maximum, [jnp.max(s, axis=-1, keepdims=True) for s in scores]
            )
            total, result = 0.0, 0.0
            for s, (a, b) in zip(scores, spans(j)):
                w = jnp.exp(s - top)
                total = total + jnp.sum(w, axis=-1, keepdims=True)
                result = result + matmul(w.astype(b16), vh[h, a:b])
            att[at, h * HD : (h + 1) * HD] = (result / total).astype(b16)
            lse[h, at] = top + jnp.log(total)

    get_attn.wait()
    ag_cot.forward()
    rs_attn = []
    for first, count in GROUPS:
        for j in range(first + count - 1, first - 1, -1):
            attend(j)
            if rs_attn and j == 1:
                rs_attn[0].forward()
        part = matmul(att[first * rows : (first + count) * rows], aw[...])
        p1[first : first + count] = part.astype(b16).reshape(count, n, quarter, width)
        rs_attn.append(Scatter(p1, r1, t1, first, count))

    arrived(hop_up)
    up_pair = links.start(upc.at[:, :, :, up_half(c)], upc.at[:, :, :, up_half(c)], to_core)
    get_down.wait()
    ag_cot.wait()
    for first, count in GROUPS:
        if first == GROUPS[1][0]:
            rs_attn[1].forward()
        dact[first * rows : (first + count) * rows] = matmul_nt(
            flat(ca[first : first + count]), dw[...]
        )

    ag_second, rstd2 = [], []
    for (first, count), item in zip(GROUPS, rs_attn):
        at = slice(first * quarter, (first + count) * quarter)
        after = item.result() + vec(attn_bias)
        aft[at] = after
        after = after + flat(xh2[first : first + count]).astype(f32)
        hat, rstd, second = layer_norm(after, vec(gain2), vec(shift2))
        hat2[at] = hat
        rstd2.append(rstd)
        sa[first : first + count, one(dp)] = second.astype(b16).reshape(count, 1, quarter, width)
        ag_second.append(Gather(sa, first, count))

    run(ag_second, "forward")
    up_pair.wait_recv()
    own_up_bias = up_bias[columns(dp)].reshape(1, hidden)
    up_sum = jnp.zeros((1, hidden), f32)
    rs_second = []
    for (first, count), item in zip(GROUPS, ag_second):
        item.wait()
        at = slice(first * rows, (first + count) * rows)
        pre_act = matmul(flat(sa[first : first + count]), flat(upc[...])) + own_up_bias
        value, slope = gelu_pair(pre_act)
        act[at] = value.astype(b16)
        if rs_second:
            rs_second[0].forward()
        pre_grad = dact[at] * slope
        up_sum += jnp.sum(pre_grad, axis=0, keepdims=True)
        pg[at] = pre_grad.astype(b16)
        part = matmul_nt(pg[at], flat(upc[...]))
        p2[first : first + count] = part.astype(b16).reshape(count, n, quarter, width)
        rs_second.append(Scatter(p2, r2, t2, first, count))
    for k in range(n):
        sm[8 + k : 9 + k] = jnp.where(dp == k, up_sum, 0.0)

    dg[...] = matmul_tn(act[...], flat(ca[...])).astype(b16).reshape(dg.shape)
    down_pair = links.start(dg.at[oc], dgr, to_core)
    rs_second[1].forward()
    ug[...] = matmul_tn(flat(sa[...]), pg[...]).astype(b16).reshape(ug.shape)
    up_grad_pair = links.start(ug.at[:, oc], ugr, to_core)

    class Reduce:
        def __init__(self, mine, sum1, sum2, total):
            self.mine, self.sum1, self.sum2, self.total = mine, sum1, sum2, total
            self.one = links.make(mine, sum1, to_z[1])
            self.two = links.make(mine, sum2, to_z[3])
            self.three = links.make(total, total, to_z[1])
            self.pair = links.make(total, total, to_core)

        def first(self):
            pl.when(outer)(lambda: self.one.start())

        def second(self):
            @pl.when(inner)
            def _():
                self.one.wait_recv()
                value = self.mine[...].astype(f32) + self.sum1[...].astype(f32)
                self.mine[...] = value.astype(b16)
                self.two.start()

        def third(self):
            @pl.when(inner)
            def _():
                self.two.wait_recv()
                value = self.mine[...].astype(f32) + self.sum2[...].astype(f32)
                self.total[...] = value.astype(b16).reshape(self.total.shape)
                self.three.start()
                self.pair.start()

        def fourth(self):
            @pl.when(outer)
            def _():
                self.three.wait_recv()
                self.pair.start()

        def done(self):
            self.pair.wait()

            @pl.when(outer)
            def _():
                self.one.wait_send()

            @pl.when(inner)
            def _():
                self.two.wait_send()
                self.three.wait_send()

    down_pair.wait_recv()
    dz[...] = (dg[one(c)].reshape(dz.shape).astype(f32) + dgr[...].astype(f32)).astype(b16)
    size = dz.shape[0] // n
    red_down = [
        Reduce(dz.at[part], dz1.at[part], dz2.at[part], down_o.at[c, part])
        for part in [pl.ds(k * size, size) for k in range(n)]
    ]
    run(red_down, "first")
    up_grad_pair.wait_recv()
    us[...] = (ug[:, one(c)].reshape(us.shape).astype(f32) + ugr[...].astype(f32)).astype(b16)
    ud[:, columns(dp)] = us[one(dp)].reshape(half, hidden)
    red_up = [
        Reduce(ud.at[:, part], uz1.at[:, part], uz2.at[:, part], up_o.at[c, :, part])
        for part in [columns(dps[k]) for k in range(n)]
    ]
    red_up[0].first()

    ag_resid = []
    gain_sum, shift_sum, bias_sum = 0.0, 0.0, 0.0
    for (first, count), item, rstd in zip(GROUPS, rs_second, rstd2):
        at = slice(first * quarter, (first + count) * quarter)
        second_grad = item.result()
        hat = hat2[at]
        back = norm_back(second_grad, hat, rstd, vec(gain2))
        res[at] = back
        resid = flat(ch2[first : first + count]).astype(f32) + back
        ra[first : first + count, one(dp)] = resid.astype(b16).reshape(count, 1, quarter, width)
        ag_resid.append(Gather(ra, first, count))
        gain_sum += jnp.sum(second_grad * hat, axis=0, keepdims=True)
        shift_sum += jnp.sum(second_grad, axis=0, keepdims=True)
        bias_sum += jnp.sum(resid, axis=0, keepdims=True)
    sm[4:5] = bias_sum
    sm[5:6] = gain_sum
    sm[6:7] = shift_sum

    run(ag_resid, "forward")
    hop_ud = [links.start(us.at[dps[k]], ud.at[:, columns(dp)], to_dp[k]) for k in (1, 2, 3)]
    part = matmul(act[...], dw[...])
    p3[...] = part.astype(b16).reshape(p3.shape)
    rs_out = Scatter(p3, r3, t3, 0, nz)
    red_down[0].second()

    def attend_back(j, fresh):
        at = slice(j * rows, (j + 1) * rows)
        for h in range(heads):
            cols = slice(h * HD, (h + 1) * HD)
            q, grad = qs[at, cols], agr[at, cols]
            delta = jnp.sum(grad.astype(f32) * att[at, cols].astype(f32), axis=-1, keepdims=True)
            base, total = lse[h, at], 0.0
            for a, b in spans(j):
                keys = kh[h, a:b]
                p = jnp.exp(matmul_nt(q, keys) - base)
                if b == (j + 1) * last:
                    p = jnp.where(allowed, p, 0.0)
                ds = (p * (matmul_nt(grad, vh[h, a:b]) - delta)).astype(b16)
                total = total + matmul(ds, keys)
                shape = ((b - a) // last, 2, rows, HD)
                dk = matmul_tn(ds, q).reshape(shape)
                dv = matmul_tn(p.astype(b16), grad).reshape(shape)
                blocks = slice(a // last, b // last)
                if fresh:
                    dka[h, blocks], dva[h, blocks] = dk, dv
                else:
                    dka[h, blocks] += dk
                    dva[h, blocks] += dv
            total = total * scale
            q_sum[h] = q_sum.get(h, 0.0) + jnp.sum(total, axis=0, keepdims=True)
            mg[at, 2 * shard + h * HD : 2 * shard + (h + 1) * HD] = total.astype(b16)

    q_sum = {}
    red_attn = Reduce(tz, tz1, tz2, attn_o.at[c])
    red_mix = [
        Reduce(md.at[dps[k]], mz1.at[k], mz2.at[k], mix_o.at[dps[k], c]) for k in range(n)
    ]

    def weights_of(first, count):
        return matmul_nt(flat(ra[first : first + count]), aw[...]).astype(b16)

    (first, count), (first2, count2) = GROUPS
    ag_resid[0].wait()
    agr[first * rows : (first + count) * rows] = weights_of(first, count)
    red_down[1].second()
    attend_back(3, True)
    red_down[0].third()
    red_down[2].second()
    attend_back(2, False)
    red_down[1].third()
    ag_resid[1].wait()
    agr[first2 * rows : (first2 + count2) * rows] = weights_of(first2, count2)
    attend_back(1, False)
    red_down[3].second()
    red_down[2].third()
    for copy, item in zip(hop_ud[:2], red_up[1:3]):
        copy.wait_recv()
        item.first()
    attend_back(0, False)
    hop_ud[2].wait_recv()
    red_up[3].first()
    red_up[0].second()

    for h in range(heads):
        dkvs[:, :, h * HD : (h + 1) * HD] = (
            dka[h, :, one(oc)].reshape(nz, rows, HD).astype(b16)
        )
        dkvs[:, :, shard + h * HD : shard + (h + 1) * HD] = (
            dva[h, :, one(oc)].reshape(nz, rows, HD).astype(b16)
        )
    dkv_pair = links.start(dkvs, dkvr, to_core)
    rs_out.forward()
    tg[...] = matmul_tn(att[...], flat(ra[...])).astype(b16).reshape(tg.shape)
    attn_pair = links.start(tg.at[oc], tgr, to_core)
    red_down[3].third()

    def place(value):
        return jnp.concatenate([jnp.where(dp == k, value, 0.0) for k in range(n)], axis=1)

    sm[2:3] = place(jnp.concatenate([q_sum[h] for h in range(heads)], axis=1))
    v_sum = [
        jnp.sum(dva[h].reshape(2 * nz * rows, HD), axis=0, keepdims=True) for h in range(heads)
    ]
    sm[3:4] = place(jnp.concatenate(v_sum, axis=1))
    dkv_pair.wait_recv()
    for h in range(heads):
        for ref, offset in ((dka, 0), (dva, shard)):
            cols = slice(offset + h * HD, offset + (h + 1) * HD)
            mg[:, cols] = (
                ref[h, :, one(c)].reshape(nz * rows, HD) + flat(dkvr[:, :, cols]).astype(f32)
            ).astype(b16)
    mgr[...] = matmul_tn(flat(fa[...]), mg[...]).astype(b16).reshape(mgr.shape)
    mix_grad_pair = links.start(mgr.at[:, oc], mgx, to_core)
    red_up[1].second()
    red_up[0].third()
    for first, count in GROUPS:
        part = matmul_nt(mg[first * rows : (first + count) * rows], flat(mixc[...]))
        p4[first : first + count] = part.astype(b16).reshape(count, n, quarter, width)
    mix_grad_pair.wait_recv()
    ms[...] = (mgr[:, one(c)].reshape(ms.shape).astype(f32) + mgx[...].astype(f32)).astype(b16)
    hop_md = [links.start(ms.at[dps[k]], md.at[dp], to_dp[k]) for k in (1, 2, 3)]
    rs_first = [Scatter(p4, r4, t4, first, count) for first, count in GROUPS]
    md[one(dp)] = ms[one(dp)]
    red_mix[0].first()
    attn_pair.wait_recv()
    tz[...] = (tg[one(c)].reshape(tz.shape).astype(f32) + tgr[...].astype(f32)).astype(b16)
    red_attn.first()
    red_up[2].second()
    red_up[1].third()
    out_delta = aft[...] + rs_out.result() + vec(down_bias)
    od[...] = out_delta.astype(b16).reshape(od.shape)
    oh1[one(z)] = od[one(z)]
    for copy, item in zip(hop_md[:2], red_mix[1:3]):
        copy.wait_recv()
        item.first()
    red_up[3].second()
    red_up[2].third()
    red_mix[0].second()
    rs_first[0].forward()
    hop_md[2].wait_recv()
    red_mix[3].first()
    rs_first[1].forward()
    hop_o = scatter_z(od, oh1)
    red_attn.second()
    red_up[3].third()
    red_mix[1].second()
    red_mix[0].third()

    gain_sum, shift_sum = 0.0, 0.0
    for (first, count), item in zip(GROUPS, rs_first):
        at = slice(first * quarter, (first + count) * quarter)
        first_grad = item.result()
        hat = hat1[at]
        back = res[at] + norm_back(first_grad, hat, rstd1[at], vec(gain1))
        idl[first : first + count] = back.astype(b16).reshape(count, quarter, width)
        gain_sum += jnp.sum(first_grad * hat, axis=0, keepdims=True)
        shift_sum += jnp.sum(first_grad, axis=0, keepdims=True)
    hop_i = scatter_z(idl, ih1)
    ih1[one(z)] = idl[one(z)]
    sm[0:1] = gain_sum
    sm[1:2] = shift_sum
    sm1[one(dp)] = sm[...].reshape(1, *sm.shape)
    small_dp = [links.start(sm, sm1.at[dp], to_dp[k]) for k in peers]

    run(red_down, "fourth")
    red_mix[2].second()
    red_attn.third()
    red_mix[1].third()
    run(red_up, "fourth")
    arrived(small_dp)
    sm2[one(z)] = jnp.sum(sm1[...], axis=0, keepdims=True)
    small_z = [links.start(sm2.at[z], sm2.at[z], to_z[k]) for k in peers]
    red_mix[3].second()
    red_mix[2].third()
    arrived(hop_o)
    hop_o = scatter_dp(oh1, out_o)
    out_o[one(dp)] = oh1[one(dp)]
    red_mix[0].fourth()
    red_mix[3].third()
    red_attn.fourth()
    red_mix[1].fourth()
    arrived(small_z)
    sm3[one(c)] = jnp.sum(sm2[...], axis=0, keepdims=True)
    small_core = links.start(sm3.at[c], sm3.at[c], to_core)
    arrived(hop_i)
    hop_i = scatter_dp(ih1, in_o)
    in_o[one(dp)] = ih1[one(dp)]
    red_mix[2].fourth()
    red_mix[3].fourth()
    small_core.wait_recv()
    small_o[...] = sm3[0] + sm3[1]
    run(red_down + red_up + [red_attn] + red_mix, "done")
    arrived(hop_o)
    arrived(hop_i)
    links.finish()


def finish_kernel(
    out_ref, in_ref, mix_ref, attn_ref, up_ref, down_ref, small_ref, x_ref, cot_ref,
    *refs,
):
    f32 = jnp.float32
    outs, mats, sems, xv, cv = refs[:15], refs[15:21], *refs[21:]
    get_x = pltpu.make_async_copy(x_ref, xv, sems.at[6])
    get_x.start()
    get_cot = pltpu.make_async_copy(cot_ref, cv, sems.at[7])
    get_cot.start()
    shard, width = mats[3].shape
    n = mix_ref.shape[0]
    copies = []

    def store(number, target):
        copy = pltpu.make_async_copy(mats[number], target, sems.at[number])
        copy.start()
        copies.append(copy)

    mats[5][...] = flat(down_ref[...]).astype(f32)
    store(5, outs[13])
    mats[4][...] = flat(up_ref[...]).astype(f32)
    store(4, outs[11])
    for d in range(n):
        value = mix_ref[d].reshape(shard, 3 * shard).astype(f32)
        for part, place_at in ((0, 1), (1, 2), (2, 0)):
            start = place_at * width + d * shard
            mats[2][:, start : start + shard] = value[:, part * shard : (part + 1) * shard]
    store(2, outs[4])
    mats[3][...] = flat(attn_ref[...]).astype(f32)
    store(3, outs[7])
    get_x.wait()
    mats[0][...] = xv[...] + flat(out_ref[...]).astype(f32)
    store(0, outs[0])
    get_cot.wait()
    mats[1][...] = cv[...] + flat(in_ref[...]).astype(f32)
    store(1, outs[1])
    for number, row in ((2, 0), (3, 1), (5, 2), (6, 3), (8, 4), (9, 5), (10, 6), (14, 7)):
        outs[number][...] = small_ref[row : row + 1].reshape(width)
    for k in range(n):
        outs[12][k * width : (k + 1) * width] = small_ref[8 + k : 9 + k].reshape(width)
    for copy in copies:
        copy.wait()


def plane_body(
    block_input,
    out_cotangent,
    first_gain,
    first_shift,
    mix_weight,
    query_bias,
    value_bias,
    attn_weight,
    attn_bias,
    second_gain,
    second_shift,
    up_weight,
    up_bias,
    down_weight,
    down_bias,
):
    b16, f32 = jnp.bfloat16, jnp.float32
    n, nz = lax.axis_size("dp"), lax.axis_size("ctx") // 2
    rows, width = block_input.shape[1:]
    quarter = rows // n
    shard = width // n
    half = shard // 2
    hidden = up_weight.shape[1] // n
    heads = H // n
    tokens = nz * rows
    keys = 2 * tokens
    x_rows = block_input.reshape(rows, width)
    cot = out_cotangent.reshape(rows, width)
    vm = pltpu.VMEM
    stack = vm((n, quarter, width), b16)
    part = vm((nz, n, quarter, width), b16)
    part_recv = vm((n - 1, nz, quarter, width), b16)
    own = vm((nz * quarter, width), f32)
    scratch = [
        pltpu.SemaphoreType.DMA((SEMS,)),
        pltpu.SemaphoreType.DMA((SEMS,)),
        pltpu.SemaphoreType.DMA((16,)),
    ] + [vm((width,), f32)] * 7 + [
        vm((n * hidden,), f32), vm((width,), f32),
        vm((rows, width), f32), vm((rows, width), f32),
        vm((half, 3 * width), b16), vm((shard, width), b16), vm((hidden, width), b16),
        stack, stack, stack, stack, stack, stack,
        vm((n, half, 3 * shard), b16), vm((n, 2, half, 3 * shard), b16),
        vm((n, nz, shard // nz, hidden), b16), part, part, part, part,
        vm((tokens, shard), b16), vm((nz, 2, rows, 2 * shard), b16),
        vm((heads, keys, HD), b16), vm((heads, keys, HD), b16),
        vm((tokens, shard), b16), vm((heads, tokens, 1), f32), vm((tokens, shard), b16),
        own, own, own, own,
        part, part, part, part, part_recv, part_recv, part_recv, part_recv,
        stack, stack, stack, stack,
        vm((tokens, hidden), f32), vm((tokens, hidden), b16), vm((tokens, hidden), b16),
        vm((2, hidden // 2, width), b16),
    ] + [vm((hidden // 2, width), b16)] * 4 + [
        vm((n, 2, half, hidden), b16), vm((n, half, hidden), b16), vm((n, half, hidden), b16),
    ] + [vm((half, n * hidden), b16)] * 3 + [
        vm((2, half, width), b16),
    ] + [vm((half, width), b16)] * 4 + [
        vm((heads, nz, 2, rows, HD), f32), vm((heads, nz, 2, rows, HD), f32),
        vm((nz, rows, 2 * shard), b16), vm((nz, rows, 2 * shard), b16),
        vm((tokens, 3 * shard), b16),
        vm((n, 2, half, 3 * shard), b16),
    ] + [vm((n, half, 3 * shard), b16)] * 5 + [
        stack, stack, stack, stack,
        vm((16, width), f32), vm((n, 16, width), f32), vm((nz, 16, width), f32),
        vm((2, 16, width), f32),
    ]
    hbm = pl.BlockSpec(memory_space=pl.ANY)
    near = pl.BlockSpec(memory_space=pltpu.VMEM)
    far = pl.BlockSpec(memory_space=pltpu.HBM)
    shapes = [
        ((n, quarter, width), b16),
        ((n, quarter, width), b16),
        ((n, 2, half, 3 * shard), b16),
        ((2, half, width), b16),
        ((2, half, n * hidden), b16),
        ((2, hidden // 2, width), b16),
        ((16, width), f32),
    ]
    pieces = pl.pallas_call(
        plane_kernel,
        out_shape=[jax.ShapeDtypeStruct(shape, dtype) for shape, dtype in shapes],
        in_specs=[far] * 15,
        out_specs=[near] * len(shapes),
        scratch_shapes=scratch,
        compiler_params=pltpu.CompilerParams(
            collective_id=0, has_side_effects=True, vmem_limit_bytes=60 * 1024 * 1024
        ),
        name="plane",
    )(
        x_rows, cot, first_gain, first_shift, mix_weight, query_bias, value_bias, attn_weight,
        attn_bias, second_gain, second_shift, up_weight, up_bias, down_weight, down_bias,
    )
    final = [
        (rows, width), (rows, width), (width,), (width,), (shard, 3 * width), (width,), (width,),
        (shard, width), (width,), (width,), (width,), (shard, n * hidden), (n * hidden,),
        (hidden, width), (width,),
    ]
    large = (0, 1, 4, 7, 11, 13)
    outs = pl.pallas_call(
        finish_kernel,
        out_shape=[jax.ShapeDtypeStruct(shape, f32) for shape in final],
        in_specs=[near] * 7 + [far] * 2,
        out_specs=[hbm if k in large else near for k in range(len(final))],
        scratch_shapes=[vm(final[k], f32) for k in large] + [
            pltpu.SemaphoreType.DMA((8,)), vm((rows, width), f32), vm((rows, width), f32)
        ],
        compiler_params=pltpu.CompilerParams(vmem_limit_bytes=60 * 1024 * 1024),
        name="finish",
    )(*pieces, x_rows, cot)
    return (
        outs[0].reshape(1, rows, width),
        outs[1].reshape(1, rows, width),
        *outs[2:],
    )


def fits(mesh):
    n, ctx = mesh.shape["dp"], mesh.shape["ctx"]
    return n == 4 and ctx == 8 and H % n == 0


def solution(mesh):
    placed = (
        P("dp", "ctx", None),
        P("dp", "ctx", None),
        P(),
        P(),
        P("dp", None),
        P(),
        P(),
        P("dp", None),
        P(),
        P(),
        P(),
        P("dp", None),
        P(),
        P("dp", None),
        P(),
    )
    return jax.shard_map(
        plane_body if fits(mesh) else body,
        mesh=mesh,
        in_specs=placed,
        out_specs=(
            P("dp", "ctx", None),
            P("dp", "ctx", None),
            P(),
            P(),
            P("dp", None),
            P(),
            P(),
            P("dp", None),
            P(),
            P(),
            P(),
            P("dp", None),
            P(),
            P("dp", None),
            P(),
        ),
        check_vma=False,
    )
```

```python
import functools
import math

import jax
import jax.numpy as jnp
from jax import lax
from jax.experimental import pallas as pl
from jax.experimental.pallas import tpu as pltpu
from jax.sharding import PartitionSpec as P

H = 12
HD = 64


EPS = 1e-05
GELU_C = math.sqrt(2.0 / math.pi)


def from_behind(value, axis, steps):
    count = lax.axis_size(axis)
    pairs = [(source, (source + steps) % count) for source in range(count)]
    return lax.ppermute(value, axis, pairs)


def layer_norm(x, gain, shift):
    centered = x - jnp.mean(x, axis=-1, keepdims=True)
    rstd = lax.rsqrt(jnp.mean(centered * centered, axis=-1, keepdims=True) + EPS)
    x_hat = centered * rstd
    return (x_hat, rstd, x_hat * gain + shift)


def norm_back(grad, x_hat, rstd, gain):
    g = grad * gain
    return rstd * (
        g
        - jnp.mean(g, axis=-1, keepdims=True)
        - x_hat * jnp.mean(g * x_hat, axis=-1, keepdims=True)
    )


def gelu_pair(u):
    inner = GELU_C * (u + 0.044715 * u * u * u)
    t = jnp.tanh(inner)
    value = 0.5 * u * (1.0 + t)
    slope = 0.5 * (1.0 + t) + 0.5 * u * (1.0 - t * t) * GELU_C * (1.0 + 3.0 * 0.044715 * u * u)
    return (value, slope)


def matmul(a, b):
    return jnp.dot(a, b, preferred_element_type=jnp.float32)


def matmul_tn(a, b):
    return lax.dot_general(a, b, (((0,), (0,)), ((), ())), preferred_element_type=jnp.float32)


def matmul_nt(a, b):
    return lax.dot_general(a, b, (((1,), (1,)), ((), ())), preferred_element_type=jnp.float32)


def body(
    block_input,
    out_cotangent,
    first_gain,
    first_shift,
    mix_weight,
    query_bias,
    value_bias,
    attn_weight,
    attn_bias,
    second_gain,
    second_shift,
    up_weight,
    up_bias,
    down_weight,
    down_bias,
):
    rows = block_input.shape[1]
    width = block_input.shape[2]
    scale = HD ** (-0.5)
    x_rows = block_input.reshape(rows, width)
    cot = out_cotangent.reshape(rows, width)
    mix_full, attn_full, up_full, down_full = (
        lax.all_gather(mix_weight, "dp", axis=0, tiled=True),
        lax.all_gather(attn_weight, "dp", axis=0, tiled=True),
        lax.all_gather(up_weight, "dp", axis=0, tiled=True),
        lax.all_gather(down_weight, "dp", axis=0, tiled=True),
    )
    first_hat, first_rstd, first_out = layer_norm(x_rows, first_gain, first_shift)
    first_in = first_out.astype(jnp.bfloat16)
    mixed = matmul(first_in, mix_full)
    queries = (mixed[:, :width] + query_bias).astype(jnp.bfloat16)
    keys = mixed[:, width : 2 * width].astype(jnp.bfloat16)
    values = (mixed[:, 2 * width :] + value_bias).astype(jnp.bfloat16)
    q3 = queries.reshape(rows, H, HD)
    me = lax.axis_index("ctx")
    cycle_size = lax.axis_size("ctx")
    q_pos = me * rows + jnp.arange(rows)
    q_last = me * rows + rows - 1
    start_state = (
        jnp.full((H, rows), -1e30, jnp.float32),
        jnp.zeros((H, rows), jnp.float32),
        jnp.zeros((H, rows, HD), jnp.float32),
    )
    carry = start_state
    key_piece = lax.all_gather(keys, "ctx", axis=0, tiled=True)
    value_piece = lax.all_gather(values, "ctx", axis=0, tiled=True)
    count = key_piece.shape[0]
    kblock = math.gcd(count, 512)
    nblocks = count // kblock
    key_blocks = key_piece.reshape(nblocks, kblock, H, HD)
    value_blocks = value_piece.reshape(nblocks, kblock, H, HD)
    offsets = jnp.arange(nblocks) * kblock

    def one_block(state, item):
        key_blk, value_blk, offset = item

        def compute(state_in):
            run_max, run_total, run_acc = state_in
            key_pos = offset + jnp.arange(kblock)
            allowed = (key_pos[None, :] <= q_pos[:, None])[None]
            scores = (
                jnp.einsum("qhd,khd->hqk", q3, key_blk, preferred_element_type=jnp.float32) * scale
            )
            scores = jnp.where(allowed, scores, -1e30)
            new_max = jnp.maximum(run_max, jnp.max(scores, axis=-1))
            expo = jnp.where(allowed, jnp.exp(scores - new_max[..., None]), 0.0)
            factor = jnp.exp(run_max - new_max)
            new_total = run_total * factor + jnp.sum(expo, axis=-1)
            new_acc = run_acc * factor[..., None] + jnp.einsum(
                "hqk,khd->hqd", expo, value_blk.astype(jnp.float32), precision=lax.Precision.HIGHEST
            )
            return (new_max, new_total, new_acc)

        def keep_state(state_in):
            return state_in

        return (lax.cond(offset <= q_last, compute, keep_state, state), None)

    carry, unused = lax.scan(one_block, carry, (key_blocks, value_blocks, offsets))
    run_max, run_total, run_acc = carry
    attended = (
        (run_acc / run_total[..., None])
        .transpose(1, 0, 2)
        .reshape(rows, width)
        .astype(jnp.bfloat16)
    )
    lse = run_max + jnp.log(run_total)
    after_attn = x_rows + matmul(attended, attn_full) + attn_bias
    second_hat, second_rstd, second_out = layer_norm(after_attn, second_gain, second_shift)
    second_in = second_out.astype(jnp.bfloat16)
    pre_act = matmul(second_in, up_full) + up_bias
    act_value, act_slope = gelu_pair(pre_act)
    activ = act_value.astype(jnp.bfloat16)
    block_output = after_attn + matmul(activ, down_full) + down_bias
    mix_back, attn_back, up_back, down_back = (
        lax.all_gather(mix_weight, "dp", axis=0, tiled=True),
        lax.all_gather(attn_weight, "dp", axis=0, tiled=True),
        lax.all_gather(up_weight, "dp", axis=0, tiled=True),
        lax.all_gather(down_weight, "dp", axis=0, tiled=True),
    )
    cot_b = cot.astype(jnp.bfloat16)
    down_weight_grad = matmul_tn(activ, cot_b)
    down_bias_grad = jnp.sum(cot, axis=0)
    pre_grad = matmul_nt(cot_b, down_back) * act_slope
    pre_grad_b = pre_grad.astype(jnp.bfloat16)
    up_weight_grad = matmul_tn(second_in, pre_grad_b)
    up_bias_grad = jnp.sum(pre_grad, axis=0)
    second_grad = matmul_nt(pre_grad_b, up_back)
    second_gain_grad = jnp.sum(second_grad * second_hat, axis=0)
    second_shift_grad = jnp.sum(second_grad, axis=0)
    resid_grad = cot + norm_back(second_grad, second_hat, second_rstd, second_gain)
    resid_b = resid_grad.astype(jnp.bfloat16)
    attn_weight_grad = matmul_tn(attended, resid_b)
    attn_bias_grad = jnp.sum(resid_grad, axis=0)
    attended_grad = matmul_nt(resid_b, attn_back).astype(jnp.bfloat16)
    grad3 = attended_grad.reshape(rows, H, HD)
    delta = jnp.sum(
        grad3.astype(jnp.float32) * attended.astype(jnp.float32).reshape(rows, H, HD), axis=-1
    ).T

    def block_grads(key_blk, value_blk, key_start):
        count = key_blk.shape[0]
        key3 = key_blk.reshape(count, H, HD)
        value3 = value_blk.reshape(count, H, HD)
        key_pos = key_start + jnp.arange(count)
        allowed = (key_pos[None, :] <= q_pos[:, None])[None]
        scores = jnp.einsum("qhd,khd->hqk", q3, key3, preferred_element_type=jnp.float32) * scale
        probs = jnp.where(allowed, jnp.exp(scores - lse[..., None]), 0.0)
        dprob = jnp.einsum("qhd,khd->hqk", grad3, value3, preferred_element_type=jnp.float32)
        dscore = probs * (dprob - delta[..., None])
        probs_b = probs.astype(jnp.bfloat16)
        dscore_b = dscore.astype(jnp.bfloat16)
        value_add = jnp.einsum("hqk,qhd->khd", probs_b, grad3, preferred_element_type=jnp.float32)
        key_add = (
            jnp.einsum("hqk,qhd->khd", dscore_b, q3, preferred_element_type=jnp.float32) * scale
        )
        query_add = (
            jnp.einsum("hqk,khd->qhd", dscore_b, key3, preferred_element_type=jnp.float32) * scale
        )
        return (
            query_add.reshape(rows, width),
            key_add.reshape(count, width),
            value_add.reshape(count, width),
        )

    def skip_grads(key_blk, value_blk, key_start):
        count = key_blk.shape[0]
        empty = jnp.zeros((count, width), jnp.float32)
        return (jnp.zeros((rows, width), jnp.float32), empty, empty)

    zeros = jnp.zeros((rows, width), jnp.float32)

    def pass_grads(key_acc, value_acc):
        return (
            from_behind(key_acc.astype(jnp.bfloat16), "ctx", -1).astype(key_acc.dtype),
            from_behind(value_acc.astype(jnp.bfloat16), "ctx", -1).astype(value_acc.dtype),
        )

    def cycle_turn(step, state):
        key_blk, value_blk, key_acc, value_acc, query_acc = state
        owner = (me + step) % cycle_size
        query_add, key_add, value_add = lax.cond(
            owner <= me, block_grads, skip_grads, key_blk, value_blk, owner * rows
        )
        key_blk, value_blk = from_behind((key_blk, value_blk), "ctx", -1)
        key_acc, value_acc = pass_grads(key_acc + key_add, value_acc + value_add)
        return (key_blk, value_blk, key_acc, value_acc, query_acc + query_add)

    key_blk, value_blk, key_acc, value_acc, query_acc = lax.fori_loop(
        0, cycle_size - 1, cycle_turn, (keys, values, zeros, zeros, zeros)
    )
    last_owner = (me + cycle_size - 1) % cycle_size
    query_add, key_add, value_add = lax.cond(
        last_owner <= me, block_grads, skip_grads, key_blk, value_blk, last_owner * rows
    )
    key_grad, value_grad = pass_grads(key_acc + key_add, value_acc + value_add)
    query_grad = query_acc + query_add
    query_bias_grad = jnp.sum(query_grad, axis=0)
    value_bias_grad = jnp.sum(value_grad, axis=0)
    mixed_grad = jnp.concatenate([query_grad, key_grad, value_grad], axis=1).astype(jnp.bfloat16)
    mix_weight_grad = matmul_tn(first_in, mixed_grad)
    first_grad = matmul_nt(mixed_grad, mix_back)
    first_gain_grad = jnp.sum(first_grad * first_hat, axis=0)
    first_shift_grad = jnp.sum(first_grad, axis=0)
    input_grad = resid_grad + norm_back(first_grad, first_hat, first_rstd, first_gain)
    local_mats = (mix_weight_grad, attn_weight_grad, up_weight_grad, down_weight_grad)
    shard_sums = (
        lax.psum_scatter(
            local_mats[0].astype(jnp.bfloat16), "dp", scatter_dimension=0, tiled=True
        ).astype(jnp.float32),
        lax.psum_scatter(
            local_mats[1].astype(jnp.bfloat16), "dp", scatter_dimension=0, tiled=True
        ).astype(jnp.float32),
        lax.psum_scatter(
            local_mats[2].astype(jnp.bfloat16), "dp", scatter_dimension=0, tiled=True
        ).astype(jnp.float32),
        lax.psum_scatter(
            local_mats[3].astype(jnp.bfloat16), "dp", scatter_dimension=0, tiled=True
        ).astype(jnp.float32),
    )
    mats = (
        lax.psum(shard_sums[0].astype(jnp.bfloat16), "ctx").astype(jnp.float32),
        lax.psum(shard_sums[1].astype(jnp.bfloat16), "ctx").astype(jnp.float32),
        lax.psum(shard_sums[2].astype(jnp.bfloat16), "ctx").astype(jnp.float32),
        lax.psum(shard_sums[3].astype(jnp.bfloat16), "ctx").astype(jnp.float32),
    )
    smalls = lax.psum(
        (
            first_gain_grad,
            first_shift_grad,
            query_bias_grad,
            value_bias_grad,
            attn_bias_grad,
            second_gain_grad,
            second_shift_grad,
            up_bias_grad,
            down_bias_grad,
        ),
        ("dp", "ctx"),
    )
    return (
        block_output.reshape(1, rows, width),
        input_grad.reshape(1, rows, width),
        smalls[0],
        smalls[1],
        mats[0],
        smalls[2],
        smalls[3],
        mats[1],
        smalls[4],
        smalls[5],
        smalls[6],
        mats[2],
        smalls[7],
        mats[3],
        smalls[8],
    )


def flip(index, mask):
    bit = 1
    while bit <= mask:
        if mask & bit:
            index = index + bit - 2 * bit * ((index // bit) % 2)
        bit *= 2
    return index


MESH = pl.DeviceIdType.MESH
GROUPS = ((2, 2), (0, 2))
SEMS = 224


class Links:
    def __init__(self, send, recv):
        self.send, self.recv, self.count, self.open = send, recv, 0, []

    def make(self, source, target, device):
        number = self.count
        self.count += 1
        return pltpu.make_async_remote_copy(
            src_ref=source,
            dst_ref=target,
            send_sem=self.send.at[number],
            recv_sem=self.recv.at[number],
            device_id=device,
            device_id_type=MESH,
        )

    def start(self, source, target, device):
        copy = self.make(source, target, device)
        copy.start()
        self.open.append(copy)
        return copy

    def finish(self):
        for copy in self.open:
            copy.wait_send()


def arrived(copies):
    for copy in copies:
        copy.wait_recv()


def flat(value):
    return value.reshape(-1, value.shape[-1])


def plane_kernel(
    x_in, cot_in, gain1_in, shift1_in, mix_w, q_bias_in, v_bias_in, attn_w, attn_bias_in, gain2_in,
    shift2_in, up_w, up_bias_in, down_w, down_bias_in,
    out_hbm, in_hbm, mix_hbm, attn_hbm, up_hbm, down_hbm, small_o,
    send_sem, recv_sem, local_sem,
    out_o, in_o, mix_o, attn_o, up_o, down_o,
    gain1, shift1, q_bias, v_bias, attn_bias, gain2, shift2, up_bias, down_bias,
    xv, cv, mw, aw, dw,
    xs, xh1, xh2, cs, ch1, ch2,
    mst, mixc, upc, fa, ca, sa, ra,
    qs, kv, kh, vh, att, lse, agr,
    hat1, aft, hat2, res,
    p1, p2, p3, p4, r1, r2, r3, r4, t1, t2, t3, t4,
    dact, act, pg,
    dg, dgr, dz, dz1, dz2,
    ug, ugr, us, ud, uz1, uz2,
    tg, tgr, tz, tz1, tz2,
    dka, dva, dkvs, dkvr, mg,
    mgr, mgx, ms, md, mz1, mz2,
    od, oh1, idl, ih1,
    sm, sm1, sm2, sm3,
):
    b16, f32 = jnp.bfloat16, jnp.float32
    n, quarter, width = xs.shape
    nz = xh2.shape[0]
    rows = n * quarter
    half, hidden = mixc.shape[2], upc.shape[3]
    shard = 2 * half
    heads = kh.shape[0]
    dp, ctx = lax.axis_index("dp"), lax.axis_index("ctx")
    z, c = ctx // 2, ctx % 2
    oc = 1 - c
    dps = [flip(dp, k) for k in range(n)]
    zs = [flip(z, k) for k in range(nz)]
    to_dp = [(dps[k], ctx) for k in range(n)]
    to_z = [(dp, 2 * zs[k] + c) for k in range(nz)]
    to_core = (dp, 2 * z + oc)
    inner = (z + 1) // 2 % 2 == 1
    outer = (z + 1) // 2 % 2 == 0
    peers = (3, 1, 2)
    links = Links(send_sem, recv_sem)
    one = lambda index: pl.ds(index, 1)

    locals_ = []

    def fetch(source, target):
        copy = pltpu.make_async_copy(source, target, local_sem.at[len(locals_)])
        copy.start()
        locals_.append(copy)
        return copy

    my_half = pl.ds(pl.multiple_of(c * half, 16), half)
    get_x = fetch(x_in, xv)
    get_mix = fetch(mix_w.at[my_half], mw)
    get_cot = fetch(cot_in, cv)
    get_vectors = [
        fetch(source, target)
        for source, target in (
            (gain1_in, gain1), (shift1_in, shift1), (q_bias_in, q_bias), (v_bias_in, v_bias),
            (attn_bias_in, attn_bias), (gain2_in, gain2), (shift2_in, shift2),
            (up_bias_in, up_bias), (down_bias_in, down_bias),
        )
    ]
    get_attn = fetch(attn_w, aw)
    get_down = fetch(down_w, dw)
    columns = lambda index: pl.ds(pl.multiple_of(index * hidden, 128), hidden)
    strip = shard // nz
    up_rows = pl.ds(pl.multiple_of(z * strip, 16), strip)
    up_half = lambda index: pl.ds(pl.multiple_of(index * (hidden // 2), 128), hidden // 2)
    up_piece = lambda index: up_w.at[
        up_rows, pl.ds(pl.multiple_of(index * hidden + c * (hidden // 2), 128), hidden // 2)
    ]
    get_up = fetch(up_piece(dp), upc.at[dp, z, :, up_half(c)])

    barrier = pltpu.get_barrier_semaphore()
    everyone = to_dp[1:] + to_z[1:] + [to_core]
    for device in everyone:
        pl.semaphore_signal(barrier, inc=1, device_id=device, device_id_type=MESH)

    get_x.wait()
    xs[...] = xv[...].astype(b16).reshape(n, quarter, width)
    pl.semaphore_wait(barrier, len(everyone))

    def scatter_dp(source, target):
        return [links.start(source.at[dps[k]], target.at[dp], to_dp[k]) for k in peers]

    def scatter_z(source, target):
        return [links.start(source.at[zs[k]], target.at[z], to_z[k]) for k in peers]

    class Gather:
        def __init__(self, ref, first, count):
            self.ref, self.first, self.mid = ref, first, first + count // 2
            part = ref.at[pl.ds(first, count), dp]
            self.near = [links.start(part, part, to_dp[k]) for k in (1, 2)]

        def forward(self):
            arrived(self.near)
            self.far = []
            for begin, origin, target in ((self.first, 1, 2), (self.mid, 2, 1)):
                part = self.ref.at[pl.ds(begin, self.mid - self.first), dps[origin]]
                self.far.append(links.start(part, part, to_dp[target]))

        def wait(self):
            arrived(self.far)

    class Scatter:
        def __init__(self, ref, recv, stage, first, count):
            self.ref, self.recv, self.stage = ref, recv, stage
            self.first, self.count, step = first, count, count // 2
            self.ways = ((first, step, 1, 2), (first + step, step, 2, 1))
            self.pass_on, self.mine = [], []
            for begin, size, near, _ in self.ways:
                for role, slot, copies in ((1, 3, self.pass_on), (0, near, self.mine)):
                    source = ref.at[pl.ds(begin, size), dps[slot]]
                    target = recv.at[role, pl.ds(begin, size)]
                    copies.append(links.start(source, target, to_dp[near]))

        def forward(self):
            self.last = []
            for (begin, size, _, beyond), copy in zip(self.ways, self.pass_on):
                copy.wait_recv()
                at = pl.ds(begin, size)
                value = self.ref[at, one(dps[beyond])].astype(f32).reshape(size, quarter, width)
                value = value + self.recv[1, at].astype(f32)
                self.stage[at] = value.astype(b16)
                self.last.append(
                    links.start(self.stage.at[at], self.recv.at[2, at], to_dp[beyond])
                )

        def result(self):
            arrived(self.mine)
            arrived(self.last)
            at = slice(self.first, self.first + self.count)
            total = self.ref[at, one(dp)].astype(f32).reshape(self.count * quarter, width)
            return total + flat(self.recv[0, at].astype(f32)) + flat(self.recv[2, at].astype(f32))

    def run(items, step):
        for item in items:
            getattr(item, step)()

    hop_x = scatter_dp(xs, xh1)
    xh1[one(dp)] = xs[one(dp)]
    get_mix.wait()
    mv = mw[...]
    for d in range(n):
        mst[d] = jnp.concatenate(
            [mv[:, part * width + d * shard : part * width + (d + 1) * shard] for part in (1, 2, 0)],
            axis=1,
        )
    mixc[one(dp), one(c)] = mst[one(dp)].reshape(1, 1, half, 3 * shard)
    for copy in [get_cot] + get_vectors:
        copy.wait()
    cot = cv[...]
    cs[...] = cot.astype(b16).reshape(n, quarter, width)
    ch1[one(dp)] = cs[one(dp)]
    arrived(hop_x)
    hop_x = scatter_z(xh1, xh2)
    hop_mix = [links.start(mst.at[dps[k]], mixc.at[dp, c], to_dp[k]) for k in peers]
    hop_c = scatter_dp(cs, ch1)
    xh2[one(z)] = xh1[one(z)]
    sm[...] = jnp.zeros(sm.shape, f32)
    sm[7:8] = jnp.sum(cot, axis=0, keepdims=True)

    vec = lambda ref: ref[...].reshape(1, -1)

    def pick(ref, size):
        value = vec(ref)
        total = jnp.zeros((1, size), f32)
        for k in range(n):
            total = jnp.where(dp == k, value[:, k * size : (k + 1) * size], total)
        return total

    arrived(hop_x)
    x_hat, rstd1, first = layer_norm(flat(xh2[...]).astype(f32), vec(gain1), vec(shift1))
    hat1[...] = x_hat
    fa[:, one(dp)] = first.astype(b16).reshape(nz, 1, quarter, width)
    ag_first = [Gather(fa, first, count) for first, count in GROUPS]
    kv_bias = jnp.concatenate([jnp.zeros((1, shard), f32), pick(v_bias, shard)], axis=1)
    own_q_bias = pick(q_bias, shard)
    arrived(hop_mix)
    mix_pair = links.start(mixc.at[:, c], mixc.at[:, c], to_core)
    arrived(hop_c)
    hop_c = scatter_z(ch1, ch2)
    ch2[one(z)] = ch1[one(z)]

    run(ag_first, "forward")
    run(ag_first, "wait")
    hop_up = [
        links.start(up_piece(dps[k]), upc.at[dp, z, :, up_half(c)], to_dp[k]) for k in peers
    ]
    arrived(hop_c)
    ca[:, one(dp)] = ch2[...].reshape(nz, 1, quarter, width)
    ag_cot = Gather(ca, 0, nz)
    mix_pair.wait_recv()
    first_all = flat(fa[...])
    mixed = matmul(first_all, flat(mixc[:, :, :, : 2 * shard])) + kv_bias
    kv[:, one(c)] = mixed.astype(b16).reshape(nz, 1, rows, 2 * shard)
    kv_pair = links.start(kv.at[:, c], kv.at[:, c], to_core)
    scale = HD ** (-0.5)
    queries = matmul(first_all, flat(mixc[:, :, :, 2 * shard :])) + own_q_bias
    qs[...] = (queries * scale).astype(b16)
    arrived(hop_up)
    get_up.wait()
    up_strip = upc.at[:, z, :, up_half(c)]
    hop_up = [links.start(up_strip, up_strip, to_z[k]) for k in peers]
    kv_pair.wait_recv()
    for h in range(heads):
        kh[h] = flat(kv[:, :, :, h * HD : (h + 1) * HD])
        vh[h] = flat(kv[:, :, :, shard + h * HD : shard + (h + 1) * HD])

    last = 2 * rows
    allowed = (
        lax.broadcasted_iota(jnp.int32, (rows, last), 1)
        <= lax.broadcasted_iota(jnp.int32, (rows, last), 0) + c * rows
    )

    def spans(j):
        return ([(0, j * last)] if j else []) + [(j * last, (j + 1) * last)]

    def attend(j):
        at = slice(j * rows, (j + 1) * rows)
        for h in range(heads):
            q = qs[at, h * HD : (h + 1) * HD]
            scores = []
            for a, b in spans(j):
                s = matmul_nt(q, kh[h, a:b])
                scores.append(jnp.where(allowed, s, -1e30) if b == (j + 1) * last else s)
            top = functools.reduce(
                jnp.maximum, [jnp.max(s, axis=-1, keepdims=True) for s in scores]
            )
            total, result = 0.0, 0.0
            for s, (a, b) in zip(scores, spans(j)):
                w = jnp.exp(s - top)
                total = total + jnp.sum(w, axis=-1, keepdims=True)
                result = result + matmul(w.astype(b16), vh[h, a:b])
            att[at, h * HD : (h + 1) * HD] = (result / total).astype(b16)
            lse[h, at] = top + jnp.log(total)

    get_attn.wait()
    ag_cot.forward()
    rs_attn = []
    for first, count in GROUPS:
        for j in range(first + count - 1, first - 1, -1):
            attend(j)
            if rs_attn and j == 1:
                rs_attn[0].forward()
        part = matmul(att[first * rows : (first + count) * rows], aw[...])
        p1[first : first + count] = part.astype(b16).reshape(count, n, quarter, width)
        rs_attn.append(Scatter(p1, r1, t1, first, count))

    arrived(hop_up)
    up_pair = links.start(upc.at[:, :, :, up_half(c)], upc.at[:, :, :, up_half(c)], to_core)
    get_down.wait()
    ag_cot.wait()
    for first, count in GROUPS:
        if first == GROUPS[1][0]:
            rs_attn[1].forward()
        dact[first * rows : (first + count) * rows] = matmul_nt(
            flat(ca[first : first + count]), dw[...]
        )

    ag_second, rstd2 = [], []
    for (first, count), item in zip(GROUPS, rs_attn):
        at = slice(first * quarter, (first + count) * quarter)
        after = item.result() + vec(attn_bias)
        aft[at] = after
        after = after + flat(xh2[first : first + count]).astype(f32)
        hat, rstd, second = layer_norm(after, vec(gain2), vec(shift2))
        hat2[at] = hat
        rstd2.append(rstd)
        sa[first : first + count, one(dp)] = second.astype(b16).reshape(count, 1, quarter, width)
        ag_second.append(Gather(sa, first, count))

    run(ag_second, "forward")
    up_pair.wait_recv()
    own_up_bias = up_bias[columns(dp)].reshape(1, hidden)
    up_sum = jnp.zeros((1, hidden), f32)
    rs_second = []
    for (first, count), item in zip(GROUPS, ag_second):
        item.wait()
        at = slice(first * rows, (first + count) * rows)
        pre_act = matmul(flat(sa[first : first + count]), flat(upc[...])) + own_up_bias
        value, slope = gelu_pair(pre_act)
        act[at] = value.astype(b16)
        if rs_second:
            rs_second[0].forward()
        pre_grad = dact[at] * slope
        up_sum += jnp.sum(pre_grad, axis=0, keepdims=True)
        pg[at] = pre_grad.astype(b16)
        part = matmul_nt(pg[at], flat(upc[...]))
        p2[first : first + count] = part.astype(b16).reshape(count, n, quarter, width)
        rs_second.append(Scatter(p2, r2, t2, first, count))
    for k in range(n):
        sm[8 + k : 9 + k] = jnp.where(dp == k, up_sum, 0.0)

    dg[...] = matmul_tn(act[...], flat(ca[...])).astype(b16).reshape(dg.shape)
    down_pair = links.start(dg.at[oc], dgr, to_core)
    rs_second[1].forward()
    ug[...] = matmul_tn(flat(sa[...]), pg[...]).astype(b16).reshape(ug.shape)
    up_grad_pair = links.start(ug.at[:, oc], ugr, to_core)

    class Reduce:
        def __init__(self, mine, sum1, sum2, total):
            self.mine, self.sum1, self.sum2, self.total = mine, sum1, sum2, total
            self.one = links.make(mine, sum1, to_z[1])
            self.two = links.make(mine, sum2, to_z[3])
            self.three = links.make(total, total, to_z[1])
            self.pair = links.make(total, total, to_core)

        def first(self):
            pl.when(outer)(lambda: self.one.start())

        def second(self):
            @pl.when(inner)
            def _():
                self.one.wait_recv()
                value = self.mine[...].astype(f32) + self.sum1[...].astype(f32)
                self.mine[...] = value.astype(b16)
                self.two.start()

        def third(self):
            @pl.when(inner)
            def _():
                self.two.wait_recv()
                value = self.mine[...].astype(f32) + self.sum2[...].astype(f32)
                self.total[...] = value.astype(b16).reshape(self.total.shape)
                self.three.start()
                self.pair.start()

        def fourth(self):
            @pl.when(outer)
            def _():
                self.three.wait_recv()
                self.pair.start()

        def done(self):
            self.pair.wait()

            @pl.when(outer)
            def _():
                self.one.wait_send()

            @pl.when(inner)
            def _():
                self.two.wait_send()
                self.three.wait_send()

    down_pair.wait_recv()
    dz[...] = (dg[one(c)].reshape(dz.shape).astype(f32) + dgr[...].astype(f32)).astype(b16)
    size = dz.shape[0] // n
    red_down = [
        Reduce(dz.at[part], dz1.at[part], dz2.at[part], down_o.at[c, part])
        for part in [pl.ds(k * size, size) for k in range(n)]
    ]
    run(red_down, "first")
    up_grad_pair.wait_recv()
    us[...] = (ug[:, one(c)].reshape(us.shape).astype(f32) + ugr[...].astype(f32)).astype(b16)
    ud[:, columns(dp)] = us[one(dp)].reshape(half, hidden)
    red_up = [
        Reduce(ud.at[:, part], uz1.at[:, part], uz2.at[:, part], up_o.at[c, :, part])
        for part in [columns(dps[k]) for k in range(n)]
    ]
    red_up[0].first()

    ag_resid = []
    gain_sum, shift_sum, bias_sum = 0.0, 0.0, 0.0
    for (first, count), item, rstd in zip(GROUPS, rs_second, rstd2):
        at = slice(first * quarter, (first + count) * quarter)
        second_grad = item.result()
        hat = hat2[at]
        back = norm_back(second_grad, hat, rstd, vec(gain2))
        res[at] = back
        resid = flat(ch2[first : first + count]).astype(f32) + back
        ra[first : first + count, one(dp)] = resid.astype(b16).reshape(count, 1, quarter, width)
        ag_resid.append(Gather(ra, first, count))
        gain_sum += jnp.sum(second_grad * hat, axis=0, keepdims=True)
        shift_sum += jnp.sum(second_grad, axis=0, keepdims=True)
        bias_sum += jnp.sum(resid, axis=0, keepdims=True)
    sm[4:5] = bias_sum
    sm[5:6] = gain_sum
    sm[6:7] = shift_sum

    red_down[0].second()
    run(ag_resid, "forward")
    hop_ud = [links.start(us.at[dps[k]], ud.at[:, columns(dp)], to_dp[k]) for k in (1, 2, 3)]
    red_down[1].second()
    part = matmul(act[...], dw[...])
    p3[...] = part.astype(b16).reshape(p3.shape)
    rs_out = Scatter(p3, r3, t3, 0, nz)
    red_down[0].third()

    def attend_back(j, fresh):
        at = slice(j * rows, (j + 1) * rows)
        for h in range(heads):
            cols = slice(h * HD, (h + 1) * HD)
            q, grad = qs[at, cols], agr[at, cols]
            delta = jnp.sum(grad.astype(f32) * att[at, cols].astype(f32), axis=-1, keepdims=True)
            base, total = lse[h, at], 0.0
            for a, b in spans(j):
                keys = kh[h, a:b]
                p = jnp.exp(matmul_nt(q, keys) - base)
                if b == (j + 1) * last:
                    p = jnp.where(allowed, p, 0.0)
                ds = (p * (matmul_nt(grad, vh[h, a:b]) - delta)).astype(b16)
                total = total + matmul(ds, keys)
                shape = ((b - a) // last, 2, rows, HD)
                dk = matmul_tn(ds, q).reshape(shape)
                dv = matmul_tn(p.astype(b16), grad).reshape(shape)
                blocks = slice(a // last, b // last)
                if fresh:
                    dka[h, blocks], dva[h, blocks] = dk, dv
                else:
                    dka[h, blocks] += dk
                    dva[h, blocks] += dv
            total = total * scale
            q_sum[h] = q_sum.get(h, 0.0) + jnp.sum(total, axis=0, keepdims=True)
            mg[at, 2 * shard + h * HD : 2 * shard + (h + 1) * HD] = total.astype(b16)

    q_sum = {}
    red_attn = Reduce(tz, tz1, tz2, attn_o.at[c])
    red_mix = [
        Reduce(md.at[dps[k]], mz1.at[k], mz2.at[k], mix_o.at[dps[k], c]) for k in range(n)
    ]

    def weights_of(first, count):
        return matmul_nt(flat(ra[first : first + count]), aw[...]).astype(b16)

    (first, count), (first2, count2) = GROUPS
    ag_resid[0].wait()
    agr[first * rows : (first + count) * rows] = weights_of(first, count)
    attend_back(3, True)
    red_down[2].second()
    red_down[1].third()
    attend_back(2, False)
    red_down[3].second()
    red_down[2].third()
    ag_resid[1].wait()
    agr[first2 * rows : (first2 + count2) * rows] = weights_of(first2, count2)
    attend_back(1, False)
    for copy, item in zip(hop_ud[:2], red_up[1:3]):
        copy.wait_recv()
        item.first()
    red_up[0].second()
    red_down[3].third()
    attend_back(0, False)
    hop_ud[2].wait_recv()
    red_up[3].first()

    for h in range(heads):
        dkvs[:, :, h * HD : (h + 1) * HD] = (
            dka[h, :, one(oc)].reshape(nz, rows, HD).astype(b16)
        )
        dkvs[:, :, shard + h * HD : shard + (h + 1) * HD] = (
            dva[h, :, one(oc)].reshape(nz, rows, HD).astype(b16)
        )
    dkv_pair = links.start(dkvs, dkvr, to_core)
    rs_out.forward()
    tg[...] = matmul_tn(att[...], flat(ra[...])).astype(b16).reshape(tg.shape)
    attn_pair = links.start(tg.at[oc], tgr, to_core)
    red_up[1].second()
    red_up[0].third()

    def place(value):
        return jnp.concatenate([jnp.where(dp == k, value, 0.0) for k in range(n)], axis=1)

    sm[2:3] = place(jnp.concatenate([q_sum[h] for h in range(heads)], axis=1))
    v_sum = [
        jnp.sum(dva[h].reshape(2 * nz * rows, HD), axis=0, keepdims=True) for h in range(heads)
    ]
    sm[3:4] = place(jnp.concatenate(v_sum, axis=1))
    dkv_pair.wait_recv()
    for h in range(heads):
        for ref, offset in ((dka, 0), (dva, shard)):
            cols = slice(offset + h * HD, offset + (h + 1) * HD)
            mg[:, cols] = (
                ref[h, :, one(c)].reshape(nz * rows, HD) + flat(dkvr[:, :, cols]).astype(f32)
            ).astype(b16)
    mgr[...] = matmul_tn(flat(fa[...]), mg[...]).astype(b16).reshape(mgr.shape)
    mix_grad_pair = links.start(mgr.at[:, oc], mgx, to_core)
    red_up[2].second()
    red_up[1].third()
    for first, count in GROUPS:
        part = matmul_nt(mg[first * rows : (first + count) * rows], flat(mixc[...]))
        p4[first : first + count] = part.astype(b16).reshape(count, n, quarter, width)
    attn_pair.wait_recv()
    tz[...] = (tg[one(c)].reshape(tz.shape).astype(f32) + tgr[...].astype(f32)).astype(b16)
    red_attn.first()
    out_delta = aft[...] + rs_out.result() + vec(down_bias)
    od[...] = out_delta.astype(b16).reshape(od.shape)
    hop_o = scatter_z(od, oh1)
    oh1[one(z)] = od[one(z)]
    mix_grad_pair.wait_recv()
    ms[...] = (mgr[:, one(c)].reshape(ms.shape).astype(f32) + mgx[...].astype(f32)).astype(b16)
    hop_md = [links.start(ms.at[dps[k]], md.at[dp], to_dp[k]) for k in (1, 2, 3)]
    rs_first = [Scatter(p4, r4, t4, first, count) for first, count in GROUPS]
    md[one(dp)] = ms[one(dp)]
    red_mix[0].first()
    red_up[3].second()
    red_up[2].third()
    for copy, item in zip(hop_md[:2], red_mix[1:3]):
        copy.wait_recv()
        item.first()
    rs_first[0].forward()
    hop_md[2].wait_recv()
    red_mix[3].first()
    red_attn.second()
    red_up[3].third()
    red_mix[0].second()
    red_attn.third()
    rs_first[1].forward()
    red_mix[1].second()
    red_mix[0].third()

    gain_sum, shift_sum = 0.0, 0.0
    for (first, count), item in zip(GROUPS, rs_first):
        at = slice(first * quarter, (first + count) * quarter)
        first_grad = item.result()
        hat = hat1[at]
        back = res[at] + norm_back(first_grad, hat, rstd1[at], vec(gain1))
        idl[first : first + count] = back.astype(b16).reshape(count, quarter, width)
        gain_sum += jnp.sum(first_grad * hat, axis=0, keepdims=True)
        shift_sum += jnp.sum(first_grad, axis=0, keepdims=True)
    hop_i = scatter_z(idl, ih1)
    ih1[one(z)] = idl[one(z)]
    sm[0:1] = gain_sum
    sm[1:2] = shift_sum
    sm1[one(dp)] = sm[...].reshape(1, *sm.shape)
    small_dp = [links.start(sm, sm1.at[dp], to_dp[k]) for k in peers]

    run(red_down, "fourth")
    red_mix[2].second()
    red_mix[1].third()
    run(red_up, "fourth")
    red_attn.fourth()
    arrived(small_dp)
    sm2[one(z)] = jnp.sum(sm1[...], axis=0, keepdims=True)
    small_z = [links.start(sm2.at[z], sm2.at[z], to_z[k]) for k in peers]
    red_mix[3].second()
    red_mix[2].third()
    arrived(hop_o)
    hop_o = scatter_dp(oh1, out_o)
    out_o[one(dp)] = oh1[one(dp)]
    red_mix[0].fourth()
    red_mix[3].third()
    red_mix[1].fourth()
    arrived(small_z)
    sm3[one(c)] = jnp.sum(sm2[...], axis=0, keepdims=True)
    small_core = links.start(sm3.at[c], sm3.at[c], to_core)
    arrived(hop_i)
    hop_i = scatter_dp(ih1, in_o)
    in_o[one(dp)] = ih1[one(dp)]
    run(red_down + red_up + [red_attn], "done")
    outgoing = [fetch(down_o, down_hbm), fetch(up_o, up_hbm), fetch(attn_o, attn_hbm)]
    red_mix[2].fourth()
    red_mix[3].fourth()
    small_core.wait_recv()
    small_o[...] = sm3[0] + sm3[1]
    arrived(hop_o)
    outgoing.append(fetch(out_o, out_hbm))
    run(red_mix, "done")
    outgoing.append(fetch(mix_o, mix_hbm))
    arrived(hop_i)
    outgoing.append(fetch(in_o, in_hbm))
    links.finish()
    for copy in outgoing:
        copy.wait()


def finish_kernel(*refs):
    f32 = jnp.float32
    ins, outs, mats, held, sems = refs[:9], refs[9:24], refs[24:30], refs[30:39], refs[39]
    out_ref, in_ref, mix_ref, attn_ref, up_ref, down_ref, small_ref, x_ref, cot_ref = held
    shard, width = mats[3].shape
    n = mix_ref.shape[0]
    fetches = {}
    for number in (5, 4, 2, 3, 0, 7, 1, 8, 6):
        fetches[number] = pltpu.make_async_copy(ins[number], held[number], sems.at[6 + number])
        fetches[number].start()
    copies = []

    def store(number, target):
        copy = pltpu.make_async_copy(mats[number], target, sems.at[number])
        copy.start()
        copies.append(copy)

    fetches[5].wait()
    mats[5][...] = flat(down_ref[...]).astype(f32)
    store(5, outs[13])
    fetches[4].wait()
    mats[4][...] = flat(up_ref[...]).astype(f32)
    store(4, outs[11])
    fetches[2].wait()
    for d in range(n):
        value = mix_ref[d].reshape(shard, 3 * shard).astype(f32)
        for part, place_at in ((0, 1), (1, 2), (2, 0)):
            start = place_at * width + d * shard
            mats[2][:, start : start + shard] = value[:, part * shard : (part + 1) * shard]
    store(2, outs[4])
    fetches[3].wait()
    mats[3][...] = flat(attn_ref[...]).astype(f32)
    store(3, outs[7])
    fetches[0].wait()
    fetches[7].wait()
    mats[0][...] = x_ref[...] + flat(out_ref[...]).astype(f32)
    store(0, outs[0])
    fetches[1].wait()
    fetches[8].wait()
    mats[1][...] = cot_ref[...] + flat(in_ref[...]).astype(f32)
    store(1, outs[1])
    fetches[6].wait()
    for number, row in ((2, 0), (3, 1), (5, 2), (6, 3), (8, 4), (9, 5), (10, 6), (14, 7)):
        outs[number][...] = small_ref[row : row + 1].reshape(width)
    for k in range(n):
        outs[12][k * width : (k + 1) * width] = small_ref[8 + k : 9 + k].reshape(width)
    for copy in copies:
        copy.wait()


def plane_body(
    block_input,
    out_cotangent,
    first_gain,
    first_shift,
    mix_weight,
    query_bias,
    value_bias,
    attn_weight,
    attn_bias,
    second_gain,
    second_shift,
    up_weight,
    up_bias,
    down_weight,
    down_bias,
):
    b16, f32 = jnp.bfloat16, jnp.float32
    n, nz = lax.axis_size("dp"), lax.axis_size("ctx") // 2
    rows, width = block_input.shape[1:]
    quarter = rows // n
    shard = width // n
    half = shard // 2
    hidden = up_weight.shape[1] // n
    heads = H // n
    tokens = nz * rows
    keys = 2 * tokens
    x_rows = block_input.reshape(rows, width)
    cot = out_cotangent.reshape(rows, width)
    vm = pltpu.VMEM
    stack = vm((n, quarter, width), b16)
    part = vm((nz, n, quarter, width), b16)
    part_recv = vm((n - 1, nz, quarter, width), b16)
    own = vm((nz * quarter, width), f32)
    results = [
        (n, quarter, width),
        (n, quarter, width),
        (n, 2, half, 3 * shard),
        (2, half, width),
        (2, half, n * hidden),
        (2, hidden // 2, width),
    ]
    scratch = [
        pltpu.SemaphoreType.DMA((SEMS,)),
        pltpu.SemaphoreType.DMA((SEMS,)),
        pltpu.SemaphoreType.DMA((24,)),
    ] + [vm(shape, b16) for shape in results] + [vm((width,), f32)] * 7 + [
        vm((n * hidden,), f32), vm((width,), f32),
        vm((rows, width), f32), vm((rows, width), f32),
        vm((half, 3 * width), b16), vm((shard, width), b16), vm((hidden, width), b16),
        stack, stack, stack, stack, stack, stack,
        vm((n, half, 3 * shard), b16), vm((n, 2, half, 3 * shard), b16),
        vm((n, nz, shard // nz, hidden), b16), part, part, part, part,
        vm((tokens, shard), b16), vm((nz, 2, rows, 2 * shard), b16),
        vm((heads, keys, HD), b16), vm((heads, keys, HD), b16),
        vm((tokens, shard), b16), vm((heads, tokens, 1), f32), vm((tokens, shard), b16),
        own, own, own, own,
        part, part, part, part, part_recv, part_recv, part_recv, part_recv,
        stack, stack, stack, stack,
        vm((tokens, hidden), f32), vm((tokens, hidden), b16), vm((tokens, hidden), b16),
        vm((2, hidden // 2, width), b16),
    ] + [vm((hidden // 2, width), b16)] * 4 + [
        vm((n, 2, half, hidden), b16), vm((n, half, hidden), b16), vm((n, half, hidden), b16),
    ] + [vm((half, n * hidden), b16)] * 3 + [
        vm((2, half, width), b16),
    ] + [vm((half, width), b16)] * 4 + [
        vm((heads, nz, 2, rows, HD), f32), vm((heads, nz, 2, rows, HD), f32),
        vm((nz, rows, 2 * shard), b16), vm((nz, rows, 2 * shard), b16),
        vm((tokens, 3 * shard), b16),
        vm((n, 2, half, 3 * shard), b16),
    ] + [vm((n, half, 3 * shard), b16)] * 5 + [
        stack, stack, stack, stack,
        vm((16, width), f32), vm((n, 16, width), f32), vm((nz, 16, width), f32),
        vm((2, 16, width), f32),
    ]
    hbm = pl.BlockSpec(memory_space=pl.ANY)
    near = pl.BlockSpec(memory_space=pltpu.VMEM)
    far = pl.BlockSpec(memory_space=pltpu.HBM)
    shapes = [(shape, b16) for shape in results] + [((16, width), f32)]
    pieces = pl.pallas_call(
        plane_kernel,
        out_shape=[jax.ShapeDtypeStruct(shape, dtype) for shape, dtype in shapes],
        in_specs=[far] * 15,
        out_specs=[hbm] * len(results) + [near],
        scratch_shapes=scratch,
        compiler_params=pltpu.CompilerParams(
            collective_id=0, has_side_effects=True, vmem_limit_bytes=60 * 1024 * 1024
        ),
        name="plane",
    )(
        x_rows, cot, first_gain, first_shift, mix_weight, query_bias, value_bias, attn_weight,
        attn_bias, second_gain, second_shift, up_weight, up_bias, down_weight, down_bias,
    )
    final = [
        (rows, width), (rows, width), (width,), (width,), (shard, 3 * width), (width,), (width,),
        (shard, width), (width,), (width,), (width,), (shard, n * hidden), (n * hidden,),
        (hidden, width), (width,),
    ]
    large = (0, 1, 4, 7, 11, 13)
    outs = pl.pallas_call(
        finish_kernel,
        out_shape=[jax.ShapeDtypeStruct(shape, f32) for shape in final],
        in_specs=[far] * 9,
        out_specs=[hbm if k in large else near for k in range(len(final))],
        scratch_shapes=[vm(final[k], f32) for k in large]
        + [vm(shape, dtype) for shape, dtype in shapes]
        + [vm((rows, width), f32), vm((rows, width), f32), pltpu.SemaphoreType.DMA((16,))],
        compiler_params=pltpu.CompilerParams(vmem_limit_bytes=60 * 1024 * 1024),
        name="finish",
    )(*pieces, x_rows, cot)
    return (
        outs[0].reshape(1, rows, width),
        outs[1].reshape(1, rows, width),
        *outs[2:],
    )


def fits(mesh):
    n, ctx = mesh.shape["dp"], mesh.shape["ctx"]
    return n == 4 and ctx == 8 and H % n == 0


def solution(mesh):
    placed = (
        P("dp", "ctx", None),
        P("dp", "ctx", None),
        P(),
        P(),
        P("dp", None),
        P(),
        P(),
        P("dp", None),
        P(),
        P(),
        P(),
        P("dp", None),
        P(),
        P("dp", None),
        P(),
    )
    return jax.shard_map(
        plane_body if fits(mesh) else body,
        mesh=mesh,
        in_specs=placed,
        out_specs=(
            P("dp", "ctx", None),
            P("dp", "ctx", None),
            P(),
            P(),
            P("dp", None),
            P(),
            P(),
            P("dp", None),
            P(),
            P(),
            P(),
            P("dp", None),
            P(),
            P("dp", None),
            P(),
        ),
        check_vma=False,
    )
```

```python
import functools
import math

import jax
import jax.numpy as jnp
from jax import lax
from jax.experimental import pallas as pl
from jax.experimental.pallas import tpu as pltpu
from jax.sharding import PartitionSpec as P

H = 12
HD = 64


EPS = 1e-05
GELU_C = math.sqrt(2.0 / math.pi)


def from_behind(value, axis, steps):
    count = lax.axis_size(axis)
    pairs = [(source, (source + steps) % count) for source in range(count)]
    return lax.ppermute(value, axis, pairs)


def layer_norm(x, gain, shift):
    centered = x - jnp.mean(x, axis=-1, keepdims=True)
    rstd = lax.rsqrt(jnp.mean(centered * centered, axis=-1, keepdims=True) + EPS)
    x_hat = centered * rstd
    return (x_hat, rstd, x_hat * gain + shift)


def norm_back(grad, x_hat, rstd, gain):
    g = grad * gain
    return rstd * (
        g
        - jnp.mean(g, axis=-1, keepdims=True)
        - x_hat * jnp.mean(g * x_hat, axis=-1, keepdims=True)
    )


def gelu_pair(u):
    inner = GELU_C * (u + 0.044715 * u * u * u)
    t = jnp.tanh(inner)
    value = 0.5 * u * (1.0 + t)
    slope = 0.5 * (1.0 + t) + 0.5 * u * (1.0 - t * t) * GELU_C * (1.0 + 3.0 * 0.044715 * u * u)
    return (value, slope)


def matmul(a, b):
    return jnp.dot(a, b, preferred_element_type=jnp.float32)


def matmul_tn(a, b):
    return lax.dot_general(a, b, (((0,), (0,)), ((), ())), preferred_element_type=jnp.float32)


def matmul_nt(a, b):
    return lax.dot_general(a, b, (((1,), (1,)), ((), ())), preferred_element_type=jnp.float32)


def body(
    block_input,
    out_cotangent,
    first_gain,
    first_shift,
    mix_weight,
    query_bias,
    value_bias,
    attn_weight,
    attn_bias,
    second_gain,
    second_shift,
    up_weight,
    up_bias,
    down_weight,
    down_bias,
):
    rows = block_input.shape[1]
    width = block_input.shape[2]
    scale = HD ** (-0.5)
    x_rows = block_input.reshape(rows, width)
    cot = out_cotangent.reshape(rows, width)
    mix_full, attn_full, up_full, down_full = (
        lax.all_gather(mix_weight, "dp", axis=0, tiled=True),
        lax.all_gather(attn_weight, "dp", axis=0, tiled=True),
        lax.all_gather(up_weight, "dp", axis=0, tiled=True),
        lax.all_gather(down_weight, "dp", axis=0, tiled=True),
    )
    first_hat, first_rstd, first_out = layer_norm(x_rows, first_gain, first_shift)
    first_in = first_out.astype(jnp.bfloat16)
    mixed = matmul(first_in, mix_full)
    queries = (mixed[:, :width] + query_bias).astype(jnp.bfloat16)
    keys = mixed[:, width : 2 * width].astype(jnp.bfloat16)
    values = (mixed[:, 2 * width :] + value_bias).astype(jnp.bfloat16)
    q3 = queries.reshape(rows, H, HD)
    me = lax.axis_index("ctx")
    cycle_size = lax.axis_size("ctx")
    q_pos = me * rows + jnp.arange(rows)
    q_last = me * rows + rows - 1
    start_state = (
        jnp.full((H, rows), -1e30, jnp.float32),
        jnp.zeros((H, rows), jnp.float32),
        jnp.zeros((H, rows, HD), jnp.float32),
    )
    carry = start_state
    key_piece = lax.all_gather(keys, "ctx", axis=0, tiled=True)
    value_piece = lax.all_gather(values, "ctx", axis=0, tiled=True)
    count = key_piece.shape[0]
    kblock = math.gcd(count, 512)
    nblocks = count // kblock
    key_blocks = key_piece.reshape(nblocks, kblock, H, HD)
    value_blocks = value_piece.reshape(nblocks, kblock, H, HD)
    offsets = jnp.arange(nblocks) * kblock

    def one_block(state, item):
        key_blk, value_blk, offset = item

        def compute(state_in):
            run_max, run_total, run_acc = state_in
            key_pos = offset + jnp.arange(kblock)
            allowed = (key_pos[None, :] <= q_pos[:, None])[None]
            scores = (
                jnp.einsum("qhd,khd->hqk", q3, key_blk, preferred_element_type=jnp.float32) * scale
            )
            scores = jnp.where(allowed, scores, -1e30)
            new_max = jnp.maximum(run_max, jnp.max(scores, axis=-1))
            expo = jnp.where(allowed, jnp.exp(scores - new_max[..., None]), 0.0)
            factor = jnp.exp(run_max - new_max)
            new_total = run_total * factor + jnp.sum(expo, axis=-1)
            new_acc = run_acc * factor[..., None] + jnp.einsum(
                "hqk,khd->hqd", expo, value_blk.astype(jnp.float32), precision=lax.Precision.HIGHEST
            )
            return (new_max, new_total, new_acc)

        def keep_state(state_in):
            return state_in

        return (lax.cond(offset <= q_last, compute, keep_state, state), None)

    carry, unused = lax.scan(one_block, carry, (key_blocks, value_blocks, offsets))
    run_max, run_total, run_acc = carry
    attended = (
        (run_acc / run_total[..., None])
        .transpose(1, 0, 2)
        .reshape(rows, width)
        .astype(jnp.bfloat16)
    )
    lse = run_max + jnp.log(run_total)
    after_attn = x_rows + matmul(attended, attn_full) + attn_bias
    second_hat, second_rstd, second_out = layer_norm(after_attn, second_gain, second_shift)
    second_in = second_out.astype(jnp.bfloat16)
    pre_act = matmul(second_in, up_full) + up_bias
    act_value, act_slope = gelu_pair(pre_act)
    activ = act_value.astype(jnp.bfloat16)
    block_output = after_attn + matmul(activ, down_full) + down_bias
    mix_back, attn_back, up_back, down_back = (
        lax.all_gather(mix_weight, "dp", axis=0, tiled=True),
        lax.all_gather(attn_weight, "dp", axis=0, tiled=True),
        lax.all_gather(up_weight, "dp", axis=0, tiled=True),
        lax.all_gather(down_weight, "dp", axis=0, tiled=True),
    )
    cot_b = cot.astype(jnp.bfloat16)
    down_weight_grad = matmul_tn(activ, cot_b)
    down_bias_grad = jnp.sum(cot, axis=0)
    pre_grad = matmul_nt(cot_b, down_back) * act_slope
    pre_grad_b = pre_grad.astype(jnp.bfloat16)
    up_weight_grad = matmul_tn(second_in, pre_grad_b)
    up_bias_grad = jnp.sum(pre_grad, axis=0)
    second_grad = matmul_nt(pre_grad_b, up_back)
    second_gain_grad = jnp.sum(second_grad * second_hat, axis=0)
    second_shift_grad = jnp.sum(second_grad, axis=0)
    resid_grad = cot + norm_back(second_grad, second_hat, second_rstd, second_gain)
    resid_b = resid_grad.astype(jnp.bfloat16)
    attn_weight_grad = matmul_tn(attended, resid_b)
    attn_bias_grad = jnp.sum(resid_grad, axis=0)
    attended_grad = matmul_nt(resid_b, attn_back).astype(jnp.bfloat16)
    grad3 = attended_grad.reshape(rows, H, HD)
    delta = jnp.sum(
        grad3.astype(jnp.float32) * attended.astype(jnp.float32).reshape(rows, H, HD), axis=-1
    ).T

    def block_grads(key_blk, value_blk, key_start):
        count = key_blk.shape[0]
        key3 = key_blk.reshape(count, H, HD)
        value3 = value_blk.reshape(count, H, HD)
        key_pos = key_start + jnp.arange(count)
        allowed = (key_pos[None, :] <= q_pos[:, None])[None]
        scores = jnp.einsum("qhd,khd->hqk", q3, key3, preferred_element_type=jnp.float32) * scale
        probs = jnp.where(allowed, jnp.exp(scores - lse[..., None]), 0.0)
        dprob = jnp.einsum("qhd,khd->hqk", grad3, value3, preferred_element_type=jnp.float32)
        dscore = probs * (dprob - delta[..., None])
        probs_b = probs.astype(jnp.bfloat16)
        dscore_b = dscore.astype(jnp.bfloat16)
        value_add = jnp.einsum("hqk,qhd->khd", probs_b, grad3, preferred_element_type=jnp.float32)
        key_add = (
            jnp.einsum("hqk,qhd->khd", dscore_b, q3, preferred_element_type=jnp.float32) * scale
        )
        query_add = (
            jnp.einsum("hqk,khd->qhd", dscore_b, key3, preferred_element_type=jnp.float32) * scale
        )
        return (
            query_add.reshape(rows, width),
            key_add.reshape(count, width),
            value_add.reshape(count, width),
        )

    def skip_grads(key_blk, value_blk, key_start):
        count = key_blk.shape[0]
        empty = jnp.zeros((count, width), jnp.float32)
        return (jnp.zeros((rows, width), jnp.float32), empty, empty)

    zeros = jnp.zeros((rows, width), jnp.float32)

    def pass_grads(key_acc, value_acc):
        return (
            from_behind(key_acc.astype(jnp.bfloat16), "ctx", -1).astype(key_acc.dtype),
            from_behind(value_acc.astype(jnp.bfloat16), "ctx", -1).astype(value_acc.dtype),
        )

    def cycle_turn(step, state):
        key_blk, value_blk, key_acc, value_acc, query_acc = state
        owner = (me + step) % cycle_size
        query_add, key_add, value_add = lax.cond(
            owner <= me, block_grads, skip_grads, key_blk, value_blk, owner * rows
        )
        key_blk, value_blk = from_behind((key_blk, value_blk), "ctx", -1)
        key_acc, value_acc = pass_grads(key_acc + key_add, value_acc + value_add)
        return (key_blk, value_blk, key_acc, value_acc, query_acc + query_add)

    key_blk, value_blk, key_acc, value_acc, query_acc = lax.fori_loop(
        0, cycle_size - 1, cycle_turn, (keys, values, zeros, zeros, zeros)
    )
    last_owner = (me + cycle_size - 1) % cycle_size
    query_add, key_add, value_add = lax.cond(
        last_owner <= me, block_grads, skip_grads, key_blk, value_blk, last_owner * rows
    )
    key_grad, value_grad = pass_grads(key_acc + key_add, value_acc + value_add)
    query_grad = query_acc + query_add
    query_bias_grad = jnp.sum(query_grad, axis=0)
    value_bias_grad = jnp.sum(value_grad, axis=0)
    mixed_grad = jnp.concatenate([query_grad, key_grad, value_grad], axis=1).astype(jnp.bfloat16)
    mix_weight_grad = matmul_tn(first_in, mixed_grad)
    first_grad = matmul_nt(mixed_grad, mix_back)
    first_gain_grad = jnp.sum(first_grad * first_hat, axis=0)
    first_shift_grad = jnp.sum(first_grad, axis=0)
    input_grad = resid_grad + norm_back(first_grad, first_hat, first_rstd, first_gain)
    local_mats = (mix_weight_grad, attn_weight_grad, up_weight_grad, down_weight_grad)
    shard_sums = (
        lax.psum_scatter(
            local_mats[0].astype(jnp.bfloat16), "dp", scatter_dimension=0, tiled=True
        ).astype(jnp.float32),
        lax.psum_scatter(
            local_mats[1].astype(jnp.bfloat16), "dp", scatter_dimension=0, tiled=True
        ).astype(jnp.float32),
        lax.psum_scatter(
            local_mats[2].astype(jnp.bfloat16), "dp", scatter_dimension=0, tiled=True
        ).astype(jnp.float32),
        lax.psum_scatter(
            local_mats[3].astype(jnp.bfloat16), "dp", scatter_dimension=0, tiled=True
        ).astype(jnp.float32),
    )
    mats = (
        lax.psum(shard_sums[0].astype(jnp.bfloat16), "ctx").astype(jnp.float32),
        lax.psum(shard_sums[1].astype(jnp.bfloat16), "ctx").astype(jnp.float32),
        lax.psum(shard_sums[2].astype(jnp.bfloat16), "ctx").astype(jnp.float32),
        lax.psum(shard_sums[3].astype(jnp.bfloat16), "ctx").astype(jnp.float32),
    )
    smalls = lax.psum(
        (
            first_gain_grad,
            first_shift_grad,
            query_bias_grad,
            value_bias_grad,
            attn_bias_grad,
            second_gain_grad,
            second_shift_grad,
            up_bias_grad,
            down_bias_grad,
        ),
        ("dp", "ctx"),
    )
    return (
        block_output.reshape(1, rows, width),
        input_grad.reshape(1, rows, width),
        smalls[0],
        smalls[1],
        mats[0],
        smalls[2],
        smalls[3],
        mats[1],
        smalls[4],
        smalls[5],
        smalls[6],
        mats[2],
        smalls[7],
        mats[3],
        smalls[8],
    )


def flip(index, mask):
    bit = 1
    while bit <= mask:
        if mask & bit:
            index = index + bit - 2 * bit * ((index // bit) % 2)
        bit *= 2
    return index


MESH = pl.DeviceIdType.MESH
GROUPS = ((2, 2), (0, 2))
SEMS = 224


class Links:
    def __init__(self, send, recv):
        self.send, self.recv, self.count, self.open = send, recv, 0, []

    def make(self, source, target, device):
        number = self.count
        self.count += 1
        return pltpu.make_async_remote_copy(
            src_ref=source,
            dst_ref=target,
            send_sem=self.send.at[number],
            recv_sem=self.recv.at[number],
            device_id=device,
            device_id_type=MESH,
        )

    def start(self, source, target, device):
        copy = self.make(source, target, device)
        copy.start()
        self.open.append(copy)
        return copy

    def finish(self):
        for copy in self.open:
            copy.wait_send()


def arrived(copies):
    for copy in copies:
        copy.wait_recv()


def flat(value):
    return value.reshape(-1, value.shape[-1])


def plane_kernel(
    x_in, cot_in, gain1_in, shift1_in, mix_w, q_bias_in, v_bias_in, attn_w, attn_bias_in, gain2_in,
    shift2_in, up_w, up_bias_in, down_w, down_bias_in,
    out_hbm, in_hbm, mix_hbm, attn_hbm, up_hbm, down_hbm, small_o,
    send_sem, recv_sem, local_sem,
    out_o, in_o, mix_o, attn_o, up_o, down_o,
    gain1, shift1, q_bias, v_bias, attn_bias, gain2, shift2, up_bias, down_bias,
    xv, cv, mw, aw, dw,
    xs, xh1, xh2, cs, ch1, ch2,
    mst, mixc, upc, fa, ca, sa, ra,
    qs, kv, kh, vh, att, lse, agr,
    hat1, aft, hat2, res,
    p1, p2, p3, p4, r1, r2, r3, r4, t1, t2, t3, t4,
    dact, act, pg,
    dg, dgr, dz, dz1, dz2,
    ug, ugr, us, ud, uz1, uz2,
    tg, tgr, tz, tz1, tz2,
    dka, dva, dkvs, dkvr, mg,
    mgr, mgx, ms, md, mz1, mz2,
    od, oh1, idl, ih1,
    sm, sm1, sm2, sm3,
):
    b16, f32 = jnp.bfloat16, jnp.float32
    n, quarter, width = xs.shape
    nz = xh2.shape[0]
    rows = n * quarter
    half, hidden = mixc.shape[2], upc.shape[3]
    shard = 2 * half
    heads = kh.shape[0]
    dp, ctx = lax.axis_index("dp"), lax.axis_index("ctx")
    z, c = ctx // 2, ctx % 2
    oc = 1 - c
    dps = [flip(dp, k) for k in range(n)]
    zs = [flip(z, k) for k in range(nz)]
    to_dp = [(dps[k], ctx) for k in range(n)]
    to_z = [(dp, 2 * zs[k] + c) for k in range(nz)]
    to_core = (dp, 2 * z + oc)
    inner = (z + 1) // 2 % 2 == 1
    outer = (z + 1) // 2 % 2 == 0
    peers = (3, 1, 2)
    links = Links(send_sem, recv_sem)
    one = lambda index: pl.ds(index, 1)

    locals_ = []

    def fetch(source, target):
        copy = pltpu.make_async_copy(source, target, local_sem.at[len(locals_)])
        copy.start()
        locals_.append(copy)
        return copy

    my_half = pl.ds(pl.multiple_of(c * half, 16), half)
    get_x = fetch(x_in, xv)
    get_mix = fetch(mix_w.at[my_half], mw)
    get_cot = fetch(cot_in, cv)
    get_vectors = [
        fetch(source, target)
        for source, target in (
            (gain1_in, gain1), (shift1_in, shift1), (q_bias_in, q_bias), (v_bias_in, v_bias),
            (attn_bias_in, attn_bias), (gain2_in, gain2), (shift2_in, shift2),
            (up_bias_in, up_bias), (down_bias_in, down_bias),
        )
    ]
    get_attn = fetch(attn_w, aw)
    get_down = fetch(down_w, dw)
    columns = lambda index: pl.ds(pl.multiple_of(index * hidden, 128), hidden)
    strip = shard // nz
    up_rows = pl.ds(pl.multiple_of(z * strip, 16), strip)
    up_half = lambda index: pl.ds(pl.multiple_of(index * (hidden // 2), 128), hidden // 2)
    up_piece = lambda index: up_w.at[
        up_rows, pl.ds(pl.multiple_of(index * hidden + c * (hidden // 2), 128), hidden // 2)
    ]
    get_up = fetch(up_piece(dp), upc.at[dp, z, :, up_half(c)])

    barrier = pltpu.get_barrier_semaphore()
    everyone = to_dp[1:] + to_z[1:] + [to_core]
    for device in everyone:
        pl.semaphore_signal(barrier, inc=1, device_id=device, device_id_type=MESH)

    get_x.wait()
    xs[...] = xv[...].astype(b16).reshape(n, quarter, width)
    pl.semaphore_wait(barrier, len(everyone))

    def scatter_dp(source, target):
        return [links.start(source.at[dps[k]], target.at[dp], to_dp[k]) for k in peers]

    def scatter_z(source, target):
        return [links.start(source.at[zs[k]], target.at[z], to_z[k]) for k in peers]

    class Gather:
        def __init__(self, ref, first, count):
            self.ref, self.first, self.mid = ref, first, first + count // 2
            part = ref.at[pl.ds(first, count), dp]
            self.near = [links.start(part, part, to_dp[k]) for k in (1, 2)]

        def forward(self):
            arrived(self.near)
            self.far = []
            for begin, origin, target in ((self.first, 1, 2), (self.mid, 2, 1)):
                part = self.ref.at[pl.ds(begin, self.mid - self.first), dps[origin]]
                self.far.append(links.start(part, part, to_dp[target]))

        def wait(self):
            arrived(self.far)

    class Scatter:
        def __init__(self, ref, recv, stage, first, count):
            self.ref, self.recv, self.stage = ref, recv, stage
            self.first, self.count, step = first, count, count // 2
            self.ways = ((first, step, 1, 2), (first + step, step, 2, 1))
            self.pass_on, self.mine = [], []
            for begin, size, near, _ in self.ways:
                for role, slot, copies in ((1, 3, self.pass_on), (0, near, self.mine)):
                    source = ref.at[pl.ds(begin, size), dps[slot]]
                    target = recv.at[role, pl.ds(begin, size)]
                    copies.append(links.start(source, target, to_dp[near]))

        def forward(self):
            self.last = []
            for (begin, size, _, beyond), copy in zip(self.ways, self.pass_on):
                copy.wait_recv()
                at = pl.ds(begin, size)
                value = self.ref[at, one(dps[beyond])].astype(f32).reshape(size, quarter, width)
                value = value + self.recv[1, at].astype(f32)
                self.stage[at] = value.astype(b16)
                self.last.append(
                    links.start(self.stage.at[at], self.recv.at[2, at], to_dp[beyond])
                )

        def result(self):
            arrived(self.mine)
            arrived(self.last)
            at = slice(self.first, self.first + self.count)
            total = self.ref[at, one(dp)].astype(f32).reshape(self.count * quarter, width)
            return total + flat(self.recv[0, at].astype(f32)) + flat(self.recv[2, at].astype(f32))

    class DirectGather:
        def __init__(self, ref, first, count):
            part = ref.at[pl.ds(first, count), dp]
            self.all = [links.start(part, part, to_dp[k]) for k in peers]

        def forward(self):
            pass

        def wait(self):
            arrived(self.all)

    class DirectScatter:
        def __init__(self, ref, recv, stage, first, count):
            self.ref, self.recv, self.first, self.count = ref, recv, first, count
            at = pl.ds(first, count)
            self.all = [
                links.start(ref.at[at, dps[k]], recv.at[k - 1, at], to_dp[k]) for k in peers
            ]

        def forward(self):
            pass

        def result(self):
            arrived(self.all)
            at = slice(self.first, self.first + self.count)
            total = self.ref[at, one(dp)].astype(f32).reshape(self.count * quarter, width)
            for k in range(1, n):
                total += flat(self.recv[k - 1, at].astype(f32))
            return total

    def gather(*spec):
        return (Gather if spec[1] else DirectGather)(*spec)

    def scatter(*spec):
        return (Scatter if spec[3] else DirectScatter)(*spec)

    def run(items, step):
        for item in items:
            getattr(item, step)()

    hop_x = scatter_dp(xs, xh1)
    xh1[one(dp)] = xs[one(dp)]
    get_mix.wait()
    mv = mw[...]
    for d in range(n):
        mst[d] = jnp.concatenate(
            [mv[:, part * width + d * shard : part * width + (d + 1) * shard] for part in (1, 2, 0)],
            axis=1,
        )
    mixc[one(dp), one(c)] = mst[one(dp)].reshape(1, 1, half, 3 * shard)
    for copy in [get_cot] + get_vectors:
        copy.wait()
    cot = cv[...]
    cs[...] = cot.astype(b16).reshape(n, quarter, width)
    ch1[one(dp)] = cs[one(dp)]
    arrived(hop_x)
    hop_x = scatter_z(xh1, xh2)
    hop_mix = [links.start(mst.at[dps[k]], mixc.at[dp, c], to_dp[k]) for k in peers]
    hop_c = scatter_dp(cs, ch1)
    xh2[one(z)] = xh1[one(z)]
    sm[...] = jnp.zeros(sm.shape, f32)
    sm[7:8] = jnp.sum(cot, axis=0, keepdims=True)

    vec = lambda ref: ref[...].reshape(1, -1)

    def pick(ref, size):
        value = vec(ref)
        total = jnp.zeros((1, size), f32)
        for k in range(n):
            total = jnp.where(dp == k, value[:, k * size : (k + 1) * size], total)
        return total

    arrived(hop_x)
    x_hat, rstd1, first = layer_norm(flat(xh2[...]).astype(f32), vec(gain1), vec(shift1))
    hat1[...] = x_hat
    fa[:, one(dp)] = first.astype(b16).reshape(nz, 1, quarter, width)
    ag_first = [Gather(fa, first, count) for first, count in GROUPS]
    kv_bias = jnp.concatenate([jnp.zeros((1, shard), f32), pick(v_bias, shard)], axis=1)
    own_q_bias = pick(q_bias, shard)
    arrived(hop_mix)
    mix_pair = links.start(mixc.at[:, c], mixc.at[:, c], to_core)
    arrived(hop_c)
    hop_c = scatter_z(ch1, ch2)
    ch2[one(z)] = ch1[one(z)]

    run(ag_first, "forward")
    run(ag_first, "wait")
    hop_up = [
        links.start(up_piece(dps[k]), upc.at[dp, z, :, up_half(c)], to_dp[k]) for k in peers
    ]
    arrived(hop_c)
    ca[:, one(dp)] = ch2[...].reshape(nz, 1, quarter, width)
    ag_cot = Gather(ca, 0, nz)
    mix_pair.wait_recv()
    first_all = flat(fa[...])
    mixed = matmul(first_all, flat(mixc[:, :, :, : 2 * shard])) + kv_bias
    kv[:, one(c)] = mixed.astype(b16).reshape(nz, 1, rows, 2 * shard)
    kv_pair = links.start(kv.at[:, c], kv.at[:, c], to_core)
    scale = HD ** (-0.5)
    queries = matmul(first_all, flat(mixc[:, :, :, 2 * shard :])) + own_q_bias
    qs[...] = (queries * scale).astype(b16)
    arrived(hop_up)
    get_up.wait()
    up_strip = upc.at[:, z, :, up_half(c)]
    hop_up = [links.start(up_strip, up_strip, to_z[k]) for k in peers]
    kv_pair.wait_recv()
    for h in range(heads):
        kh[h] = flat(kv[:, :, :, h * HD : (h + 1) * HD])
        vh[h] = flat(kv[:, :, :, shard + h * HD : shard + (h + 1) * HD])

    last = 2 * rows
    allowed = (
        lax.broadcasted_iota(jnp.int32, (rows, last), 1)
        <= lax.broadcasted_iota(jnp.int32, (rows, last), 0) + c * rows
    )

    def spans(j):
        return ([(0, j * last)] if j else []) + [(j * last, (j + 1) * last)]

    def attend(j):
        at = slice(j * rows, (j + 1) * rows)
        for h in range(heads):
            q = qs[at, h * HD : (h + 1) * HD]
            scores = []
            for a, b in spans(j):
                s = matmul_nt(q, kh[h, a:b])
                scores.append(jnp.where(allowed, s, -1e30) if b == (j + 1) * last else s)
            top = functools.reduce(
                jnp.maximum, [jnp.max(s, axis=-1, keepdims=True) for s in scores]
            )
            total, result = 0.0, 0.0
            for s, (a, b) in zip(scores, spans(j)):
                w = jnp.exp(s - top)
                total = total + jnp.sum(w, axis=-1, keepdims=True)
                result = result + matmul(w.astype(b16), vh[h, a:b])
            att[at, h * HD : (h + 1) * HD] = (result / total).astype(b16)
            lse[h, at] = top + jnp.log(total)

    get_attn.wait()
    ag_cot.forward()
    rs_attn = []
    for first, count in GROUPS:
        for j in range(first + count - 1, first - 1, -1):
            attend(j)
            if rs_attn and j == 1:
                rs_attn[0].forward()
        part = matmul(att[first * rows : (first + count) * rows], aw[...])
        p1[first : first + count] = part.astype(b16).reshape(count, n, quarter, width)
        rs_attn.append(scatter(p1, r1, t1, first, count))

    arrived(hop_up)
    up_pair = links.start(upc.at[:, :, :, up_half(c)], upc.at[:, :, :, up_half(c)], to_core)
    get_down.wait()
    ag_cot.wait()
    for first, count in GROUPS:
        if first == GROUPS[1][0]:
            rs_attn[1].forward()
        dact[first * rows : (first + count) * rows] = matmul_nt(
            flat(ca[first : first + count]), dw[...]
        )

    ag_second, rstd2 = [], []
    for (first, count), item in zip(GROUPS, rs_attn):
        at = slice(first * quarter, (first + count) * quarter)
        after = item.result() + vec(attn_bias)
        aft[at] = after
        after = after + flat(xh2[first : first + count]).astype(f32)
        hat, rstd, second = layer_norm(after, vec(gain2), vec(shift2))
        hat2[at] = hat
        rstd2.append(rstd)
        sa[first : first + count, one(dp)] = second.astype(b16).reshape(count, 1, quarter, width)
        ag_second.append(Gather(sa, first, count))

    run(ag_second, "forward")
    up_pair.wait_recv()
    own_up_bias = up_bias[columns(dp)].reshape(1, hidden)
    up_sum = jnp.zeros((1, hidden), f32)
    rs_second = []
    for (first, count), item in zip(GROUPS, ag_second):
        item.wait()
        at = slice(first * rows, (first + count) * rows)
        pre_act = matmul(flat(sa[first : first + count]), flat(upc[...])) + own_up_bias
        value, slope = gelu_pair(pre_act)
        act[at] = value.astype(b16)
        if rs_second:
            rs_second[0].forward()
        pre_grad = dact[at] * slope
        up_sum += jnp.sum(pre_grad, axis=0, keepdims=True)
        pg[at] = pre_grad.astype(b16)
        part = matmul_nt(pg[at], flat(upc[...]))
        p2[first : first + count] = part.astype(b16).reshape(count, n, quarter, width)
        rs_second.append(scatter(p2, r2, t2, first, count))
    for k in range(n):
        sm[8 + k : 9 + k] = jnp.where(dp == k, up_sum, 0.0)

    dg[...] = matmul_tn(act[...], flat(ca[...])).astype(b16).reshape(dg.shape)
    down_pair = links.start(dg.at[oc], dgr, to_core)
    rs_second[1].forward()
    ug[...] = matmul_tn(flat(sa[...]), pg[...]).astype(b16).reshape(ug.shape)
    up_grad_pair = links.start(ug.at[:, oc], ugr, to_core)

    class Reduce:
        def __init__(self, mine, sum1, sum2, total):
            self.mine, self.sum1, self.sum2, self.total = mine, sum1, sum2, total
            self.one = links.make(mine, sum1, to_z[1])
            self.two = links.make(mine, sum2, to_z[3])
            self.three = links.make(total, total, to_z[1])
            self.pair = links.make(total, total, to_core)

        def first(self):
            pl.when(outer)(lambda: self.one.start())

        def second(self):
            @pl.when(inner)
            def _():
                self.one.wait_recv()
                value = self.mine[...].astype(f32) + self.sum1[...].astype(f32)
                self.mine[...] = value.astype(b16)
                self.two.start()

        def third(self):
            @pl.when(inner)
            def _():
                self.two.wait_recv()
                value = self.mine[...].astype(f32) + self.sum2[...].astype(f32)
                self.total[...] = value.astype(b16).reshape(self.total.shape)
                self.three.start()
                self.pair.start()

        def fourth(self):
            @pl.when(outer)
            def _():
                self.three.wait_recv()
                self.pair.start()

        def done(self):
            self.pair.wait()

            @pl.when(outer)
            def _():
                self.one.wait_send()

            @pl.when(inner)
            def _():
                self.two.wait_send()
                self.three.wait_send()

    down_pair.wait_recv()
    dz[...] = (dg[one(c)].reshape(dz.shape).astype(f32) + dgr[...].astype(f32)).astype(b16)
    size = dz.shape[0] // n
    red_down = [
        Reduce(dz.at[part], dz1.at[part], dz2.at[part], down_o.at[c, part])
        for part in [pl.ds(k * size, size) for k in range(n)]
    ]
    run(red_down, "first")
    up_grad_pair.wait_recv()
    us[...] = (ug[:, one(c)].reshape(us.shape).astype(f32) + ugr[...].astype(f32)).astype(b16)
    ud[:, columns(dp)] = us[one(dp)].reshape(half, hidden)
    red_up = [
        Reduce(ud.at[:, part], uz1.at[:, part], uz2.at[:, part], up_o.at[c, :, part])
        for part in [columns(dps[k]) for k in range(n)]
    ]
    red_up[0].first()

    ag_resid = []
    gain_sum, shift_sum, bias_sum = 0.0, 0.0, 0.0
    for (first, count), item, rstd in zip(GROUPS, rs_second, rstd2):
        at = slice(first * quarter, (first + count) * quarter)
        second_grad = item.result()
        hat = hat2[at]
        back = norm_back(second_grad, hat, rstd, vec(gain2))
        res[at] = back
        resid = flat(ch2[first : first + count]).astype(f32) + back
        ra[first : first + count, one(dp)] = resid.astype(b16).reshape(count, 1, quarter, width)
        ag_resid.append(Gather(ra, first, count))
        gain_sum += jnp.sum(second_grad * hat, axis=0, keepdims=True)
        shift_sum += jnp.sum(second_grad, axis=0, keepdims=True)
        bias_sum += jnp.sum(resid, axis=0, keepdims=True)
    sm[4:5] = bias_sum
    sm[5:6] = gain_sum
    sm[6:7] = shift_sum

    red_down[0].second()
    run(ag_resid, "forward")
    hop_ud = [links.start(us.at[dps[k]], ud.at[:, columns(dp)], to_dp[k]) for k in (1, 2, 3)]
    red_down[1].second()
    part = matmul(act[...], dw[...])
    p3[...] = part.astype(b16).reshape(p3.shape)
    rs_out = Scatter(p3, r3, t3, 0, nz)
    red_down[0].third()

    def attend_back(j, fresh):
        at = slice(j * rows, (j + 1) * rows)
        for h in range(heads):
            cols = slice(h * HD, (h + 1) * HD)
            q, grad = qs[at, cols], agr[at, cols]
            delta = jnp.sum(grad.astype(f32) * att[at, cols].astype(f32), axis=-1, keepdims=True)
            base, total = lse[h, at], 0.0
            for a, b in spans(j):
                keys = kh[h, a:b]
                p = jnp.exp(matmul_nt(q, keys) - base)
                if b == (j + 1) * last:
                    p = jnp.where(allowed, p, 0.0)
                ds = (p * (matmul_nt(grad, vh[h, a:b]) - delta)).astype(b16)
                total = total + matmul(ds, keys)
                shape = ((b - a) // last, 2, rows, HD)
                dk = matmul_tn(ds, q).reshape(shape)
                dv = matmul_tn(p.astype(b16), grad).reshape(shape)
                blocks = slice(a // last, b // last)
                if fresh:
                    dka[h, blocks], dva[h, blocks] = dk, dv
                else:
                    dka[h, blocks] += dk
                    dva[h, blocks] += dv
            total = total * scale
            q_sum[h] = q_sum.get(h, 0.0) + jnp.sum(total, axis=0, keepdims=True)
            mg[at, 2 * shard + h * HD : 2 * shard + (h + 1) * HD] = total.astype(b16)

    q_sum = {}
    red_attn = Reduce(tz, tz1, tz2, attn_o.at[c])
    red_mix = [
        Reduce(md.at[dps[k]], mz1.at[k], mz2.at[k], mix_o.at[dps[k], c]) for k in range(n)
    ]

    def weights_of(first, count):
        return matmul_nt(flat(ra[first : first + count]), aw[...]).astype(b16)

    (first, count), (first2, count2) = GROUPS
    ag_resid[0].wait()
    agr[first * rows : (first + count) * rows] = weights_of(first, count)
    attend_back(3, True)
    red_down[2].second()
    red_down[1].third()
    attend_back(2, False)
    red_down[3].second()
    red_down[2].third()
    ag_resid[1].wait()
    agr[first2 * rows : (first2 + count2) * rows] = weights_of(first2, count2)
    attend_back(1, False)
    for copy, item in zip(hop_ud[:2], red_up[1:3]):
        copy.wait_recv()
        item.first()
    red_up[0].second()
    red_down[3].third()
    attend_back(0, False)
    hop_ud[2].wait_recv()
    red_up[3].first()

    for h in range(heads):
        dkvs[:, :, h * HD : (h + 1) * HD] = (
            dka[h, :, one(oc)].reshape(nz, rows, HD).astype(b16)
        )
        dkvs[:, :, shard + h * HD : shard + (h + 1) * HD] = (
            dva[h, :, one(oc)].reshape(nz, rows, HD).astype(b16)
        )
    dkv_pair = links.start(dkvs, dkvr, to_core)
    rs_out.forward()
    tg[...] = matmul_tn(att[...], flat(ra[...])).astype(b16).reshape(tg.shape)
    attn_pair = links.start(tg.at[oc], tgr, to_core)
    red_up[1].second()
    red_up[0].third()

    def place(value):
        return jnp.concatenate([jnp.where(dp == k, value, 0.0) for k in range(n)], axis=1)

    sm[2:3] = place(jnp.concatenate([q_sum[h] for h in range(heads)], axis=1))
    v_sum = [
        jnp.sum(dva[h].reshape(2 * nz * rows, HD), axis=0, keepdims=True) for h in range(heads)
    ]
    sm[3:4] = place(jnp.concatenate(v_sum, axis=1))
    dkv_pair.wait_recv()
    for h in range(heads):
        for ref, offset in ((dka, 0), (dva, shard)):
            cols = slice(offset + h * HD, offset + (h + 1) * HD)
            mg[:, cols] = (
                ref[h, :, one(c)].reshape(nz * rows, HD) + flat(dkvr[:, :, cols]).astype(f32)
            ).astype(b16)
    mgr[...] = matmul_tn(flat(fa[...]), mg[...]).astype(b16).reshape(mgr.shape)
    mix_grad_pair = links.start(mgr.at[:, oc], mgx, to_core)
    red_up[2].second()
    red_up[1].third()
    for first, count in GROUPS:
        part = matmul_nt(mg[first * rows : (first + count) * rows], flat(mixc[...]))
        p4[first : first + count] = part.astype(b16).reshape(count, n, quarter, width)
    attn_pair.wait_recv()
    tz[...] = (tg[one(c)].reshape(tz.shape).astype(f32) + tgr[...].astype(f32)).astype(b16)
    red_attn.first()
    out_delta = aft[...] + rs_out.result() + vec(down_bias)
    od[...] = out_delta.astype(b16).reshape(od.shape)
    hop_o = scatter_z(od, oh1)
    oh1[one(z)] = od[one(z)]
    mix_grad_pair.wait_recv()
    ms[...] = (mgr[:, one(c)].reshape(ms.shape).astype(f32) + mgx[...].astype(f32)).astype(b16)
    hop_md = [links.start(ms.at[dps[k]], md.at[dp], to_dp[k]) for k in (1, 2, 3)]
    rs_first = [scatter(p4, r4, t4, first, count) for first, count in GROUPS]
    md[one(dp)] = ms[one(dp)]
    red_mix[0].first()
    red_up[3].second()
    red_up[2].third()
    for copy, item in zip(hop_md[:2], red_mix[1:3]):
        copy.wait_recv()
        item.first()
    rs_first[0].forward()
    hop_md[2].wait_recv()
    red_mix[3].first()
    red_attn.second()
    red_up[3].third()
    red_mix[0].second()
    red_attn.third()
    rs_first[1].forward()
    red_mix[1].second()
    red_mix[0].third()

    gain_sum, shift_sum = 0.0, 0.0
    for (first, count), item in zip(GROUPS, rs_first):
        at = slice(first * quarter, (first + count) * quarter)
        first_grad = item.result()
        hat = hat1[at]
        back = res[at] + norm_back(first_grad, hat, rstd1[at], vec(gain1))
        idl[first : first + count] = back.astype(b16).reshape(count, quarter, width)
        gain_sum += jnp.sum(first_grad * hat, axis=0, keepdims=True)
        shift_sum += jnp.sum(first_grad, axis=0, keepdims=True)
    hop_i = scatter_z(idl, ih1)
    ih1[one(z)] = idl[one(z)]
    sm[0:1] = gain_sum
    sm[1:2] = shift_sum
    sm1[one(dp)] = sm[...].reshape(1, *sm.shape)
    small_dp = [links.start(sm, sm1.at[dp], to_dp[k]) for k in peers]

    run(red_down, "fourth")
    red_mix[2].second()
    red_mix[1].third()
    run(red_up, "fourth")
    red_attn.fourth()
    arrived(small_dp)
    sm2[one(z)] = jnp.sum(sm1[...], axis=0, keepdims=True)
    small_z = [links.start(sm2.at[z], sm2.at[z], to_z[k]) for k in peers]
    red_mix[3].second()
    red_mix[2].third()
    arrived(hop_o)
    hop_o = scatter_dp(oh1, out_o)
    out_o[one(dp)] = oh1[one(dp)]
    red_mix[0].fourth()
    red_mix[3].third()
    red_mix[1].fourth()
    arrived(small_z)
    sm3[one(c)] = jnp.sum(sm2[...], axis=0, keepdims=True)
    small_core = links.start(sm3.at[c], sm3.at[c], to_core)
    arrived(hop_i)
    hop_i = scatter_dp(ih1, in_o)
    in_o[one(dp)] = ih1[one(dp)]
    run(red_down + red_up + [red_attn], "done")
    outgoing = [fetch(down_o, down_hbm), fetch(up_o, up_hbm), fetch(attn_o, attn_hbm)]
    red_mix[2].fourth()
    red_mix[3].fourth()
    small_core.wait_recv()
    small_o[...] = sm3[0] + sm3[1]
    arrived(hop_o)
    outgoing.append(fetch(out_o, out_hbm))
    run(red_mix, "done")
    outgoing.append(fetch(mix_o, mix_hbm))
    arrived(hop_i)
    outgoing.append(fetch(in_o, in_hbm))
    links.finish()
    for copy in outgoing:
        copy.wait()


def finish_kernel(*refs):
    f32 = jnp.float32
    ins, outs, mats, held, sems = refs[:9], refs[9:24], refs[24:30], refs[30:39], refs[39]
    out_ref, in_ref, mix_ref, attn_ref, up_ref, down_ref, small_ref, x_ref, cot_ref = held
    shard, width = mats[3].shape
    n = mix_ref.shape[0]
    fetches = {}
    for number in (5, 4, 2, 3, 0, 7, 1, 8, 6):
        fetches[number] = pltpu.make_async_copy(ins[number], held[number], sems.at[6 + number])
        fetches[number].start()
    copies = []

    def store(number, target):
        copy = pltpu.make_async_copy(mats[number], target, sems.at[number])
        copy.start()
        copies.append(copy)

    fetches[5].wait()
    mats[5][...] = flat(down_ref[...]).astype(f32)
    store(5, outs[13])
    fetches[4].wait()
    mats[4][...] = flat(up_ref[...]).astype(f32)
    store(4, outs[11])
    fetches[2].wait()
    for d in range(n):
        value = mix_ref[d].reshape(shard, 3 * shard).astype(f32)
        for part, place_at in ((0, 1), (1, 2), (2, 0)):
            start = place_at * width + d * shard
            mats[2][:, start : start + shard] = value[:, part * shard : (part + 1) * shard]
    store(2, outs[4])
    fetches[3].wait()
    mats[3][...] = flat(attn_ref[...]).astype(f32)
    store(3, outs[7])
    fetches[0].wait()
    fetches[7].wait()
    mats[0][...] = x_ref[...] + flat(out_ref[...]).astype(f32)
    store(0, outs[0])
    fetches[1].wait()
    fetches[8].wait()
    mats[1][...] = cot_ref[...] + flat(in_ref[...]).astype(f32)
    store(1, outs[1])
    fetches[6].wait()
    for number, row in ((2, 0), (3, 1), (5, 2), (6, 3), (8, 4), (9, 5), (10, 6), (14, 7)):
        outs[number][...] = small_ref[row : row + 1].reshape(width)
    for k in range(n):
        outs[12][k * width : (k + 1) * width] = small_ref[8 + k : 9 + k].reshape(width)
    for copy in copies:
        copy.wait()


def plane_body(
    block_input,
    out_cotangent,
    first_gain,
    first_shift,
    mix_weight,
    query_bias,
    value_bias,
    attn_weight,
    attn_bias,
    second_gain,
    second_shift,
    up_weight,
    up_bias,
    down_weight,
    down_bias,
):
    b16, f32 = jnp.bfloat16, jnp.float32
    n, nz = lax.axis_size("dp"), lax.axis_size("ctx") // 2
    rows, width = block_input.shape[1:]
    quarter = rows // n
    shard = width // n
    half = shard // 2
    hidden = up_weight.shape[1] // n
    heads = H // n
    tokens = nz * rows
    keys = 2 * tokens
    x_rows = block_input.reshape(rows, width)
    cot = out_cotangent.reshape(rows, width)
    vm = pltpu.VMEM
    stack = vm((n, quarter, width), b16)
    part = vm((nz, n, quarter, width), b16)
    part_recv = vm((n - 1, nz, quarter, width), b16)
    own = vm((nz * quarter, width), f32)
    results = [
        (n, quarter, width),
        (n, quarter, width),
        (n, 2, half, 3 * shard),
        (2, half, width),
        (2, half, n * hidden),
        (2, hidden // 2, width),
    ]
    scratch = [
        pltpu.SemaphoreType.DMA((SEMS,)),
        pltpu.SemaphoreType.DMA((SEMS,)),
        pltpu.SemaphoreType.DMA((24,)),
    ] + [vm(shape, b16) for shape in results] + [vm((width,), f32)] * 7 + [
        vm((n * hidden,), f32), vm((width,), f32),
        vm((rows, width), f32), vm((rows, width), f32),
        vm((half, 3 * width), b16), vm((shard, width), b16), vm((hidden, width), b16),
        stack, stack, stack, stack, stack, stack,
        vm((n, half, 3 * shard), b16), vm((n, 2, half, 3 * shard), b16),
        vm((n, nz, shard // nz, hidden), b16), part, part, part, part,
        vm((tokens, shard), b16), vm((nz, 2, rows, 2 * shard), b16),
        vm((heads, keys, HD), b16), vm((heads, keys, HD), b16),
        vm((tokens, shard), b16), vm((heads, tokens, 1), f32), vm((tokens, shard), b16),
        own, own, own, own,
        part, part, part, part, part_recv, part_recv, part_recv, part_recv,
        stack, stack, stack, stack,
        vm((tokens, hidden), f32), vm((tokens, hidden), b16), vm((tokens, hidden), b16),
        vm((2, hidden // 2, width), b16),
    ] + [vm((hidden // 2, width), b16)] * 4 + [
        vm((n, 2, half, hidden), b16), vm((n, half, hidden), b16), vm((n, half, hidden), b16),
    ] + [vm((half, n * hidden), b16)] * 3 + [
        vm((2, half, width), b16),
    ] + [vm((half, width), b16)] * 4 + [
        vm((heads, nz, 2, rows, HD), f32), vm((heads, nz, 2, rows, HD), f32),
        vm((nz, rows, 2 * shard), b16), vm((nz, rows, 2 * shard), b16),
        vm((tokens, 3 * shard), b16),
        vm((n, 2, half, 3 * shard), b16),
    ] + [vm((n, half, 3 * shard), b16)] * 5 + [
        stack, stack, stack, stack,
        vm((16, width), f32), vm((n, 16, width), f32), vm((nz, 16, width), f32),
        vm((2, 16, width), f32),
    ]
    hbm = pl.BlockSpec(memory_space=pl.ANY)
    near = pl.BlockSpec(memory_space=pltpu.VMEM)
    far = pl.BlockSpec(memory_space=pltpu.HBM)
    shapes = [(shape, b16) for shape in results] + [((16, width), f32)]
    pieces = pl.pallas_call(
        plane_kernel,
        out_shape=[jax.ShapeDtypeStruct(shape, dtype) for shape, dtype in shapes],
        in_specs=[far] * 15,
        out_specs=[hbm] * len(results) + [near],
        scratch_shapes=scratch,
        compiler_params=pltpu.CompilerParams(
            collective_id=0, has_side_effects=True, vmem_limit_bytes=60 * 1024 * 1024
        ),
        name="plane",
    )(
        x_rows, cot, first_gain, first_shift, mix_weight, query_bias, value_bias, attn_weight,
        attn_bias, second_gain, second_shift, up_weight, up_bias, down_weight, down_bias,
    )
    final = [
        (rows, width), (rows, width), (width,), (width,), (shard, 3 * width), (width,), (width,),
        (shard, width), (width,), (width,), (width,), (shard, n * hidden), (n * hidden,),
        (hidden, width), (width,),
    ]
    large = (0, 1, 4, 7, 11, 13)
    outs = pl.pallas_call(
        finish_kernel,
        out_shape=[jax.ShapeDtypeStruct(shape, f32) for shape in final],
        in_specs=[far] * 9,
        out_specs=[hbm if k in large else near for k in range(len(final))],
        scratch_shapes=[vm(final[k], f32) for k in large]
        + [vm(shape, dtype) for shape, dtype in shapes]
        + [vm((rows, width), f32), vm((rows, width), f32), pltpu.SemaphoreType.DMA((16,))],
        compiler_params=pltpu.CompilerParams(vmem_limit_bytes=60 * 1024 * 1024),
        name="finish",
    )(*pieces, x_rows, cot)
    return (
        outs[0].reshape(1, rows, width),
        outs[1].reshape(1, rows, width),
        *outs[2:],
    )


def fits(mesh):
    n, ctx = mesh.shape["dp"], mesh.shape["ctx"]
    return n == 4 and ctx == 8 and H % n == 0


def solution(mesh):
    placed = (
        P("dp", "ctx", None),
        P("dp", "ctx", None),
        P(),
        P(),
        P("dp", None),
        P(),
        P(),
        P("dp", None),
        P(),
        P(),
        P(),
        P("dp", None),
        P(),
        P("dp", None),
        P(),
    )
    return jax.shard_map(
        plane_body if fits(mesh) else body,
        mesh=mesh,
        in_specs=placed,
        out_specs=(
            P("dp", "ctx", None),
            P("dp", "ctx", None),
            P(),
            P(),
            P("dp", None),
            P(),
            P(),
            P("dp", None),
            P(),
            P(),
            P(),
            P("dp", None),
            P(),
            P("dp", None),
            P(),
        ),
        check_vma=False,
    )
```

```python
import functools
import math

import jax
import jax.numpy as jnp
from jax import lax
from jax.experimental import pallas as pl
from jax.experimental.pallas import tpu as pltpu
from jax.sharding import PartitionSpec as P

H = 12
HD = 64


EPS = 1e-05
GELU_C = math.sqrt(2.0 / math.pi)


def from_behind(value, axis, steps):
    count = lax.axis_size(axis)
    pairs = [(source, (source + steps) % count) for source in range(count)]
    return lax.ppermute(value, axis, pairs)


def layer_norm(x, gain, shift):
    centered = x - jnp.mean(x, axis=-1, keepdims=True)
    rstd = lax.rsqrt(jnp.mean(centered * centered, axis=-1, keepdims=True) + EPS)
    x_hat = centered * rstd
    return (x_hat, rstd, x_hat * gain + shift)


def norm_back(grad, x_hat, rstd, gain):
    g = grad * gain
    return rstd * (
        g
        - jnp.mean(g, axis=-1, keepdims=True)
        - x_hat * jnp.mean(g * x_hat, axis=-1, keepdims=True)
    )


def gelu_pair(u):
    inner = GELU_C * (u + 0.044715 * u * u * u)
    t = jnp.tanh(inner)
    value = 0.5 * u * (1.0 + t)
    slope = 0.5 * (1.0 + t) + 0.5 * u * (1.0 - t * t) * GELU_C * (1.0 + 3.0 * 0.044715 * u * u)
    return (value, slope)


def matmul(a, b):
    return jnp.dot(a, b, preferred_element_type=jnp.float32)


def matmul_tn(a, b):
    return lax.dot_general(a, b, (((0,), (0,)), ((), ())), preferred_element_type=jnp.float32)


def matmul_nt(a, b):
    return lax.dot_general(a, b, (((1,), (1,)), ((), ())), preferred_element_type=jnp.float32)


def body(
    block_input,
    out_cotangent,
    first_gain,
    first_shift,
    mix_weight,
    query_bias,
    value_bias,
    attn_weight,
    attn_bias,
    second_gain,
    second_shift,
    up_weight,
    up_bias,
    down_weight,
    down_bias,
):
    rows = block_input.shape[1]
    width = block_input.shape[2]
    scale = HD ** (-0.5)
    x_rows = block_input.reshape(rows, width)
    cot = out_cotangent.reshape(rows, width)
    mix_full, attn_full, up_full, down_full = (
        lax.all_gather(mix_weight, "dp", axis=0, tiled=True),
        lax.all_gather(attn_weight, "dp", axis=0, tiled=True),
        lax.all_gather(up_weight, "dp", axis=0, tiled=True),
        lax.all_gather(down_weight, "dp", axis=0, tiled=True),
    )
    first_hat, first_rstd, first_out = layer_norm(x_rows, first_gain, first_shift)
    first_in = first_out.astype(jnp.bfloat16)
    mixed = matmul(first_in, mix_full)
    queries = (mixed[:, :width] + query_bias).astype(jnp.bfloat16)
    keys = mixed[:, width : 2 * width].astype(jnp.bfloat16)
    values = (mixed[:, 2 * width :] + value_bias).astype(jnp.bfloat16)
    q3 = queries.reshape(rows, H, HD)
    me = lax.axis_index("ctx")
    cycle_size = lax.axis_size("ctx")
    q_pos = me * rows + jnp.arange(rows)
    q_last = me * rows + rows - 1
    start_state = (
        jnp.full((H, rows), -1e30, jnp.float32),
        jnp.zeros((H, rows), jnp.float32),
        jnp.zeros((H, rows, HD), jnp.float32),
    )
    carry = start_state
    key_piece = lax.all_gather(keys, "ctx", axis=0, tiled=True)
    value_piece = lax.all_gather(values, "ctx", axis=0, tiled=True)
    count = key_piece.shape[0]
    kblock = math.gcd(count, 512)
    nblocks = count // kblock
    key_blocks = key_piece.reshape(nblocks, kblock, H, HD)
    value_blocks = value_piece.reshape(nblocks, kblock, H, HD)
    offsets = jnp.arange(nblocks) * kblock

    def one_block(state, item):
        key_blk, value_blk, offset = item

        def compute(state_in):
            run_max, run_total, run_acc = state_in
            key_pos = offset + jnp.arange(kblock)
            allowed = (key_pos[None, :] <= q_pos[:, None])[None]
            scores = (
                jnp.einsum("qhd,khd->hqk", q3, key_blk, preferred_element_type=jnp.float32) * scale
            )
            scores = jnp.where(allowed, scores, -1e30)
            new_max = jnp.maximum(run_max, jnp.max(scores, axis=-1))
            expo = jnp.where(allowed, jnp.exp(scores - new_max[..., None]), 0.0)
            factor = jnp.exp(run_max - new_max)
            new_total = run_total * factor + jnp.sum(expo, axis=-1)
            new_acc = run_acc * factor[..., None] + jnp.einsum(
                "hqk,khd->hqd", expo, value_blk.astype(jnp.float32), precision=lax.Precision.HIGHEST
            )
            return (new_max, new_total, new_acc)

        def keep_state(state_in):
            return state_in

        return (lax.cond(offset <= q_last, compute, keep_state, state), None)

    carry, unused = lax.scan(one_block, carry, (key_blocks, value_blocks, offsets))
    run_max, run_total, run_acc = carry
    attended = (
        (run_acc / run_total[..., None])
        .transpose(1, 0, 2)
        .reshape(rows, width)
        .astype(jnp.bfloat16)
    )
    lse = run_max + jnp.log(run_total)
    after_attn = x_rows + matmul(attended, attn_full) + attn_bias
    second_hat, second_rstd, second_out = layer_norm(after_attn, second_gain, second_shift)
    second_in = second_out.astype(jnp.bfloat16)
    pre_act = matmul(second_in, up_full) + up_bias
    act_value, act_slope = gelu_pair(pre_act)
    activ = act_value.astype(jnp.bfloat16)
    block_output = after_attn + matmul(activ, down_full) + down_bias
    mix_back, attn_back, up_back, down_back = (
        lax.all_gather(mix_weight, "dp", axis=0, tiled=True),
        lax.all_gather(attn_weight, "dp", axis=0, tiled=True),
        lax.all_gather(up_weight, "dp", axis=0, tiled=True),
        lax.all_gather(down_weight, "dp", axis=0, tiled=True),
    )
    cot_b = cot.astype(jnp.bfloat16)
    down_weight_grad = matmul_tn(activ, cot_b)
    down_bias_grad = jnp.sum(cot, axis=0)
    pre_grad = matmul_nt(cot_b, down_back) * act_slope
    pre_grad_b = pre_grad.astype(jnp.bfloat16)
    up_weight_grad = matmul_tn(second_in, pre_grad_b)
    up_bias_grad = jnp.sum(pre_grad, axis=0)
    second_grad = matmul_nt(pre_grad_b, up_back)
    second_gain_grad = jnp.sum(second_grad * second_hat, axis=0)
    second_shift_grad = jnp.sum(second_grad, axis=0)
    resid_grad = cot + norm_back(second_grad, second_hat, second_rstd, second_gain)
    resid_b = resid_grad.astype(jnp.bfloat16)
    attn_weight_grad = matmul_tn(attended, resid_b)
    attn_bias_grad = jnp.sum(resid_grad, axis=0)
    attended_grad = matmul_nt(resid_b, attn_back).astype(jnp.bfloat16)
    grad3 = attended_grad.reshape(rows, H, HD)
    delta = jnp.sum(
        grad3.astype(jnp.float32) * attended.astype(jnp.float32).reshape(rows, H, HD), axis=-1
    ).T

    def block_grads(key_blk, value_blk, key_start):
        count = key_blk.shape[0]
        key3 = key_blk.reshape(count, H, HD)
        value3 = value_blk.reshape(count, H, HD)
        key_pos = key_start + jnp.arange(count)
        allowed = (key_pos[None, :] <= q_pos[:, None])[None]
        scores = jnp.einsum("qhd,khd->hqk", q3, key3, preferred_element_type=jnp.float32) * scale
        probs = jnp.where(allowed, jnp.exp(scores - lse[..., None]), 0.0)
        dprob = jnp.einsum("qhd,khd->hqk", grad3, value3, preferred_element_type=jnp.float32)
        dscore = probs * (dprob - delta[..., None])
        probs_b = probs.astype(jnp.bfloat16)
        dscore_b = dscore.astype(jnp.bfloat16)
        value_add = jnp.einsum("hqk,qhd->khd", probs_b, grad3, preferred_element_type=jnp.float32)
        key_add = (
            jnp.einsum("hqk,qhd->khd", dscore_b, q3, preferred_element_type=jnp.float32) * scale
        )
        query_add = (
            jnp.einsum("hqk,khd->qhd", dscore_b, key3, preferred_element_type=jnp.float32) * scale
        )
        return (
            query_add.reshape(rows, width),
            key_add.reshape(count, width),
            value_add.reshape(count, width),
        )

    def skip_grads(key_blk, value_blk, key_start):
        count = key_blk.shape[0]
        empty = jnp.zeros((count, width), jnp.float32)
        return (jnp.zeros((rows, width), jnp.float32), empty, empty)

    zeros = jnp.zeros((rows, width), jnp.float32)

    def pass_grads(key_acc, value_acc):
        return (
            from_behind(key_acc.astype(jnp.bfloat16), "ctx", -1).astype(key_acc.dtype),
            from_behind(value_acc.astype(jnp.bfloat16), "ctx", -1).astype(value_acc.dtype),
        )

    def cycle_turn(step, state):
        key_blk, value_blk, key_acc, value_acc, query_acc = state
        owner = (me + step) % cycle_size
        query_add, key_add, value_add = lax.cond(
            owner <= me, block_grads, skip_grads, key_blk, value_blk, owner * rows
        )
        key_blk, value_blk = from_behind((key_blk, value_blk), "ctx", -1)
        key_acc, value_acc = pass_grads(key_acc + key_add, value_acc + value_add)
        return (key_blk, value_blk, key_acc, value_acc, query_acc + query_add)

    key_blk, value_blk, key_acc, value_acc, query_acc = lax.fori_loop(
        0, cycle_size - 1, cycle_turn, (keys, values, zeros, zeros, zeros)
    )
    last_owner = (me + cycle_size - 1) % cycle_size
    query_add, key_add, value_add = lax.cond(
        last_owner <= me, block_grads, skip_grads, key_blk, value_blk, last_owner * rows
    )
    key_grad, value_grad = pass_grads(key_acc + key_add, value_acc + value_add)
    query_grad = query_acc + query_add
    query_bias_grad = jnp.sum(query_grad, axis=0)
    value_bias_grad = jnp.sum(value_grad, axis=0)
    mixed_grad = jnp.concatenate([query_grad, key_grad, value_grad], axis=1).astype(jnp.bfloat16)
    mix_weight_grad = matmul_tn(first_in, mixed_grad)
    first_grad = matmul_nt(mixed_grad, mix_back)
    first_gain_grad = jnp.sum(first_grad * first_hat, axis=0)
    first_shift_grad = jnp.sum(first_grad, axis=0)
    input_grad = resid_grad + norm_back(first_grad, first_hat, first_rstd, first_gain)
    local_mats = (mix_weight_grad, attn_weight_grad, up_weight_grad, down_weight_grad)
    shard_sums = (
        lax.psum_scatter(
            local_mats[0].astype(jnp.bfloat16), "dp", scatter_dimension=0, tiled=True
        ).astype(jnp.float32),
        lax.psum_scatter(
            local_mats[1].astype(jnp.bfloat16), "dp", scatter_dimension=0, tiled=True
        ).astype(jnp.float32),
        lax.psum_scatter(
            local_mats[2].astype(jnp.bfloat16), "dp", scatter_dimension=0, tiled=True
        ).astype(jnp.float32),
        lax.psum_scatter(
            local_mats[3].astype(jnp.bfloat16), "dp", scatter_dimension=0, tiled=True
        ).astype(jnp.float32),
    )
    mats = (
        lax.psum(shard_sums[0].astype(jnp.bfloat16), "ctx").astype(jnp.float32),
        lax.psum(shard_sums[1].astype(jnp.bfloat16), "ctx").astype(jnp.float32),
        lax.psum(shard_sums[2].astype(jnp.bfloat16), "ctx").astype(jnp.float32),
        lax.psum(shard_sums[3].astype(jnp.bfloat16), "ctx").astype(jnp.float32),
    )
    smalls = lax.psum(
        (
            first_gain_grad,
            first_shift_grad,
            query_bias_grad,
            value_bias_grad,
            attn_bias_grad,
            second_gain_grad,
            second_shift_grad,
            up_bias_grad,
            down_bias_grad,
        ),
        ("dp", "ctx"),
    )
    return (
        block_output.reshape(1, rows, width),
        input_grad.reshape(1, rows, width),
        smalls[0],
        smalls[1],
        mats[0],
        smalls[2],
        smalls[3],
        mats[1],
        smalls[4],
        smalls[5],
        smalls[6],
        mats[2],
        smalls[7],
        mats[3],
        smalls[8],
    )


def flip(index, mask):
    bit = 1
    while bit <= mask:
        if mask & bit:
            index = index + bit - 2 * bit * ((index // bit) % 2)
        bit *= 2
    return index


MESH = pl.DeviceIdType.MESH
GROUPS = ((2, 2), (0, 2))
SEMS = 224


class Links:
    def __init__(self, send, recv):
        self.send, self.recv, self.count, self.open = send, recv, 0, []

    def make(self, source, target, device):
        number = self.count
        self.count += 1
        return pltpu.make_async_remote_copy(
            src_ref=source,
            dst_ref=target,
            send_sem=self.send.at[number],
            recv_sem=self.recv.at[number],
            device_id=device,
            device_id_type=MESH,
        )

    def start(self, source, target, device):
        copy = self.make(source, target, device)
        copy.start()
        self.open.append(copy)
        return copy

    def finish(self):
        for copy in self.open:
            copy.wait_send()


def arrived(copies):
    for copy in copies:
        copy.wait_recv()


def flat(value):
    return value.reshape(-1, value.shape[-1])


def plane_kernel(
    x_in, cot_in, gain1_in, shift1_in, mix_w, q_bias_in, v_bias_in, attn_w, attn_bias_in, gain2_in,
    shift2_in, up_w, up_bias_in, down_w, down_bias_in,
    out_hbm, in_hbm, mix_hbm, attn_hbm, up_hbm, down_hbm, small_o,
    send_sem, recv_sem, local_sem,
    out_o, in_o, mix_o, attn_o, up_o, down_o,
    gain1, shift1, q_bias, v_bias, attn_bias, gain2, shift2, up_bias, down_bias,
    xv, cv, mw, aw, dw,
    xs, xh1, xh2, cs, ch1, ch2,
    mst, mixc, upc, fa, ca, sa, ra,
    qs, kv, kh, vh, att, lse, agr,
    hat1, aft, hat2, res,
    p1, p2, p3, p4, r1, r2, r3, r4, t1, t2, t3, t4,
    dact, act, pg,
    dg, dgr, dz, dz1, dz2,
    ug, ugr, us, ud, uz1, uz2,
    tg, tgr, tz, tz1, tz2,
    dka, dva, dkvs, dkvr, mg,
    mgr, mgx, ms, md, mz1, mz2,
    od, oh1, idl, ih1,
    sm, sm1, sm2, sm3,
):
    b16, f32 = jnp.bfloat16, jnp.float32
    n, quarter, width = xs.shape
    nz = xh2.shape[0]
    rows = n * quarter
    half, hidden = mixc.shape[2], upc.shape[3]
    shard = 2 * half
    heads = kh.shape[0]
    dp, ctx = lax.axis_index("dp"), lax.axis_index("ctx")
    z, c = ctx // 2, ctx % 2
    oc = 1 - c
    dps = [flip(dp, k) for k in range(n)]
    zs = [flip(z, k) for k in range(nz)]
    to_dp = [(dps[k], ctx) for k in range(n)]
    to_z = [(dp, 2 * zs[k] + c) for k in range(nz)]
    to_core = (dp, 2 * z + oc)
    inner = (z + 1) // 2 % 2 == 1
    outer = (z + 1) // 2 % 2 == 0
    peers = (3, 1, 2)
    links = Links(send_sem, recv_sem)
    one = lambda index: pl.ds(index, 1)

    locals_ = []

    def fetch(source, target):
        copy = pltpu.make_async_copy(source, target, local_sem.at[len(locals_)])
        copy.start()
        locals_.append(copy)
        return copy

    my_half = pl.ds(pl.multiple_of(c * half, 16), half)
    get_x = fetch(x_in, xv)
    get_mix = fetch(mix_w.at[my_half], mw)
    get_cot = fetch(cot_in, cv)
    get_vectors = [
        fetch(source, target)
        for source, target in (
            (gain1_in, gain1), (shift1_in, shift1), (q_bias_in, q_bias), (v_bias_in, v_bias),
            (attn_bias_in, attn_bias), (gain2_in, gain2), (shift2_in, shift2),
            (up_bias_in, up_bias), (down_bias_in, down_bias),
        )
    ]
    get_attn = fetch(attn_w, aw)
    get_down = fetch(down_w, dw)
    columns = lambda index: pl.ds(pl.multiple_of(index * hidden, 128), hidden)
    strip = shard // nz
    up_rows = pl.ds(pl.multiple_of(z * strip, 16), strip)
    up_half = lambda index: pl.ds(pl.multiple_of(index * (hidden // 2), 128), hidden // 2)
    up_piece = lambda index: up_w.at[
        up_rows, pl.ds(pl.multiple_of(index * hidden + c * (hidden // 2), 128), hidden // 2)
    ]
    get_up = fetch(up_piece(dp), upc.at[dp, z, :, up_half(c)])

    barrier = pltpu.get_barrier_semaphore()
    everyone = to_dp[1:] + to_z[1:] + [to_core]
    for device in everyone:
        pl.semaphore_signal(barrier, inc=1, device_id=device, device_id_type=MESH)

    get_x.wait()
    xs[...] = xv[...].astype(b16).reshape(n, quarter, width)
    pl.semaphore_wait(barrier, len(everyone))

    def scatter_dp(source, target):
        return [links.start(source.at[dps[k]], target.at[dp], to_dp[k]) for k in peers]

    def scatter_z(source, target):
        return [links.start(source.at[zs[k]], target.at[z], to_z[k]) for k in peers]

    class Gather:
        def __init__(self, ref, first, count):
            self.ref, self.first, self.mid = ref, first, first + count // 2
            part = ref.at[pl.ds(first, count), dp]
            self.near = [links.start(part, part, to_dp[k]) for k in (1, 2)]

        def forward(self):
            arrived(self.near)
            self.far = []
            for begin, origin, target in ((self.first, 1, 2), (self.mid, 2, 1)):
                part = self.ref.at[pl.ds(begin, self.mid - self.first), dps[origin]]
                self.far.append(links.start(part, part, to_dp[target]))

        def wait(self):
            arrived(self.far)

    class Scatter:
        def __init__(self, ref, recv, stage, first, count):
            self.ref, self.recv, self.stage = ref, recv, stage
            self.first, self.count, step = first, count, count // 2
            self.ways = ((first, step, 1, 2), (first + step, step, 2, 1))
            self.pass_on, self.mine = [], []
            for begin, size, near, _ in self.ways:
                for role, slot, copies in ((1, 3, self.pass_on), (0, near, self.mine)):
                    source = ref.at[pl.ds(begin, size), dps[slot]]
                    target = recv.at[role, pl.ds(begin, size)]
                    copies.append(links.start(source, target, to_dp[near]))

        def forward(self):
            self.last = []
            for (begin, size, _, beyond), copy in zip(self.ways, self.pass_on):
                copy.wait_recv()
                at = pl.ds(begin, size)
                value = self.ref[at, one(dps[beyond])].astype(f32).reshape(size, quarter, width)
                value = value + self.recv[1, at].astype(f32)
                self.stage[at] = value.astype(b16)
                self.last.append(
                    links.start(self.stage.at[at], self.recv.at[2, at], to_dp[beyond])
                )

        def result(self):
            arrived(self.mine)
            arrived(self.last)
            at = slice(self.first, self.first + self.count)
            total = self.ref[at, one(dp)].astype(f32).reshape(self.count * quarter, width)
            return total + flat(self.recv[0, at].astype(f32)) + flat(self.recv[2, at].astype(f32))

    class DirectGather:
        def __init__(self, ref, first, count):
            part = ref.at[pl.ds(first, count), dp]
            self.all = [links.start(part, part, to_dp[k]) for k in peers]

        def forward(self):
            pass

        def wait(self):
            arrived(self.all)

    class DirectScatter:
        def __init__(self, ref, recv, stage, first, count):
            self.ref, self.recv, self.first, self.count = ref, recv, first, count
            at = pl.ds(first, count)
            self.all = [
                links.start(ref.at[at, dps[k]], recv.at[k - 1, at], to_dp[k]) for k in peers
            ]

        def forward(self):
            pass

        def result(self):
            arrived(self.all)
            at = slice(self.first, self.first + self.count)
            total = self.ref[at, one(dp)].astype(f32).reshape(self.count * quarter, width)
            for k in range(1, n):
                total += flat(self.recv[k - 1, at].astype(f32))
            return total

    def gather(*spec):
        return (Gather if spec[1] else DirectGather)(*spec)

    def scatter(*spec):
        return (Scatter if spec[3] else DirectScatter)(*spec)

    def run(items, step):
        for item in items:
            getattr(item, step)()

    hop_x = scatter_dp(xs, xh1)
    xh1[one(dp)] = xs[one(dp)]
    get_mix.wait()
    mv = mw[...]
    for d in range(n):
        mst[d] = jnp.concatenate(
            [mv[:, part * width + d * shard : part * width + (d + 1) * shard] for part in (1, 2, 0)],
            axis=1,
        )
    mixc[one(dp), one(c)] = mst[one(dp)].reshape(1, 1, half, 3 * shard)
    for copy in [get_cot] + get_vectors:
        copy.wait()
    cot = cv[...]
    cs[...] = cot.astype(b16).reshape(n, quarter, width)
    ch1[one(dp)] = cs[one(dp)]
    arrived(hop_x)
    hop_x = scatter_z(xh1, xh2)
    hop_mix = [links.start(mst.at[dps[k]], mixc.at[dp, c], to_dp[k]) for k in peers]
    hop_c = scatter_dp(cs, ch1)
    xh2[one(z)] = xh1[one(z)]
    sm[...] = jnp.zeros(sm.shape, f32)
    sm[7:8] = jnp.sum(cot, axis=0, keepdims=True)

    vec = lambda ref: ref[...].reshape(1, -1)

    def pick(ref, size):
        value = vec(ref)
        total = jnp.zeros((1, size), f32)
        for k in range(n):
            total = jnp.where(dp == k, value[:, k * size : (k + 1) * size], total)
        return total

    arrived(hop_x)
    x_hat, rstd1, first = layer_norm(flat(xh2[...]).astype(f32), vec(gain1), vec(shift1))
    hat1[...] = x_hat
    fa[:, one(dp)] = first.astype(b16).reshape(nz, 1, quarter, width)
    ag_first = [Gather(fa, first, count) for first, count in GROUPS]
    kv_bias = jnp.concatenate([jnp.zeros((1, shard), f32), pick(v_bias, shard)], axis=1)
    own_q_bias = pick(q_bias, shard)
    arrived(hop_mix)
    mix_pair = links.start(mixc.at[:, c], mixc.at[:, c], to_core)
    arrived(hop_c)
    hop_c = scatter_z(ch1, ch2)
    ch2[one(z)] = ch1[one(z)]

    run(ag_first, "forward")
    run(ag_first, "wait")
    hop_up = [
        links.start(up_piece(dps[k]), upc.at[dp, z, :, up_half(c)], to_dp[k]) for k in peers
    ]
    arrived(hop_c)
    ca[:, one(dp)] = ch2[...].reshape(nz, 1, quarter, width)
    ag_cot = Gather(ca, 0, nz)
    mix_pair.wait_recv()
    first_all = flat(fa[...])
    mixed = matmul(first_all, flat(mixc[:, :, :, : 2 * shard])) + kv_bias
    kv[:, one(c)] = mixed.astype(b16).reshape(nz, 1, rows, 2 * shard)
    kv_pair = links.start(kv.at[:, c], kv.at[:, c], to_core)
    scale = HD ** (-0.5)
    queries = matmul(first_all, flat(mixc[:, :, :, 2 * shard :])) + own_q_bias
    qs[...] = (queries * scale).astype(b16)
    arrived(hop_up)
    get_up.wait()
    up_strip = upc.at[:, z, :, up_half(c)]
    hop_up = [links.start(up_strip, up_strip, to_z[k]) for k in peers]
    kv_pair.wait_recv()
    for h in range(heads):
        kh[h] = flat(kv[:, :, :, h * HD : (h + 1) * HD])
        vh[h] = flat(kv[:, :, :, shard + h * HD : shard + (h + 1) * HD])

    last = 2 * rows
    allowed = (
        lax.broadcasted_iota(jnp.int32, (rows, last), 1)
        <= lax.broadcasted_iota(jnp.int32, (rows, last), 0) + c * rows
    )

    def spans(j):
        return ([(0, j * last)] if j else []) + [(j * last, (j + 1) * last)]

    def attend(j):
        at = slice(j * rows, (j + 1) * rows)
        for h in range(heads):
            q = qs[at, h * HD : (h + 1) * HD]
            scores = []
            for a, b in spans(j):
                s = matmul_nt(q, kh[h, a:b])
                scores.append(jnp.where(allowed, s, -1e30) if b == (j + 1) * last else s)
            top = functools.reduce(
                jnp.maximum, [jnp.max(s, axis=-1, keepdims=True) for s in scores]
            )
            total, result = 0.0, 0.0
            for s, (a, b) in zip(scores, spans(j)):
                w = jnp.exp(s - top)
                total = total + jnp.sum(w, axis=-1, keepdims=True)
                result = result + matmul(w.astype(b16), vh[h, a:b])
            att[at, h * HD : (h + 1) * HD] = (result / total).astype(b16)
            lse[h, at] = top + jnp.log(total)

    get_attn.wait()
    ag_cot.forward()
    rs_attn = []
    for first, count in GROUPS:
        for j in range(first + count - 1, first - 1, -1):
            attend(j)
            if rs_attn and j == 1:
                rs_attn[0].forward()
        part = matmul(att[first * rows : (first + count) * rows], aw[...])
        p1[first : first + count] = part.astype(b16).reshape(count, n, quarter, width)
        rs_attn.append(scatter(p1, r1, t1, first, count))

    arrived(hop_up)
    up_pair = links.start(upc.at[:, :, :, up_half(c)], upc.at[:, :, :, up_half(c)], to_core)
    get_down.wait()
    ag_cot.wait()
    for first, count in GROUPS:
        if first == GROUPS[1][0]:
            rs_attn[1].forward()
        dact[first * rows : (first + count) * rows] = matmul_nt(
            flat(ca[first : first + count]), dw[...]
        )

    ag_second, rstd2 = [], []
    for (first, count), item in zip(GROUPS, rs_attn):
        at = slice(first * quarter, (first + count) * quarter)
        after = item.result() + vec(attn_bias)
        aft[at] = after
        after = after + flat(xh2[first : first + count]).astype(f32)
        hat, rstd, second = layer_norm(after, vec(gain2), vec(shift2))
        hat2[at] = hat
        rstd2.append(rstd)
        sa[first : first + count, one(dp)] = second.astype(b16).reshape(count, 1, quarter, width)
        ag_second.append(Gather(sa, first, count))

    run(ag_second, "forward")
    up_pair.wait_recv()
    own_up_bias = up_bias[columns(dp)].reshape(1, hidden)
    up_sum = jnp.zeros((1, hidden), f32)
    rs_second = []
    for (first, count), item in zip(GROUPS, ag_second):
        item.wait()
        at = slice(first * rows, (first + count) * rows)
        pre_act = matmul(flat(sa[first : first + count]), flat(upc[...])) + own_up_bias
        value, slope = gelu_pair(pre_act)
        act[at] = value.astype(b16)
        if rs_second:
            rs_second[0].forward()
        pre_grad = dact[at] * slope
        up_sum += jnp.sum(pre_grad, axis=0, keepdims=True)
        pg[at] = pre_grad.astype(b16)
        part = matmul_nt(pg[at], flat(upc[...]))
        p2[first : first + count] = part.astype(b16).reshape(count, n, quarter, width)
        rs_second.append(scatter(p2, r2, t2, first, count))
    for k in range(n):
        sm[8 + k : 9 + k] = jnp.where(dp == k, up_sum, 0.0)

    dg[...] = matmul_tn(act[...], flat(ca[...])).astype(b16).reshape(dg.shape)
    down_pair = links.start(dg.at[oc], dgr, to_core)
    rs_second[1].forward()
    ug[...] = matmul_tn(flat(sa[...]), pg[...]).astype(b16).reshape(ug.shape)
    up_grad_pair = links.start(ug.at[:, oc], ugr, to_core)

    class Reduce:
        def __init__(self, mine, sum1, sum2, total):
            self.mine, self.sum1, self.sum2, self.total = mine, sum1, sum2, total
            self.one = links.make(mine, sum1, to_z[1])
            self.two = links.make(mine, sum2, to_z[3])
            self.three = links.make(total, total, to_z[1])
            self.pair = links.make(total, total, to_core)

        def first(self):
            pl.when(outer)(lambda: self.one.start())

        def second(self):
            @pl.when(inner)
            def _():
                self.one.wait_recv()
                value = self.mine[...].astype(f32) + self.sum1[...].astype(f32)
                self.mine[...] = value.astype(b16)
                self.two.start()

        def third(self):
            @pl.when(inner)
            def _():
                self.two.wait_recv()
                value = self.mine[...].astype(f32) + self.sum2[...].astype(f32)
                self.total[...] = value.astype(b16).reshape(self.total.shape)
                self.three.start()
                self.pair.start()

        def fourth(self):
            @pl.when(outer)
            def _():
                self.three.wait_recv()
                self.pair.start()

        def done(self):
            self.pair.wait()

            @pl.when(outer)
            def _():
                self.one.wait_send()

            @pl.when(inner)
            def _():
                self.two.wait_send()
                self.three.wait_send()

    down_pair.wait_recv()
    dz[...] = (dg[one(c)].reshape(dz.shape).astype(f32) + dgr[...].astype(f32)).astype(b16)
    size = dz.shape[0] // n
    red_down = [
        Reduce(dz.at[part], dz1.at[part], dz2.at[part], down_o.at[c, part])
        for part in [pl.ds(k * size, size) for k in range(n)]
    ]
    run(red_down, "first")
    up_grad_pair.wait_recv()
    us[...] = (ug[:, one(c)].reshape(us.shape).astype(f32) + ugr[...].astype(f32)).astype(b16)
    ud[:, columns(dp)] = us[one(dp)].reshape(half, hidden)
    red_up = [
        Reduce(ud.at[:, part], uz1.at[:, part], uz2.at[:, part], up_o.at[c, :, part])
        for part in [columns(dps[k]) for k in range(n)]
    ]
    red_up[0].first()

    ag_resid = []
    gain_sum, shift_sum, bias_sum = 0.0, 0.0, 0.0
    for (first, count), item, rstd in zip(GROUPS, rs_second, rstd2):
        at = slice(first * quarter, (first + count) * quarter)
        second_grad = item.result()
        hat = hat2[at]
        back = norm_back(second_grad, hat, rstd, vec(gain2))
        res[at] = back
        resid = flat(ch2[first : first + count]).astype(f32) + back
        ra[first : first + count, one(dp)] = resid.astype(b16).reshape(count, 1, quarter, width)
        ag_resid.append(Gather(ra, first, count))
        gain_sum += jnp.sum(second_grad * hat, axis=0, keepdims=True)
        shift_sum += jnp.sum(second_grad, axis=0, keepdims=True)
        bias_sum += jnp.sum(resid, axis=0, keepdims=True)
    sm[4:5] = bias_sum
    sm[5:6] = gain_sum
    sm[6:7] = shift_sum

    red_down[0].second()
    run(ag_resid, "forward")
    hop_ud = [links.start(us.at[dps[k]], ud.at[:, columns(dp)], to_dp[k]) for k in (1, 2, 3)]
    red_down[1].second()
    part = matmul(act[...], dw[...])
    p3[...] = part.astype(b16).reshape(p3.shape)
    rs_out = DirectScatter(p3, r3, t3, 0, nz)
    red_down[0].third()

    def attend_back(j, fresh):
        at = slice(j * rows, (j + 1) * rows)
        for h in range(heads):
            cols = slice(h * HD, (h + 1) * HD)
            q, grad = qs[at, cols], agr[at, cols]
            delta = jnp.sum(grad.astype(f32) * att[at, cols].astype(f32), axis=-1, keepdims=True)
            base, total = lse[h, at], 0.0
            for a, b in spans(j):
                keys = kh[h, a:b]
                p = jnp.exp(matmul_nt(q, keys) - base)
                if b == (j + 1) * last:
                    p = jnp.where(allowed, p, 0.0)
                ds = (p * (matmul_nt(grad, vh[h, a:b]) - delta)).astype(b16)
                total = total + matmul(ds, keys)
                shape = ((b - a) // last, 2, rows, HD)
                dk = matmul_tn(ds, q).reshape(shape)
                dv = matmul_tn(p.astype(b16), grad).reshape(shape)
                blocks = slice(a // last, b // last)
                if fresh:
                    dka[h, blocks], dva[h, blocks] = dk, dv
                else:
                    dka[h, blocks] += dk
                    dva[h, blocks] += dv
            total = total * scale
            q_sum[h] = q_sum.get(h, 0.0) + jnp.sum(total, axis=0, keepdims=True)
            mg[at, 2 * shard + h * HD : 2 * shard + (h + 1) * HD] = total.astype(b16)

    q_sum = {}
    red_attn = Reduce(tz, tz1, tz2, attn_o.at[c])
    red_mix = [
        Reduce(md.at[dps[k]], mz1.at[k], mz2.at[k], mix_o.at[dps[k], c]) for k in range(n)
    ]

    def weights_of(first, count):
        return matmul_nt(flat(ra[first : first + count]), aw[...]).astype(b16)

    (first, count), (first2, count2) = GROUPS
    ag_resid[0].wait()
    agr[first * rows : (first + count) * rows] = weights_of(first, count)
    attend_back(3, True)
    red_down[2].second()
    red_down[1].third()
    attend_back(2, False)
    red_down[3].second()
    red_down[2].third()
    ag_resid[1].wait()
    agr[first2 * rows : (first2 + count2) * rows] = weights_of(first2, count2)
    attend_back(1, False)
    for copy, item in zip(hop_ud[:2], red_up[1:3]):
        copy.wait_recv()
        item.first()
    red_up[0].second()
    red_down[3].third()
    attend_back(0, False)
    hop_ud[2].wait_recv()
    red_up[3].first()

    for h in range(heads):
        dkvs[:, :, h * HD : (h + 1) * HD] = (
            dka[h, :, one(oc)].reshape(nz, rows, HD).astype(b16)
        )
        dkvs[:, :, shard + h * HD : shard + (h + 1) * HD] = (
            dva[h, :, one(oc)].reshape(nz, rows, HD).astype(b16)
        )
    dkv_pair = links.start(dkvs, dkvr, to_core)
    rs_out.forward()
    tg[...] = matmul_tn(att[...], flat(ra[...])).astype(b16).reshape(tg.shape)
    attn_pair = links.start(tg.at[oc], tgr, to_core)
    red_up[1].second()
    red_up[0].third()

    def place(value):
        return jnp.concatenate([jnp.where(dp == k, value, 0.0) for k in range(n)], axis=1)

    sm[2:3] = place(jnp.concatenate([q_sum[h] for h in range(heads)], axis=1))
    v_sum = [
        jnp.sum(dva[h].reshape(2 * nz * rows, HD), axis=0, keepdims=True) for h in range(heads)
    ]
    sm[3:4] = place(jnp.concatenate(v_sum, axis=1))
    dkv_pair.wait_recv()
    for h in range(heads):
        for ref, offset in ((dka, 0), (dva, shard)):
            cols = slice(offset + h * HD, offset + (h + 1) * HD)
            mg[:, cols] = (
                ref[h, :, one(c)].reshape(nz * rows, HD) + flat(dkvr[:, :, cols]).astype(f32)
            ).astype(b16)
    mgr[...] = matmul_tn(flat(fa[...]), mg[...]).astype(b16).reshape(mgr.shape)
    mix_grad_pair = links.start(mgr.at[:, oc], mgx, to_core)
    red_up[2].second()
    red_up[1].third()
    for first, count in GROUPS:
        part = matmul_nt(mg[first * rows : (first + count) * rows], flat(mixc[...]))
        p4[first : first + count] = part.astype(b16).reshape(count, n, quarter, width)
    attn_pair.wait_recv()
    tz[...] = (tg[one(c)].reshape(tz.shape).astype(f32) + tgr[...].astype(f32)).astype(b16)
    red_attn.first()
    out_delta = aft[...] + rs_out.result() + vec(down_bias)
    od[...] = out_delta.astype(b16).reshape(od.shape)
    hop_o = scatter_z(od, oh1)
    oh1[one(z)] = od[one(z)]
    mix_grad_pair.wait_recv()
    ms[...] = (mgr[:, one(c)].reshape(ms.shape).astype(f32) + mgx[...].astype(f32)).astype(b16)
    hop_md = [links.start(ms.at[dps[k]], md.at[dp], to_dp[k]) for k in (1, 2, 3)]
    rs_first = [scatter(p4, r4, t4, first, count) for first, count in GROUPS]
    md[one(dp)] = ms[one(dp)]
    red_mix[0].first()
    red_up[3].second()
    red_up[2].third()
    for copy, item in zip(hop_md[:2], red_mix[1:3]):
        copy.wait_recv()
        item.first()
    rs_first[0].forward()
    hop_md[2].wait_recv()
    red_mix[3].first()
    red_attn.second()
    red_up[3].third()
    red_mix[0].second()
    red_attn.third()
    rs_first[1].forward()
    red_mix[1].second()
    red_mix[0].third()

    gain_sum, shift_sum = 0.0, 0.0
    for (first, count), item in zip(GROUPS, rs_first):
        at = slice(first * quarter, (first + count) * quarter)
        first_grad = item.result()
        hat = hat1[at]
        back = res[at] + norm_back(first_grad, hat, rstd1[at], vec(gain1))
        idl[first : first + count] = back.astype(b16).reshape(count, quarter, width)
        gain_sum += jnp.sum(first_grad * hat, axis=0, keepdims=True)
        shift_sum += jnp.sum(first_grad, axis=0, keepdims=True)
    hop_i = scatter_z(idl, ih1)
    ih1[one(z)] = idl[one(z)]
    sm[0:1] = gain_sum
    sm[1:2] = shift_sum
    sm1[one(dp)] = sm[...].reshape(1, *sm.shape)
    small_dp = [links.start(sm, sm1.at[dp], to_dp[k]) for k in peers]

    run(red_down, "fourth")
    red_mix[2].second()
    red_mix[1].third()
    run(red_up, "fourth")
    red_attn.fourth()
    arrived(small_dp)
    sm2[one(z)] = jnp.sum(sm1[...], axis=0, keepdims=True)
    small_z = [links.start(sm2.at[z], sm2.at[z], to_z[k]) for k in peers]
    red_mix[3].second()
    red_mix[2].third()
    arrived(hop_o)
    hop_o = scatter_dp(oh1, out_o)
    out_o[one(dp)] = oh1[one(dp)]
    red_mix[0].fourth()
    red_mix[3].third()
    red_mix[1].fourth()
    arrived(small_z)
    sm3[one(c)] = jnp.sum(sm2[...], axis=0, keepdims=True)
    small_core = links.start(sm3.at[c], sm3.at[c], to_core)
    arrived(hop_i)
    hop_i = scatter_dp(ih1, in_o)
    in_o[one(dp)] = ih1[one(dp)]
    run(red_down + red_up + [red_attn], "done")
    outgoing = [fetch(down_o, down_hbm), fetch(up_o, up_hbm), fetch(attn_o, attn_hbm)]
    red_mix[2].fourth()
    red_mix[3].fourth()
    small_core.wait_recv()
    small_o[...] = sm3[0] + sm3[1]
    arrived(hop_o)
    outgoing.append(fetch(out_o, out_hbm))
    run(red_mix, "done")
    outgoing.append(fetch(mix_o, mix_hbm))
    arrived(hop_i)
    outgoing.append(fetch(in_o, in_hbm))
    links.finish()
    for copy in outgoing:
        copy.wait()


def finish_kernel(*refs):
    f32 = jnp.float32
    ins, outs, mats, held, sems = refs[:9], refs[9:24], refs[24:30], refs[30:39], refs[39]
    out_ref, in_ref, mix_ref, attn_ref, up_ref, down_ref, small_ref, x_ref, cot_ref = held
    shard, width = mats[3].shape
    n = mix_ref.shape[0]
    fetches = {}
    for number in (5, 4, 2, 3, 0, 7, 1, 8, 6):
        fetches[number] = pltpu.make_async_copy(ins[number], held[number], sems.at[6 + number])
        fetches[number].start()
    copies = []

    def store(number, target):
        copy = pltpu.make_async_copy(mats[number], target, sems.at[number])
        copy.start()
        copies.append(copy)

    fetches[5].wait()
    mats[5][...] = flat(down_ref[...]).astype(f32)
    store(5, outs[13])
    fetches[4].wait()
    mats[4][...] = flat(up_ref[...]).astype(f32)
    store(4, outs[11])
    fetches[2].wait()
    for d in range(n):
        value = mix_ref[d].reshape(shard, 3 * shard).astype(f32)
        for part, place_at in ((0, 1), (1, 2), (2, 0)):
            start = place_at * width + d * shard
            mats[2][:, start : start + shard] = value[:, part * shard : (part + 1) * shard]
    store(2, outs[4])
    fetches[3].wait()
    mats[3][...] = flat(attn_ref[...]).astype(f32)
    store(3, outs[7])
    fetches[0].wait()
    fetches[7].wait()
    mats[0][...] = x_ref[...] + flat(out_ref[...]).astype(f32)
    store(0, outs[0])
    fetches[1].wait()
    fetches[8].wait()
    mats[1][...] = cot_ref[...] + flat(in_ref[...]).astype(f32)
    store(1, outs[1])
    fetches[6].wait()
    for number, row in ((2, 0), (3, 1), (5, 2), (6, 3), (8, 4), (9, 5), (10, 6), (14, 7)):
        outs[number][...] = small_ref[row : row + 1].reshape(width)
    for k in range(n):
        outs[12][k * width : (k + 1) * width] = small_ref[8 + k : 9 + k].reshape(width)
    for copy in copies:
        copy.wait()


def plane_body(
    block_input,
    out_cotangent,
    first_gain,
    first_shift,
    mix_weight,
    query_bias,
    value_bias,
    attn_weight,
    attn_bias,
    second_gain,
    second_shift,
    up_weight,
    up_bias,
    down_weight,
    down_bias,
):
    b16, f32 = jnp.bfloat16, jnp.float32
    n, nz = lax.axis_size("dp"), lax.axis_size("ctx") // 2
    rows, width = block_input.shape[1:]
    quarter = rows // n
    shard = width // n
    half = shard // 2
    hidden = up_weight.shape[1] // n
    heads = H // n
    tokens = nz * rows
    keys = 2 * tokens
    x_rows = block_input.reshape(rows, width)
    cot = out_cotangent.reshape(rows, width)
    vm = pltpu.VMEM
    stack = vm((n, quarter, width), b16)
    part = vm((nz, n, quarter, width), b16)
    part_recv = vm((n - 1, nz, quarter, width), b16)
    own = vm((nz * quarter, width), f32)
    results = [
        (n, quarter, width),
        (n, quarter, width),
        (n, 2, half, 3 * shard),
        (2, half, width),
        (2, half, n * hidden),
        (2, hidden // 2, width),
    ]
    scratch = [
        pltpu.SemaphoreType.DMA((SEMS,)),
        pltpu.SemaphoreType.DMA((SEMS,)),
        pltpu.SemaphoreType.DMA((24,)),
    ] + [vm(shape, b16) for shape in results] + [vm((width,), f32)] * 7 + [
        vm((n * hidden,), f32), vm((width,), f32),
        vm((rows, width), f32), vm((rows, width), f32),
        vm((half, 3 * width), b16), vm((shard, width), b16), vm((hidden, width), b16),
        stack, stack, stack, stack, stack, stack,
        vm((n, half, 3 * shard), b16), vm((n, 2, half, 3 * shard), b16),
        vm((n, nz, shard // nz, hidden), b16), part, part, part, part,
        vm((tokens, shard), b16), vm((nz, 2, rows, 2 * shard), b16),
        vm((heads, keys, HD), b16), vm((heads, keys, HD), b16),
        vm((tokens, shard), b16), vm((heads, tokens, 1), f32), vm((tokens, shard), b16),
        own, own, own, own,
        part, part, part, part, part_recv, part_recv, part_recv, part_recv,
        stack, stack, stack, stack,
        vm((tokens, hidden), f32), vm((tokens, hidden), b16), vm((tokens, hidden), b16),
        vm((2, hidden // 2, width), b16),
    ] + [vm((hidden // 2, width), b16)] * 4 + [
        vm((n, 2, half, hidden), b16), vm((n, half, hidden), b16), vm((n, half, hidden), b16),
    ] + [vm((half, n * hidden), b16)] * 3 + [
        vm((2, half, width), b16),
    ] + [vm((half, width), b16)] * 4 + [
        vm((heads, nz, 2, rows, HD), f32), vm((heads, nz, 2, rows, HD), f32),
        vm((nz, rows, 2 * shard), b16), vm((nz, rows, 2 * shard), b16),
        vm((tokens, 3 * shard), b16),
        vm((n, 2, half, 3 * shard), b16),
    ] + [vm((n, half, 3 * shard), b16)] * 5 + [
        stack, stack, stack, stack,
        vm((16, width), f32), vm((n, 16, width), f32), vm((nz, 16, width), f32),
        vm((2, 16, width), f32),
    ]
    hbm = pl.BlockSpec(memory_space=pl.ANY)
    near = pl.BlockSpec(memory_space=pltpu.VMEM)
    far = pl.BlockSpec(memory_space=pltpu.HBM)
    shapes = [(shape, b16) for shape in results] + [((16, width), f32)]
    pieces = pl.pallas_call(
        plane_kernel,
        out_shape=[jax.ShapeDtypeStruct(shape, dtype) for shape, dtype in shapes],
        in_specs=[far] * 15,
        out_specs=[hbm] * len(results) + [near],
        scratch_shapes=scratch,
        compiler_params=pltpu.CompilerParams(
            collective_id=0, has_side_effects=True, vmem_limit_bytes=60 * 1024 * 1024
        ),
        name="plane",
    )(
        x_rows, cot, first_gain, first_shift, mix_weight, query_bias, value_bias, attn_weight,
        attn_bias, second_gain, second_shift, up_weight, up_bias, down_weight, down_bias,
    )
    final = [
        (rows, width), (rows, width), (width,), (width,), (shard, 3 * width), (width,), (width,),
        (shard, width), (width,), (width,), (width,), (shard, n * hidden), (n * hidden,),
        (hidden, width), (width,),
    ]
    large = (0, 1, 4, 7, 11, 13)
    outs = pl.pallas_call(
        finish_kernel,
        out_shape=[jax.ShapeDtypeStruct(shape, f32) for shape in final],
        in_specs=[far] * 9,
        out_specs=[hbm if k in large else near for k in range(len(final))],
        scratch_shapes=[vm(final[k], f32) for k in large]
        + [vm(shape, dtype) for shape, dtype in shapes]
        + [vm((rows, width), f32), vm((rows, width), f32), pltpu.SemaphoreType.DMA((16,))],
        compiler_params=pltpu.CompilerParams(vmem_limit_bytes=60 * 1024 * 1024),
        name="finish",
    )(*pieces, x_rows, cot)
    return (
        outs[0].reshape(1, rows, width),
        outs[1].reshape(1, rows, width),
        *outs[2:],
    )


def fits(mesh):
    n, ctx = mesh.shape["dp"], mesh.shape["ctx"]
    return n == 4 and ctx == 8 and H % n == 0


def solution(mesh):
    placed = (
        P("dp", "ctx", None),
        P("dp", "ctx", None),
        P(),
        P(),
        P("dp", None),
        P(),
        P(),
        P("dp", None),
        P(),
        P(),
        P(),
        P("dp", None),
        P(),
        P("dp", None),
        P(),
    )
    return jax.shard_map(
        plane_body if fits(mesh) else body,
        mesh=mesh,
        in_specs=placed,
        out_specs=(
            P("dp", "ctx", None),
            P("dp", "ctx", None),
            P(),
            P(),
            P("dp", None),
            P(),
            P(),
            P("dp", None),
            P(),
            P(),
            P(),
            P("dp", None),
            P(),
            P("dp", None),
            P(),
        ),
        check_vma=False,
    )
```
